32 devices in a mesh: ctx: 16 (over z, y, core), wsh: 2 (over x).
Axes of the slice: x: 2, y: 2, z: 4, core: 2. Of those that a mesh axis runs over, the one named last changes fastest.
Arguments:
- tokens: bfloat16 [2, 4096, 1472], P('wsh', 'ctx'), may hold values from -6 to 6
- lengths: int32 [2, 1], P('wsh'), may hold values from 1024 to 4096, as said below
- buckets: int32 [255], replicated, may hold values from 0 to 31, as said below
- attention_gain: bfloat16 [1472], P('wsh'), may hold values from 0.5 to 1.5
- query_weight: bfloat16 [1472, 384], P('wsh'), may hold values from -0.078125 to 0.078125
- key_weight: bfloat16 [1472, 384], P('wsh'), may hold values from -0.078125 to 0.078125
- value_weight: bfloat16 [1472, 384], P('wsh'), may hold values from -0.15625 to 0.15625
- output_weight: bfloat16 [384, 1472], P(None, 'wsh'), may hold values from -2.5 to 2.5
- bias_table: bfloat16 [32, 6], P('wsh'), may hold values from -3 to 3
- feed_gain: bfloat16 [1472], P('wsh'), may hold values from 0.5 to 1.5
- gate_weight: bfloat16 [1472, 3584], P(None, 'wsh'), may hold values from -0.15625 to 0.15625
- up_weight: bfloat16 [1472, 3584], P(None, 'wsh'), may hold values from -0.15625 to 0.15625
- down_weight: bfloat16 [3584, 1472], P('wsh'), may hold values from -0.09375 to 0.09375
- cotangent: bfloat16 [2, 4096, 1472], P('wsh', 'ctx'), may hold values from -6 to 6
Outputs:
- result: bfloat16 [2, 4096, 1472], P('wsh', 'ctx')
- input_gradient: bfloat16 [2, 4096, 1472], P('wsh', 'ctx')
- attention_gain_gradient: float32 [1472], P('wsh')
- query_gradient: float32 [1472, 384], P('wsh', 'ctx')
- key_gradient: float32 [1472, 384], P('wsh', 'ctx')
- value_gradient: float32 [1472, 384], P('wsh', 'ctx')
- output_gradient: float32 [384, 1472], P('ctx', 'wsh')
- bias_gradient: float32 [32, 6], P('wsh')
- feed_gain_gradient: float32 [1472], P('wsh')
- gate_gradient: float32 [1472, 3584], P(None, ('ctx', 'wsh'))
- up_gradient: float32 [1472, 3584], P(None, ('ctx', 'wsh'))
- down_gradient: float32 [3584, 1472], P(('ctx', 'wsh'))
The draws below stay inside these ranges and needn't reach their ends.
Inputs may be any that keep to these rules, and one draw needn't show every extreme that they name: `lengths`: every sequence has 1024 or more live tokens; in every draw one sequence has all 4096. Offsets j - i <= 0 map into buckets below 16, offsets above 0 into the upper half.
All inputs are finite; a program needn't handle non-finite values.
Results may differ from the reference program's by a relative error of at most 0.02.
Values may be sent and summed in bfloat16 or wider, within the bound.
No kernel may reach another device: no remote copies, remote signals or barrier semaphores. Data moves between devices by JAX's collectives and lax.ppermute only.
A program may use at most 256 MiB of HBM per device.

```python
import jax
import jax.numpy as jnp
from jax import lax

D = 1472
FF = 3584
HEADS = 6
DKV = 64
BUCKETS = 32
MAXD = 128
TOK_DEV = 256
INNER = 384
PACKS = 2
SEQS = 1
SLOTS = 4096
SPAN = 16
CAP = 4096
MINLEN = 1024


def draw_lengths(key, part):
    total = PACKS * SEQS
    base = jax.random.randint(jax.random.fold_in(key, 11), (total,), MINLEN, CAP + 1)
    top_entry = jax.random.randint(jax.random.fold_in(key, 12), (1,), 0, total)
    entries = jnp.arange(total, dtype=jnp.int32)
    chosen = jnp.where(entries == top_entry, CAP, base)
    return chosen.reshape(PACKS, SEQS).astype(jnp.int32)


def bucket_side(key, length, highest):
    half = BUCKETS // 2
    exact = half // 2
    cut_count = half - exact - 1
    order = jax.random.permutation(key, highest - exact)
    cuts = order[:cut_count] + exact + 1
    magnitudes = jnp.arange(length, dtype=jnp.int32)
    counted = jnp.sum((cuts[None, :] <= magnitudes[:, None]).astype(jnp.int32), axis=1)
    return jnp.where(magnitudes < exact, magnitudes, exact + counted)


def draw_buckets(key, part):
    half = BUCKETS // 2
    lower = bucket_side(jax.random.fold_in(key, 21), MAXD, MAXD - 1)
    upper = bucket_side(jax.random.fold_in(key, 22), MAXD - 1, MAXD - 2) + half
    return jnp.concatenate([lower[::-1], upper]).astype(jnp.int32)


def block_levels(key, shape, shards, least, top_value):
    gain, own = 1.0, jax.random.fold_in(key, 6)
    for dim, shards_of in shards:
        draws = jnp.exp(jax.random.uniform(jax.random.fold_in(own, dim), (shards_of,), jnp.float32, least / len(shards), top_value / len(shards)))
        gain = gain * jnp.repeat(draws, shape[dim] // shards_of).reshape([-1 if axis == dim else 1 for axis in range(len(shape))])
    return gain


def bell_draw(stream_key, dims, spread, most, shards=(), kind=jnp.bfloat16):
    gain = block_levels(stream_key, dims, shards, -0.22, 0.18) if shards else 1.0
    values = jax.random.normal(stream_key, dims, jnp.float32) * spread * gain
    return jnp.minimum(jnp.maximum(values, -most), most).astype(kind)


def setup_inputs(seed: int = 0) -> dict:
    seeds = jax.random.split(jax.random.key(seed), 15)
    tokens = bell_draw(seeds[0], (PACKS, SLOTS, D), 1.0, 6.0, ((0, 2), (1, 16)))
    lengths = draw_lengths(jax.random.fold_in(seeds[14], 71), 0)
    buckets = draw_buckets(jax.random.fold_in(seeds[14], 71), 0)
    attention_gain = jnp.clip(1.0 + 0.1 * jax.random.normal(seeds[3], (D,), jnp.float32), 0.5, 1.5).astype(jnp.bfloat16)
    query_weight = bell_draw(seeds[4], (D, INNER), (4 * D) ** -0.5, 0.078125, ((0, 2),))
    key_weight = bell_draw(seeds[5], (D, INNER), (4 * D) ** -0.5, 0.078125, ((0, 2),))
    value_weight = bell_draw(seeds[6], (D, INNER), D ** -0.5, 0.15625, ((0, 2),))
    output_weight = bell_draw(seeds[7], (INNER, D), (INNER // 64) ** -0.5, 2.5, ((1, 2),))
    bias_table = bell_draw(seeds[8], (BUCKETS, HEADS), 1.0, 3.0, ((0, 2),))
    feed_gain = jnp.clip(1.0 + 0.1 * jax.random.normal(seeds[9], (D,), jnp.float32), 0.5, 1.5).astype(jnp.bfloat16)
    gate_weight = bell_draw(seeds[10], (D, FF), D ** -0.5, 0.15625, ((1, 2),))
    up_weight = bell_draw(seeds[11], (D, FF), D ** -0.5, 0.15625, ((1, 2),))
    down_weight = bell_draw(seeds[12], (FF, D), FF ** -0.5, 0.09375, ((0, 2),))
    cotangent = bell_draw(seeds[13], (PACKS, SLOTS, D), 1.0, 6.0, ((0, 2), (1, 16)))
    return dict(tokens=tokens, lengths=lengths, buckets=buckets, attention_gain=attention_gain, query_weight=query_weight, key_weight=key_weight, value_weight=value_weight, output_weight=output_weight, bias_table=bias_table, feed_gain=feed_gain, gate_weight=gate_weight, up_weight=up_weight, down_weight=down_weight, cotangent=cotangent)


EPSILON = 1e-06
HIGH = lax.Precision.HIGHEST

@jax.custom_vjp
def low(v):
    return lax.optimization_barrier(v.astype(jnp.bfloat16)).astype(jnp.float32)

@jax.custom_vjp
def low_back(v):
    return v

def low_keep(v):
    return (low(v), None)

def low_pass(kept, grad):
    return (grad,)

def back_keep(v):
    return (v, None)

def back_low(kept, grad):
    return (low(grad),)
low.defvjp(low_keep, low_pass)
low_back.defvjp(back_keep, back_low)

def row_scale(values):
    return lax.rsqrt(lax.optimization_barrier(jnp.mean(values * values, axis=-1, keepdims=True)) + EPSILON)

def project(rows, weight):
    return jnp.dot(rows, weight, precision=HIGH, preferred_element_type=jnp.float32)

def to_sequences(values):
    depth = values.shape[-1]
    grid = values.reshape(PACKS, SPAN, SEQS, TOK_DEV, depth)
    return jnp.transpose(grid, (0, 2, 1, 3, 4)).reshape(PACKS * SEQS, CAP, depth)

def from_sequences(values):
    depth = values.shape[-1]
    grid = values.reshape(PACKS, SEQS, SPAN, TOK_DEV, depth)
    return jnp.transpose(grid, (0, 2, 1, 3, 4)).reshape(PACKS * SLOTS, depth)

def attend_one(query, keys, values, key_live, table, buckets):
    columns = jnp.arange(CAP, dtype=jnp.int32)
    keys3 = keys.reshape(CAP, HEADS, DKV)
    values3 = values.reshape(CAP, HEADS, DKV)

    def block(inputs):
        rows_query, start = inputs
        positions = start + jnp.arange(512, dtype=jnp.int32)
        spots = jnp.clip(columns[None, :] - positions[:, None], 1 - MAXD, MAXD - 1) + (MAXD - 1)
        bias = jnp.transpose(table[buckets[spots]], (2, 0, 1))
        scores = jnp.einsum('ihd,jhd->hij', rows_query.reshape(512, HEADS, DKV), keys3, precision=HIGH) + bias
        scores = low_back(jnp.where(key_live[None, None, :] > 0.5, scores, -1e+30))
        weights = low(jax.nn.softmax(scores, axis=-1))
        mixed = jnp.einsum('hij,jhd->ihd', weights, values3, precision=HIGH)
        return mixed.reshape(512, INNER)
    count = CAP // 512
    starts = jnp.arange(count, dtype=jnp.int32) * 512
    attended = lax.map(jax.checkpoint(block), (query.reshape(count, 512, INNER), starts))
    return attended.reshape(CAP, INNER)

def layer(inputs, attention_gain, query_weight, key_weight, value_weight, output_weight, bias_table, feed_gain, gate_weight, up_weight, down_weight, live, buckets):
    first = low(inputs * row_scale(inputs) * attention_gain)
    query = low(low_back(project(first, query_weight)))
    keys = low(low_back(project(first, key_weight)))
    values = low(low_back(project(first, value_weight)))
    live_seq = to_sequences(live)[:, :, 0]

    def one_sequence(inputs_seq):
        return attend_one(inputs_seq[0], inputs_seq[1], inputs_seq[2], inputs_seq[3], bias_table, buckets)
    attended = lax.map(one_sequence, (to_sequences(query), to_sequences(keys), to_sequences(values), live_seq))
    attention = low(low_back(from_sequences(attended)))
    branch = low_back(project(attention, output_weight))
    middle = inputs + live * branch
    second = low(middle * row_scale(middle) * feed_gain)
    gate = low_back(project(second, gate_weight))
    up = low_back(project(second, up_weight))
    hidden = low(jax.nn.gelu(gate, approximate=True) * up)
    return middle + live * low_back(project(hidden, down_weight))

def reference(tokens, lengths, buckets, attention_gain, query_weight, key_weight, value_weight, output_weight, bias_table, feed_gain, gate_weight, up_weight, down_weight, cotangent):
    slot = jnp.arange(SLOTS, dtype=jnp.int32)
    block_index = slot // TOK_DEV
    owner = block_index % SEQS
    position = block_index // SEQS * TOK_DEV + slot % TOK_DEV
    seq_length = lengths[:, owner]
    live = (position[None, :] < seq_length).astype(jnp.float32).reshape(PACKS * SLOTS, 1)
    inputs = tokens.reshape(PACKS * SLOTS, D).astype(jnp.float32)

    def forward(inputs_f, gain_a, query_w, key_w, value_w, output_w, table, gain_f, gate_w, up_w, down_w):
        return layer(inputs_f, gain_a, query_w, key_w, value_w, output_w, table, gain_f, gate_w, up_w, down_w, live, buckets)
    result, pull = jax.vjp(forward, inputs, attention_gain.astype(jnp.float32), query_weight.astype(jnp.float32), key_weight.astype(jnp.float32), value_weight.astype(jnp.float32), output_weight.astype(jnp.float32), bias_table.astype(jnp.float32), feed_gain.astype(jnp.float32), gate_weight.astype(jnp.float32), up_weight.astype(jnp.float32), down_weight.astype(jnp.float32))
    grads = pull(live * cotangent.reshape(PACKS * SLOTS, D).astype(jnp.float32))
    output = result.astype(jnp.bfloat16).reshape(PACKS, SLOTS, D)
    input_gradient = grads[0].astype(jnp.bfloat16).reshape(PACKS, SLOTS, D)
    return (output, input_gradient, grads[1], grads[2], grads[3], grads[4], grads[5], grads[6], grads[7], grads[8], grads[9], grads[10])
```

```python
import functools

import jax
import jax.numpy as jnp
from jax import lax
from jax.experimental import pallas as pl
from jax.experimental.pallas import tpu as pltpu
from jax.sharding import PartitionSpec as P

EPSILON = 1e-06
MASKED = -1e30
HIGH = lax.Precision.HIGHEST


def shifted(block, axis, distance):
    devices = range(lax.axis_size(axis))
    route = [((i - distance) % len(devices), i) for i in devices]
    return lax.ppermute(block, axis, route)


def row_scale(values):
    return lax.rsqrt(jnp.mean(values * values, axis=-1, keepdims=True) + EPSILON)


def normalize(values, gain):
    return values * row_scale(values) * gain


def skew_expand(offset_bias, length):
    count = offset_bias.shape[0]
    padded = jnp.pad(offset_bias, ((0, 0), (0, 1)))
    tiled = jnp.tile(padded, (1, length))[:, : length * (2 * length - 1)]
    return tiled.reshape(count, length, 2 * length - 1)[:, :, length - 1 :]


def diagonal_sums(grid, length):
    count = grid.shape[0]
    wide = jnp.pad(grid, ((0, 0), (0, 0), (length - 1, 0))).reshape(
        count, length * (2 * length - 1)
    )
    wide = jnp.pad(wide, ((0, 0), (0, length)))
    return jnp.sum(wide.reshape(count, length, 2 * length), axis=1)[:, : 2 * length - 1]


def bucket_onehot(offset_start, length, buckets, bucket_count):
    reach = (buckets.shape[0] + 1) // 2
    offsets = offset_start + jnp.arange(2 * length - 1, dtype=jnp.int32) - (length - 1)
    spots = jnp.clip(offsets, 1 - reach, reach - 1) + (reach - 1)
    table_spots = jnp.arange(buckets.shape[0], dtype=jnp.int32)
    chosen = jnp.sum(jnp.where(spots[:, None] == table_spots[None, :], buckets[None, :], 0), axis=1)
    return chosen[:, None] == jnp.arange(bucket_count, dtype=jnp.int32)[None, :]


def block_scores(query3, keys3, table, onehot, key_live, length):
    scores = jnp.einsum("ihd,jhd->hij", query3, keys3, preferred_element_type=jnp.float32)
    offset_bias = jnp.einsum(
        "ob,bh->ho", onehot.astype(jnp.bfloat16), table, preferred_element_type=jnp.float32
    )
    scores = scores + skew_expand(offset_bias, length)
    return jnp.where(key_live[None, None, :], scores, MASKED)


def body(
    tokens,
    lengths,
    buckets,
    attention_gain,
    query_weight,
    key_weight,
    value_weight,
    output_weight,
    bias_table,
    feed_gain,
    gate_weight,
    up_weight,
    down_weight,
    cotangent,
):
    (
        gain_first,
        query_full,
        key_full,
        value_full,
        output_full,
        table_full,
        gain_second,
        gate_full,
        up_full,
        down_full,
    ) = (
        lax.all_gather(attention_gain, "wsh", axis=0, tiled=True),
        lax.all_gather(query_weight, "wsh", axis=0, tiled=True),
        lax.all_gather(key_weight, "wsh", axis=0, tiled=True),
        lax.all_gather(value_weight, "wsh", axis=0, tiled=True),
        lax.all_gather(output_weight, "wsh", axis=1, tiled=True),
        lax.all_gather(bias_table, "wsh", axis=0, tiled=True),
        lax.all_gather(feed_gain, "wsh", axis=0, tiled=True),
        lax.all_gather(gate_weight, "wsh", axis=1, tiled=True),
        lax.all_gather(up_weight, "wsh", axis=1, tiled=True),
        lax.all_gather(down_weight, "wsh", axis=0, tiled=True),
    )
    length = tokens.shape[1]
    heads = table_full.shape[1]
    bucket_count = table_full.shape[0]
    inner = query_full.shape[1]
    head_size = inner // heads
    seq_count = lengths.shape[1]
    wide_count = lax.axis_size("ctx")
    span = wide_count // seq_count
    here = lax.axis_index("ctx")
    my_seq = here % seq_count
    my_block = here // seq_count
    seq_pick = jnp.arange(seq_count, dtype=jnp.int32) == my_seq
    my_length = jnp.sum(jnp.where(seq_pick, lengths[0], 0))
    positions = jnp.arange(length, dtype=jnp.int32)
    live = (my_block * length + positions < my_length).astype(jnp.float32)[:, None]
    inputs = tokens[0].astype(jnp.float32)
    gain_one = gain_first.astype(jnp.float32)
    first = normalize(inputs, gain_one).astype(jnp.bfloat16)
    query = jnp.dot(first, query_full, preferred_element_type=jnp.float32).astype(jnp.bfloat16)
    keys = jnp.dot(first, key_full, preferred_element_type=jnp.float32).astype(jnp.bfloat16)
    values = jnp.dot(first, value_full, preferred_element_type=jnp.float32).astype(jnp.bfloat16)
    query3 = query.reshape(length, heads, head_size)

    def forward_step(carry, block_keys, block_values, key_block):
        run_max, run_total, running = carry
        onehot = bucket_onehot((key_block - my_block) * length, length, buckets, bucket_count)
        key_live = key_block * length + positions < my_length
        scores = block_scores(
            query3,
            block_keys.reshape(length, heads, head_size),
            table_full,
            onehot,
            key_live,
            length,
        )
        new_max = jnp.maximum(run_max, jnp.max(scores, axis=2))
        weights = jnp.exp(scores - new_max[:, :, None])
        factor = jnp.exp(run_max - new_max)
        run_total = run_total * factor + jnp.sum(weights, axis=2)
        update = jnp.einsum(
            "hij,jhd->ihd",
            weights.astype(jnp.bfloat16),
            block_values.reshape(length, heads, head_size),
            preferred_element_type=jnp.float32,
        )
        running = running * jnp.transpose(factor)[:, :, None] + update
        return (new_max, run_total, running)

    start_carry = (
        jnp.full((heads, length), MASKED, jnp.float32),
        jnp.zeros((heads, length), jnp.float32),
        jnp.zeros((length, heads, head_size), jnp.float32),
    )
    start_carry = forward_step(start_carry, keys, values, my_block)
    stored = ()

    def cycle_turn(turn, state):
        carry, block_keys, block_values, stored_blocks = state
        block_keys, block_values = shifted((block_keys, block_values), "ctx", seq_count)
        carry = forward_step(carry, block_keys, block_values, (my_block - turn) % span)
        return (carry, block_keys, block_values, stored_blocks)

    (run_max, run_total, running), _, _, stored = lax.fori_loop(
        1, span, cycle_turn, (start_carry, keys, values, stored)
    )
    log_total = run_max + jnp.log(run_total)
    attention = (running / jnp.transpose(run_total)[:, :, None]).reshape(length, inner)
    attention_low = attention.astype(jnp.bfloat16)
    branch = jnp.dot(attention_low, output_full, preferred_element_type=jnp.float32)
    middle = inputs + live * branch
    gain_two = gain_second.astype(jnp.float32)
    second = normalize(middle, gain_two).astype(jnp.bfloat16)
    gate = jnp.dot(second, gate_full, preferred_element_type=jnp.float32)
    up = jnp.dot(second, up_full, preferred_element_type=jnp.float32)
    hidden = (jax.nn.gelu(gate, approximate=True) * up).astype(jnp.bfloat16)
    feed = jnp.dot(hidden, down_full, preferred_element_type=jnp.float32)
    result = (middle + live * feed).astype(jnp.bfloat16)
    outer = live * cotangent[0].astype(jnp.float32)
    outer_low = outer.astype(jnp.bfloat16)
    down_grad = jnp.einsum("tf,td->fd", hidden, outer_low, preferred_element_type=jnp.float32)
    hidden_grad = jnp.einsum("td,fd->tf", outer_low, down_full, preferred_element_type=jnp.float32)

    def gated(gate_in, up_in):
        return jax.nn.gelu(gate_in, approximate=True) * up_in

    _, gate_pull = jax.vjp(gated, gate, up)
    gate_back, up_back = gate_pull(hidden_grad)
    gate_low = gate_back.astype(jnp.bfloat16)
    up_low = up_back.astype(jnp.bfloat16)
    gate_grad = jnp.einsum("td,tf->df", second, gate_low, preferred_element_type=jnp.float32)
    up_grad = jnp.einsum("td,tf->df", second, up_low, preferred_element_type=jnp.float32)
    second_grad = jnp.einsum(
        "tf,df->td", gate_low, gate_full, preferred_element_type=jnp.float32
    ) + jnp.einsum("tf,df->td", up_low, up_full, preferred_element_type=jnp.float32)
    _, norm_pull = jax.vjp(normalize, middle, gain_two)
    middle_back, gain_two_grad = norm_pull(second_grad)
    middle_grad = outer + middle_back
    branch_low = (live * middle_grad).astype(jnp.bfloat16)
    output_grad = jnp.einsum(
        "ti,td->id", attention_low, branch_low, preferred_element_type=jnp.float32
    )
    attention_grad = jnp.einsum(
        "td,id->ti", branch_low, output_full, preferred_element_type=jnp.float32
    ).astype(jnp.bfloat16)
    attention_grad3 = attention_grad.reshape(length, heads, head_size)
    delta = jnp.transpose(
        jnp.sum(
            (attention_grad.astype(jnp.float32) * attention).reshape(length, heads, head_size),
            axis=2,
        )
    )

    def backward_step(block_keys, block_values, key_block):
        keys3 = block_keys.reshape(length, heads, head_size)
        values3 = block_values.reshape(length, heads, head_size)
        onehot = bucket_onehot((key_block - my_block) * length, length, buckets, bucket_count)
        key_live = key_block * length + positions < my_length
        scores = block_scores(query3, keys3, table_full, onehot, key_live, length)
        probs = jnp.exp(scores - log_total[:, :, None])
        prob_grad = jnp.einsum(
            "ihd,jhd->hij", attention_grad3, values3, preferred_element_type=jnp.float32
        )
        score_grad = (probs * (prob_grad - delta[:, :, None])).astype(jnp.bfloat16)
        part_query = jnp.einsum(
            "hij,jhd->ihd", score_grad, keys3, preferred_element_type=jnp.float32
        )
        part_keys = jnp.einsum(
            "hij,ihd->jhd", score_grad, query3, preferred_element_type=jnp.float32
        )
        part_values = jnp.einsum(
            "hij,ihd->jhd",
            probs.astype(jnp.bfloat16),
            attention_grad3,
            preferred_element_type=jnp.float32,
        )
        part_table = jnp.einsum(
            "ho,ob->bh",
            diagonal_sums(score_grad.astype(jnp.float32), length),
            onehot.astype(jnp.float32),
            precision=HIGH,
        )
        return (
            part_query.reshape(length, inner),
            part_keys.reshape(length, inner),
            part_values.reshape(length, inner),
            part_table,
        )

    def back_turn(turn, state):
        block_keys, block_values, keys_sum, values_sum, query_sum, table_sum = state
        part_query, part_keys, part_values, part_table = backward_step(
            block_keys, block_values, (my_block - turn) % span
        )
        keys_next = keys_sum + part_keys
        values_next = values_sum + part_values
        keys_sum, values_sum = (
            shifted(keys_next.astype(jnp.bfloat16), "ctx", seq_count).astype(keys_next.dtype),
            shifted(values_next.astype(jnp.bfloat16), "ctx", seq_count).astype(values_next.dtype),
        )
        block_keys, block_values = shifted((block_keys, block_values), "ctx", seq_count)
        return (
            block_keys,
            block_values,
            keys_sum,
            values_sum,
            query_sum + part_query,
            table_sum + part_table,
        )

    zeros_rows = jnp.zeros((length, inner), jnp.float32)
    back_state = (
        keys,
        values,
        zeros_rows,
        zeros_rows,
        zeros_rows,
        jnp.zeros((bucket_count, heads), jnp.float32),
    )
    _, _, keys_sum, values_sum, query_sum, table_grad = lax.fori_loop(
        0, span, back_turn, back_state
    )
    query_low = query_sum.astype(jnp.bfloat16)
    keys_low = keys_sum.astype(jnp.bfloat16)
    values_low = values_sum.astype(jnp.bfloat16)
    query_grad = jnp.einsum("td,ti->di", first, query_low, preferred_element_type=jnp.float32)
    key_grad = jnp.einsum("td,ti->di", first, keys_low, preferred_element_type=jnp.float32)
    value_grad = jnp.einsum("td,ti->di", first, values_low, preferred_element_type=jnp.float32)
    first_grad = (
        jnp.einsum("ti,di->td", query_low, query_full, preferred_element_type=jnp.float32)
        + jnp.einsum("ti,di->td", keys_low, key_full, preferred_element_type=jnp.float32)
        + jnp.einsum("ti,di->td", values_low, value_full, preferred_element_type=jnp.float32)
    )
    _, first_pull = jax.vjp(normalize, inputs, gain_one)
    inputs_back, gain_one_grad = first_pull(first_grad)
    input_gradient = (middle_grad + inputs_back).astype(jnp.bfloat16)
    small = lax.psum((gain_one_grad, table_grad, gain_two_grad), "ctx")
    wide = (
        lax.psum_scatter(query_grad, "ctx", scatter_dimension=1, tiled=True),
        lax.psum_scatter(key_grad, "ctx", scatter_dimension=1, tiled=True),
        lax.psum_scatter(value_grad, "ctx", scatter_dimension=1, tiled=True),
        lax.psum_scatter(output_grad, "ctx", scatter_dimension=0, tiled=True),
        lax.psum_scatter(gate_grad, "ctx", scatter_dimension=1, tiled=True),
        lax.psum_scatter(up_grad, "ctx", scatter_dimension=1, tiled=True),
        lax.psum_scatter(down_grad, "ctx", scatter_dimension=0, tiled=True),
    )
    final = (
        lax.psum_scatter(
            small[0].astype(jnp.bfloat16), "wsh", scatter_dimension=0, tiled=True
        ).astype(jnp.float32),
        lax.psum_scatter(
            small[1].astype(jnp.bfloat16), "wsh", scatter_dimension=0, tiled=True
        ).astype(jnp.float32),
        lax.psum_scatter(
            small[2].astype(jnp.bfloat16), "wsh", scatter_dimension=0, tiled=True
        ).astype(jnp.float32),
        lax.psum_scatter(
            wide[0].astype(jnp.bfloat16), "wsh", scatter_dimension=0, tiled=True
        ).astype(jnp.float32),
        lax.psum_scatter(
            wide[1].astype(jnp.bfloat16), "wsh", scatter_dimension=0, tiled=True
        ).astype(jnp.float32),
        lax.psum_scatter(
            wide[2].astype(jnp.bfloat16), "wsh", scatter_dimension=0, tiled=True
        ).astype(jnp.float32),
        lax.psum_scatter(
            wide[3].astype(jnp.bfloat16), "wsh", scatter_dimension=1, tiled=True
        ).astype(jnp.float32),
        lax.psum_scatter(
            wide[4].astype(jnp.bfloat16), "wsh", scatter_dimension=1, tiled=True
        ).astype(jnp.float32),
        lax.psum_scatter(
            wide[5].astype(jnp.bfloat16), "wsh", scatter_dimension=1, tiled=True
        ).astype(jnp.float32),
        lax.psum_scatter(
            wide[6].astype(jnp.bfloat16), "wsh", scatter_dimension=0, tiled=True
        ).astype(jnp.float32),
    )
    gain_one_out, table_out, gain_two_out = (final[0], final[1], final[2])
    query_out, key_out, value_out, output_out = (final[3], final[4], final[5], final[6])
    gate_out, up_out, down_out = (final[7], final[8], final[9])
    return (
        result[None],
        input_gradient[None],
        gain_one_out,
        query_out,
        key_out,
        value_out,
        output_out,
        table_out,
        gain_two_out,
        gate_out,
        up_out,
        down_out,
    )


BLOCK = 256
PAIR = 128
SPAN_ROW = 1024
CONTRACT_LAST = (((1,), (1,)), ((), ()))
AXES = ("ctx", "wsh")


def head_lanes(rows, second):
    lane = lax.broadcasted_iota(jnp.int32, (rows, PAIR), 1)
    return (lane >= PAIR // 2) if second else (lane < PAIR // 2)


def pair_select(first, second, rows):
    return jnp.where(head_lanes(rows, False), first, second)


def only_head(block, second):
    return jnp.where(head_lanes(block.shape[0], second), block, jnp.zeros_like(block))


def query_aux(rows):
    lane = lax.broadcasted_iota(jnp.int32, (rows, PAIR), 1)
    return jnp.where(lane == 0, 1.0, 0.0).astype(jnp.bfloat16)


def key_aux(start, rows, length):
    lane = lax.broadcasted_iota(jnp.int32, (rows, PAIR), 1)
    row = lax.broadcasted_iota(jnp.int32, (rows, PAIR), 0)
    dead = jnp.logical_and(lane == 0, start + row >= length)
    return jnp.where(dead, MASKED, 0.0).astype(jnp.bfloat16)


def contract_last(left, right):
    return lax.dot_general(left, right, CONTRACT_LAST, preferred_element_type=jnp.float32)


def tile_of(key_block, query_block):
    return jnp.clip(key_block - query_block, -2, 2) + 2


def tiles_kernel(row_ref, tile_ref, turned_ref):
    row = row_ref[0]
    wide = pltpu.roll(
        jnp.broadcast_to(row, (BLOCK, SPAN_ROW)), SPAN_ROW - 255, 1, stride=1, stride_axis=0
    )
    first = jnp.broadcast_to(row[:, 0:1], (BLOCK, BLOCK))
    last = jnp.broadcast_to(row[:, SPAN_ROW - 1 : SPAN_ROW], (BLOCK, BLOCK))
    tiles = [first, wide[:, 0:256], wide[:, 256:512], wide[:, 512:768], last]
    for spot, tile in enumerate(tiles):
        tile_ref[0, spot] = tile.astype(jnp.bfloat16)
        turned_ref[0, spot] = jnp.transpose(tile).astype(jnp.bfloat16)


def bias_tiles(offset_rows):
    heads = offset_rows.shape[0]
    shape = jax.ShapeDtypeStruct((heads, 5, BLOCK, BLOCK), jnp.bfloat16)
    spec = pl.BlockSpec((1, 5, BLOCK, BLOCK), lambda h: (h, 0, 0, 0))
    return pl.pallas_call(
        tiles_kernel,
        grid=(heads,),
        out_shape=(shape, shape),
        in_specs=[pl.BlockSpec((1, 1, SPAN_ROW), lambda h: (h, 0, 0))],
        out_specs=(spec, spec),
        name="bias_tiles",
    )(offset_rows[:, None, :])


def forward_kernel(count, first, last, info_ref, *refs):
    refs = list(refs)
    query_ref = refs.pop(0)
    key_refs, refs = refs[:count], refs[count:]
    value_refs, refs = refs[:count], refs[count:]
    tile_ref = refs.pop(0)
    query_block, length = info_ref[0], info_ref[1]
    query = query_ref[...]
    aux = query_aux(BLOCK)
    if first:
        old_max = jnp.full((BLOCK, PAIR), MASKED, jnp.float32)
        total = None
    else:
        max_ref, total_ref = refs.pop(0), refs.pop(0)
        old_max, total = max_ref[...], total_ref[...]
    keys = []
    for spot in range(count):
        start = info_ref[2 + spot] * BLOCK
        keys.append(
            jnp.concatenate([key_refs[spot][...], key_aux(start, BLOCK, length)], axis=1)
        )
    tops, weights = [], []
    for head in range(2):
        left = jnp.concatenate([only_head(query, head == 1), aux], axis=1)
        scores = []
        for spot in range(count):
            tile = tile_ref[head, tile_of(info_ref[2 + spot], query_block)]
            scores.append(contract_last(left, keys[spot]) + tile.astype(jnp.float32))
        top = functools.reduce(jnp.maximum, scores)
        lane = head * (PAIR // 2)
        top = jnp.maximum(old_max[:, lane : lane + 1], jnp.max(top, axis=1, keepdims=True))
        tops.append(top)
        weights.append([jnp.exp(score - top).astype(jnp.bfloat16) for score in scores])
    new_max = pair_select(tops[0], tops[1], BLOCK)
    ones = jnp.ones((BLOCK, PAIR), jnp.bfloat16)
    update = None
    for spot in range(count):
        value = value_refs[spot][...]
        right = jnp.concatenate(
            [
                jnp.concatenate([only_head(value, False), only_head(ones, False)], axis=1),
                jnp.concatenate([only_head(value, True), only_head(ones, True)], axis=1),
            ],
            axis=0,
        )
        left = jnp.concatenate([weights[0][spot], weights[1][spot]], axis=1)
        part = jnp.dot(left, right, preferred_element_type=jnp.float32)
        update = part if update is None else update + part
    if not first:
        factor = jnp.exp(old_max - new_max)
        update = update + total * jnp.concatenate([factor, factor], axis=1)
    if last:
        out_ref, low_ref, log_ref = refs
        out = update[:, :PAIR] / update[:, PAIR:]
        out_ref[...] = out
        low_ref[...] = out.astype(jnp.bfloat16)
        log_ref[...] = new_max + jnp.log(update[:, PAIR:])
    else:
        max_out, total_out = refs
        max_out[...] = new_max
        total_out[...] = update


def forward_call(info, query, keys, values, tiles, state, last):
    count = len(keys)
    inner = query.shape[1]
    pairs = inner // PAIR
    first = state is None
    block = pl.BlockSpec((BLOCK, PAIR), lambda p, s: (0, p))
    double = pl.BlockSpec((BLOCK, 2 * PAIR), lambda p, s: (0, p))
    tile_spec = pl.BlockSpec((2, 5, BLOCK, BLOCK), lambda p, s: (p, 0, 0, 0))
    in_specs = [block] * (1 + 2 * count) + [tile_spec]
    operands = [info, query, *keys, *values, tiles]
    aliases = {}
    if not first:
        in_specs += [block, double]
        operands += list(state)
    f32 = functools.partial(jax.ShapeDtypeStruct, dtype=jnp.float32)
    if last:
        out_shape = (
            f32((BLOCK, inner)),
            jax.ShapeDtypeStruct((BLOCK, inner), jnp.bfloat16),
            f32((BLOCK, inner)),
        )
        out_specs = (block, block, block)
    else:
        out_shape = (f32((BLOCK, inner)), f32((BLOCK, 2 * inner)))
        out_specs = (block, double)
    return pl.pallas_call(
        functools.partial(forward_kernel, count, first, last),
        grid_spec=pltpu.PrefetchScalarGridSpec(
            num_scalar_prefetch=1, grid=(pairs,), in_specs=in_specs, out_specs=out_specs
        ),
        out_shape=out_shape,
        input_output_aliases=aliases,
        cost_estimate=pl.CostEstimate(
            flops=2 * pairs * count * 6 * BLOCK * BLOCK * BLOCK,
            bytes_accessed=pairs * (count * 2 + 10) * BLOCK * PAIR * 2,
            transcendentals=pairs * count * 2 * BLOCK * BLOCK,
        ),
        name="attention_forward",
    )(*operands)


def query_kernel(blocks, info_ref, query_ref, grad_ref, out_ref, log_ref, key_ref, value_ref, tile_ref, part_ref, diag_ref, sums_ref):
    query_block, length = info_ref[0], info_ref[1]
    query, grad = query_ref[...], grad_ref[...]
    aux = query_aux(BLOCK)
    product = grad.astype(jnp.float32) * out_ref[...]
    logs = log_ref[...]
    sums_ref[...] = jnp.zeros_like(sums_ref)
    lefts, grads, deltas, shifts = [], [], [], []
    for head in range(2):
        lefts.append(jnp.concatenate([only_head(query, head == 1), aux], axis=1))
        grads.append(only_head(grad, head == 1))
        deltas.append(jnp.sum(only_head(product, head == 1), axis=1, keepdims=True))
        lane = head * (PAIR // 2)
        shifts.append(logs[:, lane : lane + 1])
    part_ref[...] = jnp.zeros_like(part_ref)

    def one(spot, carry):
        key_block = info_ref[2 + spot]
        rows = pl.ds(pl.multiple_of(spot * BLOCK, BLOCK), BLOCK)
        key, value = key_ref[rows, :], value_ref[rows, :]
        wide = jnp.concatenate([key, key_aux(key_block * BLOCK, BLOCK, length)], axis=1)
        tile = tile_of(key_block, query_block)
        pieces = []
        for head in range(2):
            scores = contract_last(lefts[head], wide) + tile_ref[head, tile].astype(jnp.float32)
            probs = jnp.exp(scores - shifts[head])
            slope = contract_last(grads[head], value)
            score_grad = probs * (slope - deltas[head])
            sums_ref[head, tile] += score_grad
            pieces.append(score_grad.astype(jnp.bfloat16))
        right = jnp.concatenate([only_head(key, False), only_head(key, True)], axis=0)
        part_ref[...] += jnp.dot(
            jnp.concatenate(pieces, axis=1), right, preferred_element_type=jnp.float32
        )
        return carry

    lax.fori_loop(0, blocks, one, 0)
    rows = []
    lane = lax.broadcasted_iota(jnp.int32, (1, SPAN_ROW), 1)
    flip = (
        lax.broadcasted_iota(jnp.int32, (BLOCK, BLOCK), 0)
        + lax.broadcasted_iota(jnp.int32, (BLOCK, BLOCK), 1)
        == BLOCK - 1
    ).astype(jnp.float32)
    for head in range(2):
        near = jnp.concatenate(
            [sums_ref[head, 1], sums_ref[head, 2], sums_ref[head, 3], jnp.zeros((BLOCK, BLOCK), jnp.float32)],
            axis=1,
        )
        flipped = jnp.dot(flip, near, precision=HIGH, preferred_element_type=jnp.float32)
        turned = pltpu.roll(flipped, 0, 1, stride=1, stride_axis=0)
        line = jnp.sum(turned, axis=0, keepdims=True)
        before = jnp.sum(jnp.sum(sums_ref[head, 0], axis=0, keepdims=True), axis=1, keepdims=True)
        after = jnp.sum(jnp.sum(sums_ref[head, 4], axis=0, keepdims=True), axis=1, keepdims=True)
        line = line + jnp.where(lane == 0, before, 0.0) + jnp.where(lane == SPAN_ROW - 2, after, 0.0)
        rows.append(line)
    diag_ref[0] = jnp.concatenate(rows + [jnp.zeros((6, SPAN_ROW), jnp.float32)], axis=0)


def query_call(info, query, grad, out, logs, keys, values, tiles):
    inner = query.shape[1]
    pairs = inner // PAIR
    blocks = keys.shape[0] // BLOCK
    block = pl.BlockSpec((BLOCK, PAIR), lambda p, s: (0, p))
    tall = pl.BlockSpec((blocks * BLOCK, PAIR), lambda p, s: (0, p))
    tile_spec = pl.BlockSpec((2, 5, BLOCK, BLOCK), lambda p, s: (p, 0, 0, 0))
    return pl.pallas_call(
        functools.partial(query_kernel, blocks),
        grid_spec=pltpu.PrefetchScalarGridSpec(
            num_scalar_prefetch=1,
            grid=(pairs,),
            in_specs=[block, block, block, block, tall, tall, tile_spec],
            out_specs=(block, pl.BlockSpec((1, 8, SPAN_ROW), lambda p, s: (p, 0, 0))),
            scratch_shapes=[pltpu.VMEM((2, 5, BLOCK, BLOCK), jnp.float32)],
        ),
        out_shape=(
            jax.ShapeDtypeStruct((BLOCK, inner), jnp.float32),
            jax.ShapeDtypeStruct((pairs, 8, SPAN_ROW), jnp.float32),
        ),
        cost_estimate=pl.CostEstimate(
            flops=2 * pairs * blocks * 6 * BLOCK * BLOCK * BLOCK,
            bytes_accessed=pairs * blocks * 2 * BLOCK * PAIR * 2,
            transcendentals=pairs * blocks * 2 * BLOCK * BLOCK,
        ),
        name="attention_query_grad",
    )(info, query, grad, out, logs, keys, values, tiles)


def key_kernel(count, first, last, info_ref, *refs):
    refs = list(refs)
    key_ref, value_ref = refs.pop(0), refs.pop(0)
    query_refs, refs = refs[:count], refs[count:]
    grad_refs, refs = refs[:count], refs[count:]
    log_refs, refs = refs[:count], refs[count:]
    delta_refs, refs = refs[:count], refs[count:]
    tile_ref = refs.pop(0)
    if not first:
        key_in, value_in = refs.pop(0), refs.pop(0)
    key_out, value_out = refs
    pair = pl.program_id(0)
    key_block, length = info_ref[0], info_ref[1]
    key, value = key_ref[...], value_ref[...]
    wide = jnp.concatenate([key, key_aux(key_block * BLOCK, BLOCK, length)], axis=1)
    aux = query_aux(BLOCK)
    key_sum = value_sum = None
    for spot in range(count):
        query_block = info_ref[2 + spot]
        query, grad = query_refs[spot][...], grad_refs[spot][...]
        tile = tile_of(key_block, query_block)
        probs_low, slopes_low, queries, grads = [], [], [], []
        for head in range(2):
            row = pl.ds(2 * pair + head, 1)
            my_query, my_grad = only_head(query, head == 1), only_head(grad, head == 1)
            scores = contract_last(wide, jnp.concatenate([my_query, aux], axis=1))
            scores = scores + tile_ref[head, tile].astype(jnp.float32)
            probs = jnp.exp(scores - log_refs[spot][row, :])
            slope = contract_last(value, my_grad) - delta_refs[spot][row, :]
            probs_low.append(probs.astype(jnp.bfloat16))
            slopes_low.append((probs * slope).astype(jnp.bfloat16))
            queries.append(my_query)
            grads.append(my_grad)
        part_value = jnp.dot(
            jnp.concatenate(probs_low, axis=1), jnp.concatenate(grads, axis=0), preferred_element_type=jnp.float32
        )
        part_key = jnp.dot(
            jnp.concatenate(slopes_low, axis=1), jnp.concatenate(queries, axis=0), preferred_element_type=jnp.float32
        )
        key_sum = part_key if key_sum is None else key_sum + part_key
        value_sum = part_value if value_sum is None else value_sum + part_value
    if not first:
        key_sum, value_sum = key_sum + key_in[...], value_sum + value_in[...]
    key_out[...] = key_sum.astype(key_out.dtype)
    value_out[...] = value_sum.astype(value_out.dtype)


def key_call(info, key, value, queries, grads, logs, deltas, turned, state, last):
    count = len(queries)
    inner = key.shape[1]
    pairs = inner // PAIR
    first = state is None
    block = pl.BlockSpec((BLOCK, PAIR), lambda p, s: (0, p))
    rows = pl.BlockSpec((8, BLOCK), lambda p, s: (0, 0))
    tile_spec = pl.BlockSpec((2, 5, BLOCK, BLOCK), lambda p, s: (p, 0, 0, 0))
    in_specs = [block] * (2 + 2 * count) + [rows] * (2 * count) + [tile_spec]
    operands = [info, key, value, *queries, *grads, *logs, *deltas, turned]
    if not first:
        in_specs += [block, block]
        operands += list(state)
    kind = jnp.bfloat16 if last else jnp.float32
    shape = jax.ShapeDtypeStruct((BLOCK, inner), kind)
    return pl.pallas_call(
        functools.partial(key_kernel, count, first, last),
        grid_spec=pltpu.PrefetchScalarGridSpec(
            num_scalar_prefetch=1, grid=(pairs,), in_specs=in_specs, out_specs=(block, block)
        ),
        out_shape=(shape, shape),
        cost_estimate=pl.CostEstimate(
            flops=2 * pairs * count * 8 * BLOCK * BLOCK * BLOCK,
            bytes_accessed=pairs * (count * 2 + 10) * BLOCK * PAIR * 2,
            transcendentals=pairs * count * 2 * BLOCK * BLOCK,
        ),
        name="attention_key_grad",
    )(*operands)


def grouped_body(
    tokens,
    lengths,
    buckets,
    attention_gain,
    query_weight,
    key_weight,
    value_weight,
    output_weight,
    bias_table,
    feed_gain,
    gate_weight,
    up_weight,
    down_weight,
    cotangent,
):
    bf16, f32 = jnp.bfloat16, jnp.float32
    places = lax.axis_size("ctx")
    chips = places // 2
    rows_of_chips = chips // 2
    here = lax.axis_index("ctx")
    side = lax.axis_index("wsh")
    core = here % 2
    chip = here // 2
    lane_y = chip % 2
    lane_z = chip // 2
    length = tokens.shape[1]
    width = tokens.shape[2]
    half = width // 2
    heads = bias_table.shape[1]
    inner = query_weight.shape[1]

    def spread(block, route):
        return lax.ppermute(block, AXES, route)

    def route_of(move):
        pairs = []
        for c in range(places):
            for w in range(2):
                target = move(c // 4, (c // 2) % 2, c % 2, w)
                if target is not None:
                    z, y, k, x = target
                    pairs.append((c * 2 + w, (((z * 2 + y) * 2) + k) * 2 + x))
        return pairs

    route_core = route_of(lambda z, y, k, x: (z, y, 1 - k, x))
    route_x = route_of(lambda z, y, k, x: (z, y, k, 1 - x))
    route_y = route_of(lambda z, y, k, x: (z, 1 - y, k, x))
    route_far = route_of(lambda z, y, k, x: (z ^ 2, y, k, x))
    route_near = route_of(lambda z, y, k, x: (z ^ 1, y, k, x))
    order = [(i, 0) for i in range(rows_of_chips)] + [
        (rows_of_chips - 1 - i, 1) for i in range(rows_of_chips)
    ]
    place = {spot: i for i, spot in enumerate(order)}

    def ring(distance):
        return route_of(
            lambda z, y, k, x: (*order[(place[(z, y)] + distance) % chips], k, x)
        )

    route_up, route_down = ring(1), ring(-1)
    my_place = jnp.where(lane_y == 0, lane_z, 2 * rows_of_chips - 1 - lane_z)

    def chip_at(spot):
        spot = spot % chips
        return jnp.where(
            spot < rows_of_chips, 2 * spot, 2 * (2 * rows_of_chips - 1 - spot) + 1
        )

    def swap_core(block):
        return spread(block, route_core)

    def swap_x(block):
        return spread(block, route_x)

    def all_sum(block):
        for route in (route_core, route_x, route_y, route_far, route_near):
            block = block + spread(block, route)
        return block

    def both_sides(mine, other, axis):
        return jnp.where(
            side == 0,
            jnp.concatenate([mine, other], axis=axis),
            jnp.concatenate([other, mine], axis=axis),
        )

    def fetch_rows(weight):
        count = weight.shape[0] // 2
        part = swap_x(lax.dynamic_slice_in_dim(weight, core * count, count, 0))
        return part, swap_core(part)

    def join_rows(weight, part, traded):
        other = jnp.where(
            core == 0,
            jnp.concatenate([part, traded], axis=0),
            jnp.concatenate([traded, part], axis=0),
        )
        return both_sides(weight, other, 0)

    gain_other = swap_x(attention_gain)
    projections = jnp.concatenate([key_weight, value_weight, query_weight], axis=1)
    part, traded = fetch_rows(projections)
    table_other = swap_x(bias_table)
    feed_other = swap_x(feed_gain)
    live_count = jnp.minimum(lengths[0, 0], places * length)
    count_other = swap_x(live_count.astype(f32).reshape(1, 1))[0, 0].astype(jnp.int32)
    mine = tokens[0]
    cot = cotangent[0]
    gain_one = both_sides(attention_gain, gain_other, 0).astype(f32)
    gain_two = both_sides(feed_gain, feed_other, 0).astype(f32)
    table = both_sides(bias_table, table_other, 0)

    positions = here * length + jnp.arange(length, dtype=jnp.int32)
    pair_positions = (here ^ 1) * length + jnp.arange(length, dtype=jnp.int32)
    live_own = (positions < live_count).astype(f32)[:, None]
    live_group = jnp.concatenate(
        [
            live_own,
            (pair_positions < live_count).astype(f32)[:, None],
            (positions < count_other).astype(f32)[:, None],
            (pair_positions < count_other).astype(f32)[:, None],
        ],
        axis=0,
    )

    inputs = mine.astype(f32)
    scale_one = row_scale(inputs)
    first = (inputs * scale_one * gain_one).astype(bf16)
    weight_all = join_rows(projections, part, traded)
    projected = jnp.dot(first, weight_all, preferred_element_type=f32).astype(bf16)
    keys, values, query = (projected[:, :inner], projected[:, inner : 2 * inner], projected[:, 2 * inner :])

    bucket_count = table.shape[0]
    reach = (buckets.shape[0] + 1) // 2
    offsets = jnp.clip(jnp.arange(SPAN_ROW, dtype=jnp.int32) - 511, 1 - reach, reach - 1) + (reach - 1)
    spots = jnp.arange(buckets.shape[0], dtype=jnp.int32)
    chosen = jnp.sum(jnp.where(offsets[:, None] == spots[None, :], buckets[None, :], 0), axis=1)
    onehot = (chosen[:, None] == jnp.arange(bucket_count, dtype=jnp.int32)[None, :]).astype(f32)
    offset_rows = lax.dot_general(
        table.astype(f32), onehot, (((0,), (1,)), ((), ())), precision=HIGH, preferred_element_type=f32
    )
    tiles, turned = bias_tiles(offset_rows)

    def group_rows(block):
        other = swap_x(block)
        return jnp.concatenate([block, swap_core(block), other, swap_core(other)], axis=0)

    def ring_gather(own_parts, use):
        pieces = [[part, swap_core(part)] for part in own_parts]
        use(0, pieces, [chip * 2 + core, chip * 2 + 1 - core])
        ups = downs = list(own_parts)
        middle = chips // 2
        for step in range(1, middle + 1):
            if step < middle:
                ups = [spread(part, route_up) for part in ups]
                downs = [spread(part, route_down) for part in downs]
                pieces = [
                    [u, swap_core(u), d, swap_core(d)] for u, d in zip(ups, downs)
                ]
                a, b = chip_at(my_place + chips - step), chip_at(my_place + step)
                use(step, pieces, [a * 2 + core, a * 2 + 1 - core, b * 2 + core, b * 2 + 1 - core])
            else:
                lasts = [
                    spread(part_u, route_up) if spot % 2 == 0 else spread(part_d, route_down)
                    for spot, (part_u, part_d) in enumerate(zip(ups, downs))
                ]
                pieces = [[part, swap_core(part)] for part in lasts]
                a = chip_at(my_place + step)
                use(step, pieces, [a * 2 + core, a * 2 + 1 - core])

    middle = chips // 2
    store = {"state": None, "keys": [], "values": [], "blocks": []}

    def forward_use(step, pieces, blocks):
        key_blocks, value_blocks = pieces
        info = jnp.stack([here, live_count, *blocks]).astype(jnp.int32)
        store["state"] = forward_call(
            info, query, key_blocks, value_blocks, tiles, store["state"], step == middle
        )
        store["keys"] += key_blocks
        store["values"] += value_blocks
        store["blocks"] += blocks

    ring_gather([keys, values], forward_use)
    attention, attention_low, logs = store["state"]
    keys_all = jnp.concatenate(store["keys"], axis=0)
    values_all = jnp.concatenate(store["values"], axis=0)
    info_all = jnp.stack([here, live_count, *store["blocks"]]).astype(jnp.int32)

    out_part, out_traded = fetch_columns(output_weight, core, swap_x, swap_core)
    output_full = both_sides(
        output_weight,
        jnp.where(
            core == 0,
            jnp.concatenate([out_part, out_traded], axis=0),
            jnp.concatenate([out_traded, out_part], axis=0),
        ),
        1,
    )
    tokens_group = group_rows(mine)
    cot_group = group_rows(cot)

    hidden_units = gate_weight.shape[1] // 2
    gate_mine = lax.dynamic_slice_in_dim(gate_weight, core * hidden_units, hidden_units, 1)
    up_mine = lax.dynamic_slice_in_dim(up_weight, core * hidden_units, hidden_units, 1)
    down_mine = lax.dynamic_slice_in_dim(down_weight, core * hidden_units, hidden_units, 0)
    outer_low = (cot_group.astype(f32) * live_group).astype(bf16)
    mixed = group_rows(attention_low)
    branch = jnp.dot(mixed, output_full, preferred_element_type=f32)
    middle_rows = tokens_group.astype(f32) + live_group * branch
    scale_two = row_scale(middle_rows)
    unit = middle_rows * scale_two
    second = (unit * gain_two).astype(bf16)
    gate = jnp.dot(second, gate_mine, preferred_element_type=f32)
    up = jnp.dot(second, up_mine, preferred_element_type=f32)

    def gated(gate_in, up_in):
        return jax.nn.gelu(gate_in, approximate=True) * up_in

    hidden_value, gate_pull = jax.vjp(gated, gate, up)
    hidden = hidden_value.astype(bf16)
    hidden_grad = jnp.einsum("td,fd->tf", outer_low, down_mine, preferred_element_type=f32)
    gate_back, up_back = gate_pull(hidden_grad)
    gate_low = gate_back.astype(bf16)
    up_low = up_back.astype(bf16)
    second_grad = jnp.einsum("tf,df->td", gate_low, gate_mine, preferred_element_type=f32) + jnp.einsum(
        "tf,df->td", up_low, up_mine, preferred_element_type=f32
    )
    feed_gain_part = jnp.sum(second_grad * unit, axis=0)
    scaled = second_grad * gain_two
    middle_part = scale_two * (scaled - unit * jnp.mean(scaled * unit, axis=-1, keepdims=True))
    middle_part_low = (live_group * middle_part).astype(bf16)
    grad_part = jnp.einsum("td,id->ti", middle_part_low, output_full, preferred_element_type=f32)

    def group_sum(block):
        grid = block.reshape(4, length, block.shape[-1])
        sent = swap_core(jnp.stack([grid[1], grid[3]]).astype(bf16)).astype(f32)
        kept, passed = grid[0] + sent[0], grid[2] + sent[1]
        return kept + swap_x(passed.astype(bf16)).astype(f32)

    outer_own = outer_low[:length].astype(f32)
    grad_own = jnp.einsum("td,id->ti", outer_low[:length], output_full, preferred_element_type=f32)
    attention_grad = (group_sum(grad_part) + grad_own).astype(bf16)

    lane_head = jnp.arange(inner, dtype=jnp.int32) // (inner // heads)
    head_rows = (jnp.arange(8, dtype=jnp.int32)[:, None] == lane_head[None, :]).astype(f32)
    head_first = head_rows * (jnp.arange(inner, dtype=jnp.int32) % (inner // heads) == 0).astype(f32)[None, :]
    delta_rows = lax.dot_general(
        head_rows, attention_grad.astype(f32) * attention, CONTRACT_LAST, precision=HIGH, preferred_element_type=f32
    )
    log_rows = lax.dot_general(
        head_first, logs, CONTRACT_LAST, precision=HIGH, preferred_element_type=f32
    )
    back = {"state": None}

    def backward_use(step, pieces, blocks):
        query_blocks, grad_blocks, log_blocks, delta_blocks = pieces
        info = jnp.stack([here, live_count, *blocks]).astype(jnp.int32)
        back["state"] = key_call(
            info, keys, values, query_blocks, grad_blocks, log_blocks, delta_blocks, turned, back["state"], step == middle
        )

    query_sum, diagonals = query_call(
        info_all, query, attention_grad, attention, logs, keys_all, values_all, tiles
    )
    ring_gather([query, attention_grad, log_rows, delta_rows], backward_use)
    keys_low, values_low = back["state"]
    query_low = query_sum.astype(bf16)

    feed = group_sum(jnp.dot(hidden, down_mine, preferred_element_type=f32))
    result = (middle_rows[:length] + live_own * feed).astype(bf16)
    middle_grad = outer_own + group_sum(middle_part)
    branch_low = (live_own * middle_grad).astype(bf16)

    good = (lane_z // 2) == side
    z_low = lane_z % 2
    route_one = route_of(
        lambda z, y, k, x: {(3, 0): (2, y, k, x), (0, 1): (1, y, k, x)}.get((z, x))
    )
    route_two = route_of(
        lambda z, y, k, x: {(2, 0): (1, y, k, x), (1, 1): (2, y, k, x)}.get((z, x))
    )
    route_three = route_of(
        lambda z, y, k, x: (z ^ 1, y, k, x) if z // 2 == x and z % 2 != k else None
    )
    route_four = route_of(
        lambda z, y, k, x: (z, y, 1 - k, x) if z // 2 == x and z % 2 == k else None
    )
    route_five = route_of(lambda z, y, k, x: (z, y, k, 1 - x) if z // 2 == x else None)

    def add_low(left, right):
        return (left.astype(f32) + right.astype(f32)).astype(bf16)

    def halves(block, bit):
        size = block.shape[0] // 2
        kept = lax.dynamic_slice_in_dim(block, bit * size, size, 0)
        sent = lax.dynamic_slice_in_dim(block, (1 - bit) * size, size, 0)
        return kept, sent

    def reduce_rows(block):
        kept, sent = halves(block, lane_y)
        total = add_low(kept, spread(sent, route_y))
        total = add_low(total, spread(total, route_one))
        total = add_low(total, spread(total, route_two))
        total = add_low(total, spread(total, route_three))
        kept, sent = halves(total, core)
        quarter = jnp.where(z_low == core, kept, spread(sent, route_four))
        kept, sent = halves(quarter, side)
        return jnp.where(good, kept, spread(sent, route_five)).astype(f32)

    down_full = jnp.einsum("tf,td->fd", hidden, outer_low, preferred_element_type=f32).astype(bf16)
    gate_full = jnp.einsum("tf,td->fd", gate_low, second, preferred_element_type=f32).astype(bf16)
    up_full = jnp.einsum("tf,td->fd", up_low, second, preferred_element_type=f32).astype(bf16)
    down_out = reduce_rows(down_full)
    gate_out = jnp.transpose(reduce_rows(gate_full))
    up_out = jnp.transpose(reduce_rows(up_full))

    columns = inner // places
    target = jnp.arange(inner // 2, dtype=jnp.int32)
    group_index, inside = target // columns, target % columns
    y_bit = group_index // rows_of_chips
    z_index = group_index % rows_of_chips

    def picker(which):
        source = (((z_index * 2 + y_bit) * 2) + which) * columns + inside
        return (jnp.arange(inner, dtype=jnp.int32)[:, None] == source[None, :]).astype(bf16)

    pick_kept, pick_sent = picker(core), picker(1 - core)

    def pick(block, chooser):
        return jnp.dot(block, chooser, preferred_element_type=f32).astype(bf16)

    def lanes_of(block):
        low_half, high_half = block[:, :half], block[:, half:]
        return (
            jnp.where(side == 0, low_half, high_half),
            jnp.where(side == 0, high_half, low_half),
        )

    def outer_product(left, right):
        return jnp.einsum("ti,td->id", left, right, preferred_element_type=f32)

    def reduce_projection(rows, others):
        kept_x, sent_x, kept_y, sent_y = [], [], [], []
        for block, (lane_kept, lane_sent) in zip(rows, others):
            mine_rows, other_rows = pick(block, pick_kept), pick(block, pick_sent)
            kept_x.append(outer_product(mine_rows, lane_kept))
            kept_y.append(outer_product(mine_rows, lane_sent))
            sent_x.append(outer_product(other_rows, lane_kept).astype(bf16))
            sent_y.append(outer_product(other_rows, lane_sent).astype(bf16))
        got_x = swap_core(jnp.stack(sent_x)).astype(f32)
        got_y = swap_core(jnp.stack(sent_y)).astype(f32)
        passed = (jnp.stack(kept_y) + got_y).astype(bf16)
        total = (jnp.stack(kept_x) + got_x + swap_x(passed).astype(f32)).astype(bf16)
        for bit, route in ((lane_y, route_y), (lane_z // 2, route_far), (lane_z % 2, route_near)):
            size = total.shape[1] // 2
            kept = lax.dynamic_slice_in_dim(total, bit * size, size, 1)
            sent = lax.dynamic_slice_in_dim(total, (1 - bit) * size, size, 1)
            total = add_low(kept, spread(sent, route))
        return total.astype(f32)

    output_out = reduce_projection([attention_low], [lanes_of(branch_low)])[0]
    first_lanes = lanes_of(first)
    projection_out = reduce_projection([query_low, keys_low, values_low], [first_lanes] * 3)
    projection_out = jnp.transpose(projection_out, (0, 2, 1))

    joined = jnp.concatenate([keys_low, values_low, query_low], axis=1)
    first_grad = jnp.einsum("ti,di->td", joined, weight_all, preferred_element_type=f32)
    unit_one = inputs * scale_one
    gain_one_part = jnp.sum(first_grad * unit_one, axis=0)
    scaled_one = first_grad * gain_one
    input_gradient = (
        middle_grad
        + scale_one * (scaled_one - unit_one * jnp.mean(scaled_one * unit_one, axis=-1, keepdims=True))
    ).astype(bf16)

    lines = diagonals[:, :2].reshape(heads, SPAN_ROW)
    table_part = lax.dot_general(
        onehot, lines, (((0,), (1,)), ((), ())), precision=HIGH, preferred_element_type=f32
    )
    table_sum = all_sum(table_part)
    feed_gain_sum = all_sum(feed_gain_part)
    gain_one_sum = all_sum(gain_one_part)

    def my_half(block):
        size = block.shape[0] // 2
        return lax.dynamic_slice_in_dim(block, side * size, size, 0)

    return (
        result[None],
        input_gradient[None],
        my_half(gain_one_sum),
        projection_out[0],
        projection_out[1],
        projection_out[2],
        output_out,
        my_half(table_sum),
        my_half(feed_gain_sum),
        gate_out,
        up_out,
        down_out,
    )


def fetch_columns(weight, core, swap_x, swap_core):
    count = weight.shape[0] // 2
    part = swap_x(lax.dynamic_slice_in_dim(weight, core * count, count, 0))
    return part, swap_core(part)


def solution(mesh):
    placed = (
        P("wsh", "ctx", None),
        P("wsh", None),
        P(),
        P("wsh"),
        P("wsh", None),
        P("wsh", None),
        P("wsh", None),
        P(None, "wsh"),
        P("wsh", None),
        P("wsh"),
        P(None, "wsh"),
        P(None, "wsh"),
        P("wsh", None),
        P("wsh", "ctx", None),
    )
    step = grouped_body if mesh.shape["ctx"] == 16 else body
    return jax.shard_map(
        step,
        mesh=mesh,
        in_specs=placed,
        out_specs=(
            P("wsh", "ctx", None),
            P("wsh", "ctx", None),
            P("wsh"),
            P("wsh", "ctx"),
            P("wsh", "ctx"),
            P("wsh", "ctx"),
            P("ctx", "wsh"),
            P("wsh", None),
            P("wsh"),
            P(None, ("ctx", "wsh")),
            P(None, ("ctx", "wsh")),
            P(("ctx", "wsh"), None),
        ),
        check_vma=False,
    )
```

```python
import functools

import jax
import jax.numpy as jnp
from jax import lax
from jax.experimental import pallas as pl
from jax.experimental.pallas import tpu as pltpu
from jax.sharding import PartitionSpec as P

EPSILON = 1e-06
MASKED = -1e30
HIGH = lax.Precision.HIGHEST


def shifted(block, axis, distance):
    devices = range(lax.axis_size(axis))
    route = [((i - distance) % len(devices), i) for i in devices]
    return lax.ppermute(block, axis, route)


def row_scale(values):
    return lax.rsqrt(jnp.mean(values * values, axis=-1, keepdims=True) + EPSILON)


def normalize(values, gain):
    return values * row_scale(values) * gain


def skew_expand(offset_bias, length):
    count = offset_bias.shape[0]
    padded = jnp.pad(offset_bias, ((0, 0), (0, 1)))
    tiled = jnp.tile(padded, (1, length))[:, : length * (2 * length - 1)]
    return tiled.reshape(count, length, 2 * length - 1)[:, :, length - 1 :]


def diagonal_sums(grid, length):
    count = grid.shape[0]
    wide = jnp.pad(grid, ((0, 0), (0, 0), (length - 1, 0))).reshape(
        count, length * (2 * length - 1)
    )
    wide = jnp.pad(wide, ((0, 0), (0, length)))
    return jnp.sum(wide.reshape(count, length, 2 * length), axis=1)[:, : 2 * length - 1]


def bucket_onehot(offset_start, length, buckets, bucket_count):
    reach = (buckets.shape[0] + 1) // 2
    offsets = offset_start + jnp.arange(2 * length - 1, dtype=jnp.int32) - (length - 1)
    spots = jnp.clip(offsets, 1 - reach, reach - 1) + (reach - 1)
    table_spots = jnp.arange(buckets.shape[0], dtype=jnp.int32)
    chosen = jnp.sum(jnp.where(spots[:, None] == table_spots[None, :], buckets[None, :], 0), axis=1)
    return chosen[:, None] == jnp.arange(bucket_count, dtype=jnp.int32)[None, :]


def block_scores(query3, keys3, table, onehot, key_live, length):
    scores = jnp.einsum("ihd,jhd->hij", query3, keys3, preferred_element_type=jnp.float32)
    offset_bias = jnp.einsum(
        "ob,bh->ho", onehot.astype(jnp.bfloat16), table, preferred_element_type=jnp.float32
    )
    scores = scores + skew_expand(offset_bias, length)
    return jnp.where(key_live[None, None, :], scores, MASKED)


def body(
    tokens,
    lengths,
    buckets,
    attention_gain,
    query_weight,
    key_weight,
    value_weight,
    output_weight,
    bias_table,
    feed_gain,
    gate_weight,
    up_weight,
    down_weight,
    cotangent,
):
    (
        gain_first,
        query_full,
        key_full,
        value_full,
        output_full,
        table_full,
        gain_second,
        gate_full,
        up_full,
        down_full,
    ) = (
        lax.all_gather(attention_gain, "wsh", axis=0, tiled=True),
        lax.all_gather(query_weight, "wsh", axis=0, tiled=True),
        lax.all_gather(key_weight, "wsh", axis=0, tiled=True),
        lax.all_gather(value_weight, "wsh", axis=0, tiled=True),
        lax.all_gather(output_weight, "wsh", axis=1, tiled=True),
        lax.all_gather(bias_table, "wsh", axis=0, tiled=True),
        lax.all_gather(feed_gain, "wsh", axis=0, tiled=True),
        lax.all_gather(gate_weight, "wsh", axis=1, tiled=True),
        lax.all_gather(up_weight, "wsh", axis=1, tiled=True),
        lax.all_gather(down_weight, "wsh", axis=0, tiled=True),
    )
    length = tokens.shape[1]
    heads = table_full.shape[1]
    bucket_count = table_full.shape[0]
    inner = query_full.shape[1]
    head_size = inner // heads
    seq_count = lengths.shape[1]
    wide_count = lax.axis_size("ctx")
    span = wide_count // seq_count
    here = lax.axis_index("ctx")
    my_seq = here % seq_count
    my_block = here // seq_count
    seq_pick = jnp.arange(seq_count, dtype=jnp.int32) == my_seq
    my_length = jnp.sum(jnp.where(seq_pick, lengths[0], 0))
    positions = jnp.arange(length, dtype=jnp.int32)
    live = (my_block * length + positions < my_length).astype(jnp.float32)[:, None]
    inputs = tokens[0].astype(jnp.float32)
    gain_one = gain_first.astype(jnp.float32)
    first = normalize(inputs, gain_one).astype(jnp.bfloat16)
    query = jnp.dot(first, query_full, preferred_element_type=jnp.float32).astype(jnp.bfloat16)
    keys = jnp.dot(first, key_full, preferred_element_type=jnp.float32).astype(jnp.bfloat16)
    values = jnp.dot(first, value_full, preferred_element_type=jnp.float32).astype(jnp.bfloat16)
    query3 = query.reshape(length, heads, head_size)

    def forward_step(carry, block_keys, block_values, key_block):
        run_max, run_total, running = carry
        onehot = bucket_onehot((key_block - my_block) * length, length, buckets, bucket_count)
        key_live = key_block * length + positions < my_length
        scores = block_scores(
            query3,
            block_keys.reshape(length, heads, head_size),
            table_full,
            onehot,
            key_live,
            length,
        )
        new_max = jnp.maximum(run_max, jnp.max(scores, axis=2))
        weights = jnp.exp(scores - new_max[:, :, None])
        factor = jnp.exp(run_max - new_max)
        run_total = run_total * factor + jnp.sum(weights, axis=2)
        update = jnp.einsum(
            "hij,jhd->ihd",
            weights.astype(jnp.bfloat16),
            block_values.reshape(length, heads, head_size),
            preferred_element_type=jnp.float32,
        )
        running = running * jnp.transpose(factor)[:, :, None] + update
        return (new_max, run_total, running)

    start_carry = (
        jnp.full((heads, length), MASKED, jnp.float32),
        jnp.zeros((heads, length), jnp.float32),
        jnp.zeros((length, heads, head_size), jnp.float32),
    )
    start_carry = forward_step(start_carry, keys, values, my_block)
    stored = ()

    def cycle_turn(turn, state):
        carry, block_keys, block_values, stored_blocks = state
        block_keys, block_values = shifted((block_keys, block_values), "ctx", seq_count)
        carry = forward_step(carry, block_keys, block_values, (my_block - turn) % span)
        return (carry, block_keys, block_values, stored_blocks)

    (run_max, run_total, running), _, _, stored = lax.fori_loop(
        1, span, cycle_turn, (start_carry, keys, values, stored)
    )
    log_total = run_max + jnp.log(run_total)
    attention = (running / jnp.transpose(run_total)[:, :, None]).reshape(length, inner)
    attention_low = attention.astype(jnp.bfloat16)
    branch = jnp.dot(attention_low, output_full, preferred_element_type=jnp.float32)
    middle = inputs + live * branch
    gain_two = gain_second.astype(jnp.float32)
    second = normalize(middle, gain_two).astype(jnp.bfloat16)
    gate = jnp.dot(second, gate_full, preferred_element_type=jnp.float32)
    up = jnp.dot(second, up_full, preferred_element_type=jnp.float32)
    hidden = (jax.nn.gelu(gate, approximate=True) * up).astype(jnp.bfloat16)
    feed = jnp.dot(hidden, down_full, preferred_element_type=jnp.float32)
    result = (middle + live * feed).astype(jnp.bfloat16)
    outer = live * cotangent[0].astype(jnp.float32)
    outer_low = outer.astype(jnp.bfloat16)
    down_grad = jnp.einsum("tf,td->fd", hidden, outer_low, preferred_element_type=jnp.float32)
    hidden_grad = jnp.einsum("td,fd->tf", outer_low, down_full, preferred_element_type=jnp.float32)

    def gated(gate_in, up_in):
        return jax.nn.gelu(gate_in, approximate=True) * up_in

    _, gate_pull = jax.vjp(gated, gate, up)
    gate_back, up_back = gate_pull(hidden_grad)
    gate_low = gate_back.astype(jnp.bfloat16)
    up_low = up_back.astype(jnp.bfloat16)
    gate_grad = jnp.einsum("td,tf->df", second, gate_low, preferred_element_type=jnp.float32)
    up_grad = jnp.einsum("td,tf->df", second, up_low, preferred_element_type=jnp.float32)
    second_grad = jnp.einsum(
        "tf,df->td", gate_low, gate_full, preferred_element_type=jnp.float32
    ) + jnp.einsum("tf,df->td", up_low, up_full, preferred_element_type=jnp.float32)
    _, norm_pull = jax.vjp(normalize, middle, gain_two)
    middle_back, gain_two_grad = norm_pull(second_grad)
    middle_grad = outer + middle_back
    branch_low = (live * middle_grad).astype(jnp.bfloat16)
    output_grad = jnp.einsum(
        "ti,td->id", attention_low, branch_low, preferred_element_type=jnp.float32
    )
    attention_grad = jnp.einsum(
        "td,id->ti", branch_low, output_full, preferred_element_type=jnp.float32
    ).astype(jnp.bfloat16)
    attention_grad3 = attention_grad.reshape(length, heads, head_size)
    delta = jnp.transpose(
        jnp.sum(
            (attention_grad.astype(jnp.float32) * attention).reshape(length, heads, head_size),
            axis=2,
        )
    )

    def backward_step(block_keys, block_values, key_block):
        keys3 = block_keys.reshape(length, heads, head_size)
        values3 = block_values.reshape(length, heads, head_size)
        onehot = bucket_onehot((key_block - my_block) * length, length, buckets, bucket_count)
        key_live = key_block * length + positions < my_length
        scores = block_scores(query3, keys3, table_full, onehot, key_live, length)
        probs = jnp.exp(scores - log_total[:, :, None])
        prob_grad = jnp.einsum(
            "ihd,jhd->hij", attention_grad3, values3, preferred_element_type=jnp.float32
        )
        score_grad = (probs * (prob_grad - delta[:, :, None])).astype(jnp.bfloat16)
        part_query = jnp.einsum(
            "hij,jhd->ihd", score_grad, keys3, preferred_element_type=jnp.float32
        )
        part_keys = jnp.einsum(
            "hij,ihd->jhd", score_grad, query3, preferred_element_type=jnp.float32
        )
        part_values = jnp.einsum(
            "hij,ihd->jhd",
            probs.astype(jnp.bfloat16),
            attention_grad3,
            preferred_element_type=jnp.float32,
        )
        part_table = jnp.einsum(
            "ho,ob->bh",
            diagonal_sums(score_grad.astype(jnp.float32), length),
            onehot.astype(jnp.float32),
            precision=HIGH,
        )
        return (
            part_query.reshape(length, inner),
            part_keys.reshape(length, inner),
            part_values.reshape(length, inner),
            part_table,
        )

    def back_turn(turn, state):
        block_keys, block_values, keys_sum, values_sum, query_sum, table_sum = state
        part_query, part_keys, part_values, part_table = backward_step(
            block_keys, block_values, (my_block - turn) % span
        )
        keys_next = keys_sum + part_keys
        values_next = values_sum + part_values
        keys_sum, values_sum = (
            shifted(keys_next.astype(jnp.bfloat16), "ctx", seq_count).astype(keys_next.dtype),
            shifted(values_next.astype(jnp.bfloat16), "ctx", seq_count).astype(values_next.dtype),
        )
        block_keys, block_values = shifted((block_keys, block_values), "ctx", seq_count)
        return (
            block_keys,
            block_values,
            keys_sum,
            values_sum,
            query_sum + part_query,
            table_sum + part_table,
        )

    zeros_rows = jnp.zeros((length, inner), jnp.float32)
    back_state = (
        keys,
        values,
        zeros_rows,
        zeros_rows,
        zeros_rows,
        jnp.zeros((bucket_count, heads), jnp.float32),
    )
    _, _, keys_sum, values_sum, query_sum, table_grad = lax.fori_loop(
        0, span, back_turn, back_state
    )
    query_low = query_sum.astype(jnp.bfloat16)
    keys_low = keys_sum.astype(jnp.bfloat16)
    values_low = values_sum.astype(jnp.bfloat16)
    query_grad = jnp.einsum("td,ti->di", first, query_low, preferred_element_type=jnp.float32)
    key_grad = jnp.einsum("td,ti->di", first, keys_low, preferred_element_type=jnp.float32)
    value_grad = jnp.einsum("td,ti->di", first, values_low, preferred_element_type=jnp.float32)
    first_grad = (
        jnp.einsum("ti,di->td", query_low, query_full, preferred_element_type=jnp.float32)
        + jnp.einsum("ti,di->td", keys_low, key_full, preferred_element_type=jnp.float32)
        + jnp.einsum("ti,di->td", values_low, value_full, preferred_element_type=jnp.float32)
    )
    _, first_pull = jax.vjp(normalize, inputs, gain_one)
    inputs_back, gain_one_grad = first_pull(first_grad)
    input_gradient = (middle_grad + inputs_back).astype(jnp.bfloat16)
    small = lax.psum((gain_one_grad, table_grad, gain_two_grad), "ctx")
    wide = (
        lax.psum_scatter(query_grad, "ctx", scatter_dimension=1, tiled=True),
        lax.psum_scatter(key_grad, "ctx", scatter_dimension=1, tiled=True),
        lax.psum_scatter(value_grad, "ctx", scatter_dimension=1, tiled=True),
        lax.psum_scatter(output_grad, "ctx", scatter_dimension=0, tiled=True),
        lax.psum_scatter(gate_grad, "ctx", scatter_dimension=1, tiled=True),
        lax.psum_scatter(up_grad, "ctx", scatter_dimension=1, tiled=True),
        lax.psum_scatter(down_grad, "ctx", scatter_dimension=0, tiled=True),
    )
    final = (
        lax.psum_scatter(
            small[0].astype(jnp.bfloat16), "wsh", scatter_dimension=0, tiled=True
        ).astype(jnp.float32),
        lax.psum_scatter(
            small[1].astype(jnp.bfloat16), "wsh", scatter_dimension=0, tiled=True
        ).astype(jnp.float32),
        lax.psum_scatter(
            small[2].astype(jnp.bfloat16), "wsh", scatter_dimension=0, tiled=True
        ).astype(jnp.float32),
        lax.psum_scatter(
            wide[0].astype(jnp.bfloat16), "wsh", scatter_dimension=0, tiled=True
        ).astype(jnp.float32),
        lax.psum_scatter(
            wide[1].astype(jnp.bfloat16), "wsh", scatter_dimension=0, tiled=True
        ).astype(jnp.float32),
        lax.psum_scatter(
            wide[2].astype(jnp.bfloat16), "wsh", scatter_dimension=0, tiled=True
        ).astype(jnp.float32),
        lax.psum_scatter(
            wide[3].astype(jnp.bfloat16), "wsh", scatter_dimension=1, tiled=True
        ).astype(jnp.float32),
        lax.psum_scatter(
            wide[4].astype(jnp.bfloat16), "wsh", scatter_dimension=1, tiled=True
        ).astype(jnp.float32),
        lax.psum_scatter(
            wide[5].astype(jnp.bfloat16), "wsh", scatter_dimension=1, tiled=True
        ).astype(jnp.float32),
        lax.psum_scatter(
            wide[6].astype(jnp.bfloat16), "wsh", scatter_dimension=0, tiled=True
        ).astype(jnp.float32),
    )
    gain_one_out, table_out, gain_two_out = (final[0], final[1], final[2])
    query_out, key_out, value_out, output_out = (final[3], final[4], final[5], final[6])
    gate_out, up_out, down_out = (final[7], final[8], final[9])
    return (
        result[None],
        input_gradient[None],
        gain_one_out,
        query_out,
        key_out,
        value_out,
        output_out,
        table_out,
        gain_two_out,
        gate_out,
        up_out,
        down_out,
    )


BLOCK = 256
PAIR = 128
SPAN_ROW = 1024
CONTRACT_LAST = (((1,), (1,)), ((), ()))
AXES = ("ctx", "wsh")
LEFT_LANE, RIGHT_LANE, DEAD_LANE = 125, 126, 127
NEAR, BEFORE, AFTER = 0, 1, 2


def lanes(rows=BLOCK):
    return lax.broadcasted_iota(jnp.int32, (rows, PAIR), 1)


def only_head(block, second):
    lane = lanes(block.shape[0])
    keep = lane >= PAIR // 2 if second else lane < PAIR // 2
    return jnp.where(keep, block, jnp.zeros_like(block))


def pair_select(first, second):
    return jnp.where(lanes(first.shape[0]) < PAIR // 2, first, second)


def contract_last(left, right):
    return lax.dot_general(left, right, CONTRACT_LAST, preferred_element_type=jnp.float32)


def stack_heads(block):
    return jnp.concatenate([only_head(block, False), only_head(block, True)], axis=0)


def dead_rows(start, limit):
    row = lax.broadcasted_iota(jnp.int32, (BLOCK, PAIR), 0)
    return start + row >= limit


def other_aux(start, limit, kind):
    lane = lanes()
    value = jnp.where(jnp.logical_and(lane < 48, lane % 8 < 6), 1.0, 0.0)
    value = jnp.where(jnp.logical_and(lane == LEFT_LANE, kind == BEFORE), 1.0, value)
    value = jnp.where(jnp.logical_and(lane == RIGHT_LANE, kind == AFTER), 1.0, value)
    value = jnp.where(jnp.logical_and(lane == DEAD_LANE, dead_rows(start, limit)), MASKED, value)
    return value.astype(jnp.bfloat16)


def own_lanes(far_ref, head, heads):
    lane = lanes()
    value = jnp.where(lane == DEAD_LANE, 1.0, 0.0)
    value = jnp.where(lane == LEFT_LANE, far_ref[head], value)
    return jnp.where(lane == RIGHT_LANE, far_ref[heads + head], value)


def parts_of(value):
    first = value.astype(jnp.bfloat16).astype(jnp.float32)
    second = (value - first).astype(jnp.bfloat16).astype(jnp.float32)
    return first, second, value - first - second


def place_parts(base, value, lane_start):
    lane = lanes()
    for spot, part in enumerate(parts_of(value)):
        base = jnp.where(lane == lane_start + spot, part, base)
    return base


def kind_of(block, own):
    return jnp.where(block < own, BEFORE, AFTER)


def tiles_kernel(row_ref, tile_ref, turned_ref):
    row = row_ref[0]
    wide = pltpu.roll(
        jnp.broadcast_to(row, (BLOCK, SPAN_ROW)), SPAN_ROW - 255, 1, stride=1, stride_axis=0
    )
    for spot in range(3):
        tile = wide[:, spot * BLOCK : (spot + 1) * BLOCK]
        tile_ref[0, spot] = tile.astype(jnp.bfloat16)
        turned_ref[0, spot] = jnp.transpose(tile).astype(jnp.bfloat16)


def bias_tiles(offset_rows):
    heads = offset_rows.shape[0]
    shape = jax.ShapeDtypeStruct((heads, 3, BLOCK, BLOCK), jnp.bfloat16)
    spec = pl.BlockSpec((1, 3, BLOCK, BLOCK), lambda h: (h, 0, 0, 0))
    return pl.pallas_call(
        tiles_kernel,
        grid=(heads,),
        out_shape=(shape, shape),
        in_specs=[pl.BlockSpec((1, 1, SPAN_ROW), lambda h: (h, 0, 0))],
        out_specs=(spec, spec),
        name="bias_tiles",
    )(offset_rows[:, None, :])


def view_spec(row, lane_block):
    return pl.BlockSpec((BLOCK, PAIR), lambda p, i, f: (row, lane_block(p)))


def tile_spec():
    return pl.BlockSpec((2, 3, BLOCK, BLOCK), lambda p, i, f: (p, 0, 0, 0))


def run_pairs(kernel, info, far, operands, in_specs, out_shape, out_specs, work, name):
    pairs = 3
    return pl.pallas_call(
        kernel,
        grid_spec=pltpu.PrefetchScalarGridSpec(
            num_scalar_prefetch=2, grid=(pairs,), in_specs=in_specs, out_specs=out_specs
        ),
        out_shape=out_shape,
        cost_estimate=pl.CostEstimate(
            flops=2 * pairs * work * BLOCK * BLOCK * BLOCK,
            bytes_accessed=pairs * work * BLOCK * PAIR * 2,
            transcendentals=pairs * work * BLOCK * BLOCK,
        ),
        name=name,
    )(info, far, *operands)


def forward_kernel(count, near, first, last, heads, info_ref, far_ref, *refs):
    refs = list(refs)
    query_ref = refs.pop(0)
    key_refs, refs = refs[:count], refs[count:]
    value_refs, refs = refs[:count], refs[count:]
    tile_ref = refs.pop(0) if near else None
    pair = pl.program_id(0)
    own = info_ref[0]
    query = query_ref[...]
    if first:
        old_max = jnp.full((BLOCK, PAIR), MASKED, jnp.float32)
        total = None
    else:
        max_ref, total_ref = refs.pop(0), refs.pop(0)
        old_max, total = max_ref[...], total_ref[...]
    keys = []
    for spot in range(count):
        block, limit = info_ref[1 + 2 * spot], info_ref[2 + 2 * spot]
        kind = NEAR if near else kind_of(block, own)
        keys.append(
            jnp.concatenate([key_refs[spot][...], other_aux(block * BLOCK, limit, kind)], axis=1)
        )
    tops, weights = [], []
    for head in range(2):
        aux = own_lanes(far_ref, 2 * pair + head, heads).astype(jnp.bfloat16)
        left = jnp.concatenate([only_head(query, head == 1), aux], axis=1)
        scores = []
        for spot in range(count):
            score = contract_last(left, keys[spot])
            if near:
                place = jnp.clip(info_ref[1 + 2 * spot] - own, -1, 1) + 1
                score = score + tile_ref[head, place].astype(jnp.float32)
            scores.append(score)
        top = functools.reduce(jnp.maximum, scores)
        lane = head * (PAIR // 2)
        top = jnp.maximum(old_max[:, lane : lane + 1], jnp.max(top, axis=1, keepdims=True))
        tops.append(top)
        weights.append([jnp.exp(score - top).astype(jnp.bfloat16) for score in scores])
    new_max = pair_select(tops[0], tops[1])
    ones = stack_heads(jnp.ones((BLOCK, PAIR), jnp.bfloat16))
    update = None
    for spot in range(count):
        right = jnp.concatenate([stack_heads(value_refs[spot][...]), ones], axis=1)
        left = jnp.concatenate([weights[0][spot], weights[1][spot]], axis=1)
        part = jnp.dot(left, right, preferred_element_type=jnp.float32)
        update = part if update is None else update + part
    if not first:
        factor = jnp.exp(old_max - new_max)
        update = update + total * jnp.concatenate([factor, factor], axis=1)
    if last:
        out_ref, low_ref, aux_ref = refs
        out = update[:, :PAIR] / update[:, PAIR:]
        out_ref[...] = out
        low_ref[...] = out.astype(jnp.bfloat16)
        log = -(new_max + jnp.log(update[:, PAIR:]))
        base = jnp.where(lanes() >= LEFT_LANE, 1.0, 0.0)
        base = jnp.where(pair == 0, base, aux_ref[...])
        for head in range(2):
            lane = head * (PAIR // 2)
            base = place_parts(base, log[:, lane : lane + 1], 8 * (2 * pair + head) + 3)
        aux_ref[...] = base
    else:
        max_out, total_out = refs
        max_out[...] = new_max
        total_out[...] = update


def forward_call(info, far, query, blocks, tiles, state, last):
    count, near, first = len(blocks), tiles is not None, state is None
    inner = query.shape[1]
    pairs = inner // PAIR
    in_specs = [view_spec(0, lambda p: p)]
    in_specs += [view_spec(row, lambda p: p) for _, row in blocks]
    in_specs += [view_spec(row, lambda p: p + pairs) for _, row in blocks]
    operands = [query] + [array for array, _ in blocks] * 2
    if near:
        in_specs.append(tile_spec())
        operands.append(tiles)
    block = view_spec(0, lambda p: p)
    double = pl.BlockSpec((BLOCK, 2 * PAIR), lambda p, i, f: (0, p))
    if not first:
        in_specs += [block, double]
        operands += list(state)
    f32 = functools.partial(jax.ShapeDtypeStruct, dtype=jnp.float32)
    if last:
        out_shape = (
            f32((BLOCK, inner)),
            jax.ShapeDtypeStruct((BLOCK, inner), jnp.bfloat16),
            f32((BLOCK, PAIR)),
        )
        out_specs = (block, block, view_spec(0, lambda p: 0))
    else:
        out_shape = (f32((BLOCK, inner)), f32((BLOCK, 2 * inner)))
        out_specs = (block, double)
    kernel = functools.partial(forward_kernel, count, near, first, last, 2 * pairs)
    return run_pairs(
        kernel, info, far, operands, in_specs, out_shape, out_specs, 6 * count, "attention_forward"
    )


def head_aux(aux, head, start):
    lane = lanes()
    keep = jnp.logical_and(lane // 8 == head, jnp.logical_and(lane % 8 >= start, lane % 8 < start + 3))
    return jnp.where(jnp.logical_and(keep, lane < 48), aux, 0.0)


def query_kernel(count, near, first, last, heads, info_ref, far_ref, *refs):
    refs = list(refs)
    query_ref, grad_ref, aux_ref = refs.pop(0), refs.pop(0), refs.pop(0)
    key_refs, refs = refs[:count], refs[count:]
    value_refs, refs = refs[:count], refs[count:]
    tile_ref = refs.pop(0) if near else None
    pair = pl.program_id(0)
    own = info_ref[0]
    query, grad = query_ref[...], grad_ref[...]
    aux = aux_ref[...].astype(jnp.float32)
    total = None if first else refs.pop(0)[...]
    lefts, grads = [], []
    for head in range(2):
        which = 2 * pair + head
        mine = own_lanes(far_ref, which, heads) + head_aux(aux, which, 3)
        lefts.append(jnp.concatenate([only_head(query, head == 1), mine.astype(jnp.bfloat16)], axis=1))
        delta = head_aux(aux, which, 0).astype(jnp.bfloat16)
        grads.append(jnp.concatenate([only_head(grad, head == 1), delta], axis=1))
    if near:
        diag_ref = refs.pop()
        strips = [[jnp.zeros((BLOCK, BLOCK), jnp.float32)] * 3 for _ in range(2)]
    lane = lanes()
    for spot in range(count):
        block, limit = info_ref[1 + 2 * spot], info_ref[2 + 2 * spot]
        kind = NEAR if near else kind_of(block, own)
        key, value = key_refs[spot][...], value_refs[spot][...]
        side = other_aux(block * BLOCK, limit, kind)
        wide_key = jnp.concatenate([key, side], axis=1)
        wide_value = jnp.concatenate([value, jnp.where(lane < 48, side, jnp.zeros_like(side))], axis=1)
        place = jnp.clip(block - own, -1, 1) + 1
        pieces, counts = [], []
        for head in range(2):
            scores = contract_last(lefts[head], wide_key)
            if near:
                scores = scores + tile_ref[head, place].astype(jnp.float32)
            score_grad = jnp.exp(scores) * contract_last(grads[head], wide_value)
            if near:
                strips[head] = [
                    strip + jnp.where(place == spot_of, score_grad, 0.0)
                    for spot_of, strip in enumerate(strips[head])
                ]
            pieces.append(score_grad.astype(jnp.bfloat16))
            counts.append(jnp.where(lane == 4 * head + kind, 1.0, 0.0).astype(jnp.bfloat16))
        right = jnp.concatenate([stack_heads(key), jnp.concatenate(counts, axis=0)], axis=1)
        part = jnp.dot(jnp.concatenate(pieces, axis=1), right, preferred_element_type=jnp.float32)
        total = part if total is None else total + part
    if near:
        rows = []
        flip = (
            lax.broadcasted_iota(jnp.int32, (BLOCK, BLOCK), 0)
            + lax.broadcasted_iota(jnp.int32, (BLOCK, BLOCK), 1)
            == BLOCK - 1
        ).astype(jnp.float32)
        for head in range(2):
            wide = jnp.concatenate(strips[head] + [jnp.zeros((BLOCK, BLOCK), jnp.float32)], axis=1)
            flipped = jnp.dot(flip, wide, precision=HIGH, preferred_element_type=jnp.float32)
            turned = pltpu.roll(flipped, 0, 1, stride=1, stride_axis=0)
            rows.append(jnp.sum(turned, axis=0, keepdims=True))
        diag_ref[0] = jnp.concatenate(rows + [jnp.zeros((6, SPAN_ROW), jnp.float32)], axis=0)
    if last:
        low_ref, sum_ref = refs
        low_ref[...] = total[:, :PAIR].astype(jnp.bfloat16)
        sum_ref[0] = jnp.broadcast_to(jnp.sum(total[:, PAIR:], axis=0, keepdims=True), (8, PAIR))
    else:
        (total_ref,) = refs
        total_ref[...] = total


def query_call(info, far, query, grads, blocks, tiles, state, last):
    count, near, first = len(blocks), tiles is not None, state is None
    inner = query.shape[1]
    pairs = inner // PAIR
    own = view_spec(0, lambda p: p)
    in_specs = [own, own, view_spec(0, lambda p: pairs)]
    in_specs += [view_spec(row, lambda p: p) for _, row in blocks]
    in_specs += [view_spec(row, lambda p: p + pairs) for _, row in blocks]
    operands = [query, grads, grads] + [array for array, _ in blocks] * 2
    if near:
        in_specs.append(tile_spec())
        operands.append(tiles)
    double = pl.BlockSpec((BLOCK, 2 * PAIR), lambda p, i, f: (0, p))
    if not first:
        in_specs.append(double)
        operands.append(state)
    f32 = functools.partial(jax.ShapeDtypeStruct, dtype=jnp.float32)
    if last:
        out_shape = [jax.ShapeDtypeStruct((BLOCK, inner), jnp.bfloat16), f32((pairs, 8, PAIR))]
        out_specs = [own, pl.BlockSpec((1, 8, PAIR), lambda p, i, f: (p, 0, 0))]
    else:
        out_shape, out_specs = [f32((BLOCK, 2 * inner))], [double]
    if near:
        out_shape.append(f32((pairs, 8, SPAN_ROW)))
        out_specs.append(pl.BlockSpec((1, 8, SPAN_ROW), lambda p, i, f: (p, 0, 0)))
    kernel = functools.partial(query_kernel, count, near, first, last, 2 * pairs)
    return run_pairs(
        kernel, info, far, operands, in_specs, out_shape, out_specs, 8 * count, "attention_query_grad"
    )


def key_kernel(count, near, first, last, heads, info_ref, far_ref, *refs):
    refs = list(refs)
    key_ref, value_ref = refs.pop(0), refs.pop(0)
    query_refs, refs = refs[:count], refs[count:]
    grad_refs, refs = refs[:count], refs[count:]
    aux_refs, refs = refs[:count], refs[count:]
    tile_ref = refs.pop(0) if near else None
    pair = pl.program_id(0)
    own = info_ref[0]
    key, value = key_ref[...], value_ref[...]
    key_sum = value_sum = None
    if not first:
        key_sum, value_sum = refs.pop(0)[...], refs.pop(0)[...]
    key_out, value_out = refs
    lane = lanes()
    keys = [only_head(key, False), only_head(key, True)]
    values = []
    for head in range(2):
        pick = jnp.logical_and(lane // 8 == 2 * pair + head, lane % 8 < 3)
        values.append(
            jnp.concatenate([only_head(value, head == 1), jnp.where(pick, 1.0, 0.0).astype(jnp.bfloat16)], axis=1)
        )
    for spot in range(count):
        block, limit = info_ref[1 + 2 * spot], info_ref[2 + 2 * spot]
        kind = NEAR if near else kind_of(own, block)
        query, grad, aux = query_refs[spot][...], grad_refs[spot][...], aux_refs[spot][...]
        wide_query = jnp.concatenate([query, aux], axis=1)
        wide_grad = jnp.concatenate([grad, aux], axis=1)
        place = jnp.clip(own - block, -1, 1) + 1
        dead = jnp.logical_and(lane == DEAD_LANE, dead_rows(own * BLOCK, limit))
        probs_low, slopes_low = [], []
        for head in range(2):
            which = 2 * pair + head
            pick = jnp.logical_and(lane // 8 == which, jnp.logical_and(lane % 8 >= 3, lane % 8 < 6))
            side = jnp.where(pick, 1.0, 0.0)
            if not near:
                constant = jnp.where(kind == BEFORE, far_ref[which], far_ref[heads + which])
                side = jnp.where(lane == RIGHT_LANE, constant, side)
            side = jnp.where(dead, MASKED, side).astype(jnp.bfloat16)
            scores = contract_last(jnp.concatenate([keys[head], side], axis=1), wide_query)
            if near:
                scores = scores + tile_ref[head, place].astype(jnp.float32)
            probs = jnp.exp(scores)
            slopes = probs * contract_last(values[head], wide_grad)
            probs_low.append(probs.astype(jnp.bfloat16))
            slopes_low.append(slopes.astype(jnp.bfloat16))
        part_value = jnp.dot(
            jnp.concatenate(probs_low, axis=1), stack_heads(grad), preferred_element_type=jnp.float32
        )
        part_key = jnp.dot(
            jnp.concatenate(slopes_low, axis=1), stack_heads(query), preferred_element_type=jnp.float32
        )
        key_sum = part_key if key_sum is None else key_sum + part_key
        value_sum = part_value if value_sum is None else value_sum + part_value
    key_out[...] = key_sum.astype(key_out.dtype)
    value_out[...] = value_sum.astype(value_out.dtype)


def key_call(info, far, joined, queries, grads, turned, state, last):
    count, near, first = len(queries), turned is not None, state is None
    inner = joined.shape[1] // 2
    pairs = inner // PAIR
    own = view_spec(0, lambda p: p)
    in_specs = [own, view_spec(0, lambda p: p + pairs)]
    in_specs += [view_spec(row, lambda p: p) for _, row in queries]
    in_specs += [view_spec(row, lambda p: p) for _, row in grads]
    in_specs += [view_spec(row, lambda p: pairs) for _, row in grads]
    arrays = [array for array, _ in grads]
    operands = [joined, joined] + [array for array, _ in queries] + arrays + arrays
    if near:
        in_specs.append(tile_spec())
        operands.append(turned)
    if not first:
        in_specs += [own, own]
        operands += list(state)
    shape = jax.ShapeDtypeStruct((BLOCK, inner), jnp.bfloat16 if last else jnp.float32)
    kernel = functools.partial(key_kernel, count, near, first, last, 2 * pairs)
    return run_pairs(
        kernel, info, far, operands, in_specs, (shape, shape), (own, own), 10 * count, "attention_key_grad"
    )


def grads_kernel(first_ref, second_ref, third_ref, out_ref, aux_ref, grad_ref):
    total = first_ref[...] + second_ref[...].astype(jnp.float32) + third_ref[...]
    low = total.astype(jnp.bfloat16)
    inner = low.shape[1]
    grad_ref[:, :inner] = low
    product = low.astype(jnp.float32) * out_ref[...]
    base = aux_ref[...]
    for pair in range(inner // PAIR):
        piece = product[:, pair * PAIR : (pair + 1) * PAIR]
        for head in range(2):
            delta = -jnp.sum(only_head(piece, head == 1), axis=1, keepdims=True)
            base = place_parts(base, delta, 8 * (2 * pair + head))
    grad_ref[:, inner:] = base.astype(jnp.bfloat16)


def finish_grads(first, second, third, out, aux):
    return pl.pallas_call(
        grads_kernel,
        out_shape=jax.ShapeDtypeStruct((BLOCK, out.shape[1] + PAIR), jnp.bfloat16),
        name="attention_out_grad",
    )(first, second, third, out, aux)


def grouped_body(
    tokens,
    lengths,
    buckets,
    attention_gain,
    query_weight,
    key_weight,
    value_weight,
    output_weight,
    bias_table,
    feed_gain,
    gate_weight,
    up_weight,
    down_weight,
    cotangent,
):
    bf16, f32 = jnp.bfloat16, jnp.float32
    places = lax.axis_size("ctx")
    chips = places // 2
    rows_of_chips = chips // 2
    here = lax.axis_index("ctx")
    side = lax.axis_index("wsh")
    core = here % 2
    chip = here // 2
    lane_y = chip % 2
    lane_z = chip // 2
    length = tokens.shape[1]
    half = tokens.shape[2] // 2
    heads = bias_table.shape[1]
    inner = query_weight.shape[1]
    nowhere = -(1 << 20)

    def spread(block, route):
        return lax.ppermute(block, AXES, route)

    def route_of(move):
        pairs = []
        for c in range(places):
            for w in range(2):
                target = move(c // 4, (c // 2) % 2, c % 2, w)
                if target is not None:
                    z, y, k, x = target
                    pairs.append((c * 2 + w, (((z * 2 + y) * 2) + k) * 2 + x))
        return pairs

    route_core = route_of(lambda z, y, k, x: (z, y, 1 - k, x))
    route_x = route_of(lambda z, y, k, x: (z, y, k, 1 - x))
    route_y = route_of(lambda z, y, k, x: (z, 1 - y, k, x))
    route_far = route_of(lambda z, y, k, x: (z ^ 2, y, k, x))
    route_near = route_of(lambda z, y, k, x: (z ^ 1, y, k, x))
    order = [(i, 0) for i in range(rows_of_chips)] + [
        (rows_of_chips - 1 - i, 1) for i in range(rows_of_chips)
    ]
    place = {spot: i for i, spot in enumerate(order)}
    route_ring = route_of(
        lambda z, y, k, x: (*order[(place[(z, y)] + 1 - 2 * k) % chips], k, x)
    )
    route_next = [
        ((c * 2 + w), (c + (1 if c % 2 else -1)) * 2 + w)
        for c in range(places)
        for w in range(2)
        if 0 <= c + (1 if c % 2 else -1) < places
    ]
    my_place = jnp.where(lane_y == 0, lane_z, 2 * rows_of_chips - 1 - lane_z)
    toward = jnp.where(core == 0, -1, 1)
    next_block = here - 1 + 2 * core
    has_next = jnp.logical_and(next_block >= 0, next_block < places)

    def chip_at(spot):
        spot = (spot + 2 * chips) % chips
        return jnp.where(
            spot < rows_of_chips, 2 * spot, 2 * (2 * rows_of_chips - 1 - spot) + 1
        )

    def swap_core(block):
        return spread(block, route_core)

    def swap_x(block):
        return spread(block, route_x)

    def both_sides(mine, other, axis):
        return jnp.where(
            side == 0,
            jnp.concatenate([mine, other], axis=axis),
            jnp.concatenate([other, mine], axis=axis),
        )

    def after(block, *others):
        return lax.optimization_barrier((block, *others))[0]

    live_count = jnp.minimum(lengths[0, 0], places * length)
    small = jnp.concatenate(
        [
            attention_gain,
            feed_gain,
            bias_table.reshape(-1),
            jnp.stack([live_count // 128, live_count % 128]).astype(bf16),
        ]
    )
    size_small = small.shape[0]
    small = jnp.pad(small, (0, -size_small % 2048)).reshape(-1, 128)
    small_other = swap_x(small).reshape(-1)
    gain_other = small_other[:half]
    feed_other = small_other[half : 2 * half]
    table_other = small_other[2 * half : size_small - 2].reshape(bias_table.shape)
    counts = small_other[size_small - 2 : size_small].astype(f32).astype(jnp.int32)
    count_other = counts[0] * 128 + counts[1]
    quarter = half // 2

    def my_rows(block, which, count):
        return lax.dynamic_slice_in_dim(block, which * count, count, 0)

    projections = [key_weight, value_weight, query_weight]
    sent_rows = jnp.concatenate([my_rows(w, core, quarter) for w in projections], axis=1)
    part = swap_x(sent_rows)
    traded = swap_core(part)
    other_rows = jnp.where(
        core == 0,
        jnp.concatenate([part, traded], axis=0),
        jnp.concatenate([traded, part], axis=0),
    )
    weight_all = both_sides(jnp.concatenate(projections, axis=1), other_rows, 0)
    gain_one = both_sides(attention_gain, gain_other, 0).astype(f32)
    gain_two = both_sides(feed_gain, feed_other, 0).astype(f32)
    table = both_sides(bias_table, table_other, 0)

    mine = tokens[0]
    cot = cotangent[0]
    out_rows = inner // 2
    out_part = swap_x(after(my_rows(output_weight, core, out_rows), part))
    out_traded = swap_core(out_part)
    output_full = both_sides(
        output_weight,
        jnp.where(
            core == 0,
            jnp.concatenate([out_part, out_traded], axis=0),
            jnp.concatenate([out_traded, out_part], axis=0),
        ),
        1,
    )
    rows_own = jnp.concatenate([mine, cot], axis=0)
    rows_side = swap_x(after(rows_own, part))
    rows_core = swap_core(jnp.concatenate([rows_own, rows_side], axis=0))

    def group_of(which):
        at = which * length
        return jnp.concatenate(
            [
                rows_own[at : at + length],
                rows_core[at : at + length],
                rows_side[at : at + length],
                rows_core[2 * length + at : 3 * length + at],
            ],
            axis=0,
        )

    positions = here * length + jnp.arange(length, dtype=jnp.int32)
    pair_positions = (here ^ 1) * length + jnp.arange(length, dtype=jnp.int32)
    live_group = jnp.concatenate(
        [
            (positions < live_count).astype(f32)[:, None],
            (pair_positions < live_count).astype(f32)[:, None],
            (positions < count_other).astype(f32)[:, None],
            (pair_positions < count_other).astype(f32)[:, None],
        ],
        axis=0,
    )
    live_own = live_group[:length]

    inputs = mine.astype(f32)
    scale_one = row_scale(inputs)
    first = (inputs * scale_one * gain_one).astype(bf16)
    projected = jnp.dot(first, weight_all, preferred_element_type=f32).astype(bf16)
    joined, query = projected[:, : 2 * inner], projected[:, 2 * inner :]

    bucket_count = table.shape[0]
    reach = (buckets.shape[0] + 1) // 2
    offsets = jnp.clip(jnp.arange(SPAN_ROW, dtype=jnp.int32) - 511, 1 - reach, reach - 1) + (reach - 1)
    spots = jnp.arange(buckets.shape[0], dtype=jnp.int32)
    chosen = jnp.sum(jnp.where(offsets[:, None] == spots[None, :], buckets[None, :], 0), axis=1)
    onehot = (chosen[:, None] == jnp.arange(bucket_count, dtype=jnp.int32)[None, :]).astype(f32)
    offset_rows = lax.dot_general(
        table.astype(f32), onehot, (((0,), (1,)), ((), ())), precision=HIGH, preferred_element_type=f32
    )
    tiles, turned = bias_tiles(offset_rows)
    far = jnp.concatenate([offset_rows[:, 0], offset_rows[:, SPAN_ROW - 2]])

    middle = chips // 2

    def start_ring(block):
        return jnp.concatenate([block, swap_core(block)], axis=0)

    def next_chunk(chunk, step):
        if step == middle:
            return spread(chunk[:length], route_ring)
        return spread(chunk, route_ring)

    def views(chunk):
        return [(chunk, row) for row in range(chunk.shape[0] // length)]

    def blocks_at(step):
        ahead = chip_at(my_place + toward * step)
        if step == middle:
            return [ahead * 2 + core, ahead * 2 + 1 - core]
        behind = chip_at(my_place - toward * step)
        return [ahead * 2 + core, ahead * 2 + 1 - core, behind * 2 + 1 - core, behind * 2 + core]

    def info_of(blocks, near):
        entries = [here]
        for block in blocks:
            limit = live_count
            if near:
                limit = jnp.where(jnp.logical_or(block != next_block, has_next), limit, nowhere)
            else:
                limit = jnp.where(block == next_block, nowhere, limit)
            entries += [block, limit]
        return jnp.stack(entries).astype(jnp.int32)

    near_info = info_of([here, here ^ 1, next_block], True)
    far_info = [info_of(blocks_at(step), False) for step in range(1, middle + 1)]

    chunk = start_ring(joined)
    next_joined = spread(joined, route_next)
    near_views = views(chunk) + [(next_joined, 0)]
    received = next_chunk(chunk, 1)
    state = forward_call(near_info, far, query, near_views, tiles, None, False)
    query_first = query_chunk = start_ring(query)
    query_next = spread(query, route_next)
    far_views, query_views = [], []
    for step in range(1, middle + 1):
        partner = swap_core(received)
        now = views(received) + views(partner)
        far_views.append(now)
        query_received = next_chunk(query_chunk, step)
        query_partner = swap_core(query_received)
        query_views.append(views(query_received) + views(query_partner))
        query_chunk = query_received
        if step < middle:
            received = next_chunk(received, step + 1)
        state = forward_call(far_info[step - 1], far, query, now, None, state, step == middle)
    attention, attention_low, aux = state

    hidden_units = gate_weight.shape[1] // 2
    gate_mine = lax.dynamic_slice_in_dim(gate_weight, core * hidden_units, hidden_units, 1)
    up_mine = lax.dynamic_slice_in_dim(up_weight, core * hidden_units, hidden_units, 1)
    down_mine = lax.dynamic_slice_in_dim(down_weight, core * hidden_units, hidden_units, 0)
    outer_low = (group_of(1).astype(f32) * live_group).astype(bf16)
    mixed_side = swap_x(attention_low)
    mixed_core = swap_core(jnp.concatenate([attention_low, mixed_side], axis=0))
    mixed = jnp.concatenate(
        [attention_low, mixed_core[:length], mixed_side, mixed_core[length:]], axis=0
    )
    branch = jnp.dot(mixed, output_full, preferred_element_type=f32)
    middle_rows = group_of(0).astype(f32) + live_group * branch
    scale_two = row_scale(middle_rows)
    unit = middle_rows * scale_two
    second = (unit * gain_two).astype(bf16)
    gate = jnp.dot(second, gate_mine, preferred_element_type=f32)
    up = jnp.dot(second, up_mine, preferred_element_type=f32)

    def gated(gate_in, up_in):
        return jax.nn.gelu(gate_in, approximate=True) * up_in

    def add_low(left, right):
        return (left.astype(f32) + right.astype(f32)).astype(bf16)

    def halves(block, bit):
        size = block.shape[0] // 2
        return (my_rows(block, bit, size), my_rows(block, 1 - bit, size))

    outer_chips = [0, rows_of_chips - 1]
    route_inward = route_of(
        lambda z, y, k, x: ((1 if z == 0 else 2), y, k, x) if z in outer_chips else None
    )
    route_across = route_of(lambda z, y, k, x: (3 - z, y, k, x) if z in (1, 2) else None)
    route_third = route_of(lambda z, y, k, x: (z ^ 1, y, k, x) if z % 2 != k else None)
    route_fourth = route_of(lambda z, y, k, x: (z, y, 1 - k, x) if z % 2 == k else None)
    z_low = lane_z % 2
    upper = lane_z // 2

    def reduce_y(block):
        kept, sent = halves(block, lane_y)
        return add_low(kept, spread(sent, route_y))

    def reduce_x(block):
        grid = block.reshape(2, 2, block.shape[0] // 4, block.shape[1])
        kept = lax.dynamic_index_in_dim(grid, side, 1, keepdims=False)
        sent = lax.dynamic_index_in_dim(grid, 1 - side, 1, keepdims=False)
        got = swap_x(sent)
        return jnp.where(side == upper, kept, got), jnp.where(side == upper, got, kept)

    def reduce_z(pair):
        stays, leaves = pair
        leaves = add_low(leaves, spread(leaves, route_inward))
        stays = add_low(stays, spread(leaves, route_across))
        return add_low(stays, spread(stays, route_third))

    def reduce_last(block):
        kept = lax.dynamic_index_in_dim(block, core, 0, keepdims=False)
        sent = lax.dynamic_index_in_dim(block, 1 - core, 0, keepdims=False)
        return jnp.where(z_low == core, kept, spread(sent, route_fourth)).astype(f32)

    hidden_value, gate_pull = jax.vjp(gated, gate, up)
    hidden = hidden_value.astype(bf16)
    down_full = jnp.einsum("tf,td->fd", hidden, outer_low, preferred_element_type=f32).astype(bf16)
    down_y = reduce_y(down_full)
    outer_next = after(outer_low, down_full)
    hidden_grad = jnp.einsum("td,fd->tf", outer_next, down_mine, preferred_element_type=f32)
    gate_back, up_back = gate_pull(hidden_grad)
    gate_low = gate_back.astype(bf16)
    up_low = up_back.astype(bf16)
    gate_full = jnp.einsum("tf,td->fd", gate_low, second, preferred_element_type=f32).astype(bf16)
    gate_y = reduce_y(gate_full)
    up_next = after(up_low, gate_full)
    second_grad = jnp.einsum("tf,df->td", gate_low, gate_mine, preferred_element_type=f32) + jnp.einsum(
        "tf,df->td", up_next, up_mine, preferred_element_type=f32
    )
    feed_gain_part = jnp.sum(second_grad * unit, axis=0)
    scaled = second_grad * gain_two
    middle_part = (
        live_group * scale_two * (scaled - unit * jnp.mean(scaled * unit, axis=-1, keepdims=True))
    ).astype(bf16)
    grad_part = jnp.einsum("td,id->ti", middle_part, output_full, preferred_element_type=f32)
    outer_own = outer_low[:length]
    grad_own = jnp.einsum("td,id->ti", outer_own, output_full, preferred_element_type=f32)

    def sum_core(block):
        grid = block.reshape(4, length, block.shape[-1])
        sent = swap_core(jnp.stack([grid[1], grid[3]]).astype(bf16)).astype(f32)
        return grid[0] + sent[0], grid[2] + sent[1]

    grad_kept, grad_passed = sum_core(grad_part)
    grad_got = swap_x(grad_passed.astype(bf16))
    grads = finish_grads(grad_kept, grad_got, grad_own, attention, aux)

    grad_chunk = start_ring(grads)
    grad_next = spread(grads, route_next)
    received = next_chunk(grad_chunk, 1)
    query_state, diagonals = query_call(near_info, far, query, grads, near_views, tiles, None, False)
    grad_views = []
    for step in range(1, middle + 1):
        received = after(received, query_state)
        partner = swap_core(received)
        grad_views.append(views(received) + views(partner))
        following = next_chunk(received, step + 1) if step < middle else None
        outs = query_call(
            far_info[step - 1], far, query, grads, far_views[step - 1], None, query_state, step == middle
        )
        query_state = outs[0]
        received = following
    query_low, far_sums = outs

    up_full = jnp.einsum(
        "tf,td->fd", after(up_low, grads), second, preferred_element_type=f32
    ).astype(bf16)
    up_y = reduce_y(after(up_full, grad_views[-1][0][0]))
    down_x = reduce_x(after(down_y, grads))
    gate_x = reduce_x(after(gate_y, grads))
    feed_part = jnp.dot(after(hidden, grads), down_mine, preferred_element_type=f32)
    both_parts = jnp.concatenate([feed_part.astype(bf16), middle_part], axis=1)
    both_kept, both_passed = sum_core(both_parts)
    both_sum = both_kept + swap_x(both_passed.astype(bf16)).astype(f32)
    width = tokens.shape[2]
    result = (middle_rows[:length] + live_own * both_sum[:, :width]).astype(bf16)
    middle_grad = outer_own.astype(f32) + both_sum[:, width:]
    branch_low = (live_own * middle_grad).astype(bf16)

    key_state = key_call(
        near_info,
        far,
        joined,
        views(query_first) + [(query_next, 0)],
        views(grad_chunk) + [(grad_next, 0)],
        turned,
        None,
        False,
    )
    for step in range(1, middle + 1):
        key_state = key_call(
            far_info[step - 1],
            far,
            joined,
            query_views[step - 1],
            grad_views[step - 1],
            None,
            key_state,
            step == middle,
        )
    keys_low, values_low = key_state

    down_out = reduce_last(reduce_z(after(down_x, grad_views[-1][0][0])))
    gate_out = jnp.transpose(reduce_last(reduce_z(after(gate_x, grad_views[-1][0][0]))))
    up_out = jnp.transpose(reduce_last(reduce_z(reduce_x(up_y))))

    columns = inner // places
    target = jnp.arange(inner // 2, dtype=jnp.int32)
    group_index, inside = target // columns, target % columns
    y_bit = group_index // rows_of_chips
    z_index = group_index % rows_of_chips

    def picker(which):
        source = (((z_index * 2 + y_bit) * 2) + which) * columns + inside
        return (jnp.arange(inner, dtype=jnp.int32)[:, None] == source[None, :]).astype(bf16)

    pick_kept, pick_sent = picker(core), picker(1 - core)

    def pick(block, chooser):
        return jnp.dot(block, chooser, preferred_element_type=f32).astype(bf16)

    def lanes_of(block):
        low_half, high_half = block[:, :half], block[:, half:]
        return (
            jnp.where(side == 0, low_half, high_half),
            jnp.where(side == 0, high_half, low_half),
        )

    def outer_product(left, right):
        return jnp.einsum("ti,td->id", left, right, preferred_element_type=f32)

    first_lanes = lanes_of(first)
    branch_lanes = lanes_of(branch_low)
    kept_x, kept_y, sent_x, sent_y = [], [], [], []
    for block, (lane_kept, lane_sent) in (
        (query_low, first_lanes),
        (keys_low, first_lanes),
        (values_low, first_lanes),
        (attention_low, branch_lanes),
    ):
        mine_rows, other_rows_of = pick(block, pick_kept), pick(block, pick_sent)
        kept_x.append(outer_product(mine_rows, lane_kept))
        kept_y.append(outer_product(mine_rows, lane_sent))
        sent_x.append(outer_product(other_rows_of, lane_kept).astype(bf16))
        sent_y.append(outer_product(other_rows_of, lane_sent).astype(bf16))
    got = swap_core(jnp.stack(sent_x + sent_y)).astype(f32)
    passed = (jnp.stack(kept_y) + got[4:]).astype(bf16)
    total = (jnp.stack(kept_x) + got[:4] + swap_x(passed).astype(f32)).astype(bf16)
    for bit, route in ((lane_y, route_y), (upper, route_far), (z_low, route_near)):
        size = total.shape[1] // 2
        kept = lax.dynamic_slice_in_dim(total, bit * size, size, 1)
        sent = lax.dynamic_slice_in_dim(total, (1 - bit) * size, size, 1)
        total = add_low(kept, spread(sent, route))
    total = total.astype(f32)
    projection_out = jnp.transpose(total[:3], (0, 2, 1))

    gradients = jnp.concatenate([keys_low, values_low, query_low], axis=1)
    first_grad = jnp.einsum("ti,di->td", gradients, weight_all, preferred_element_type=f32)
    unit_one = inputs * scale_one
    gain_one_part = jnp.sum(first_grad * unit_one, axis=0)
    scaled_one = first_grad * gain_one
    input_gradient = (
        middle_grad
        + scale_one * (scaled_one - unit_one * jnp.mean(scaled_one * unit_one, axis=-1, keepdims=True))
    ).astype(bf16)

    lines = diagonals[:, :2].reshape(heads, SPAN_ROW)
    outside = far_sums[:, 0].reshape(heads // 2, PAIR)[:, :8].reshape(heads, 4)
    lines = lines.at[:, 0].add(outside[:, BEFORE]).at[:, SPAN_ROW - 2].add(outside[:, AFTER])
    table_part = lax.dot_general(
        onehot, lines, (((0,), (1,)), ((), ())), precision=HIGH, preferred_element_type=f32
    )
    flat = jnp.concatenate([gain_one_part, feed_gain_part, table_part.reshape(-1)])
    used = flat.shape[0]
    flat = jnp.pad(flat, (0, -used % 1024)).reshape(-1, 128)
    for route in (route_core, route_x, route_y, route_far, route_near):
        flat = flat + spread(flat, route)
    flat = flat.reshape(-1)
    gain_one_sum = flat[:width]
    feed_gain_sum = flat[width : 2 * width]
    table_sum = flat[2 * width : used].reshape(bucket_count, heads)

    def my_half(block):
        size = block.shape[0] // 2
        return lax.dynamic_slice_in_dim(block, side * size, size, 0)

    return (
        result[None],
        input_gradient[None],
        my_half(gain_one_sum),
        projection_out[0],
        projection_out[1],
        projection_out[2],
        total[3],
        my_half(table_sum),
        my_half(feed_gain_sum),
        gate_out,
        up_out,
        down_out,
    )


def solution(mesh):
    placed = (
        P("wsh", "ctx", None),
        P("wsh", None),
        P(),
        P("wsh"),
        P("wsh", None),
        P("wsh", None),
        P("wsh", None),
        P(None, "wsh"),
        P("wsh", None),
        P("wsh"),
        P(None, "wsh"),
        P(None, "wsh"),
        P("wsh", None),
        P("wsh", "ctx", None),
    )
    step = grouped_body if mesh.shape["ctx"] == 16 else body
    return jax.shard_map(
        step,
        mesh=mesh,
        in_specs=placed,
        out_specs=(
            P("wsh", "ctx", None),
            P("wsh", "ctx", None),
            P("wsh"),
            P("wsh", "ctx"),
            P("wsh", "ctx"),
            P("wsh", "ctx"),
            P("ctx", "wsh"),
            P("wsh", None),
            P("wsh"),
            P(None, ("ctx", "wsh")),
            P(None, ("ctx", "wsh")),
            P(("ctx", "wsh"), None),
        ),
        check_vma=False,
    )
```

```python
import functools

import jax
import jax.numpy as jnp
from jax import lax
from jax.experimental import pallas as pl
from jax.experimental.layout import Layout, with_layout_constraint
from jax.experimental.pallas import tpu as pltpu
from jax.sharding import PartitionSpec as P

EPSILON = 1e-06
MASKED = -1e30
HIGH = lax.Precision.HIGHEST


def shifted(block, axis, distance):
    devices = range(lax.axis_size(axis))
    route = [((i - distance) % len(devices), i) for i in devices]
    return lax.ppermute(block, axis, route)


def row_scale(values):
    return lax.rsqrt(jnp.mean(values * values, axis=-1, keepdims=True) + EPSILON)


def normalize(values, gain):
    return values * row_scale(values) * gain


def skew_expand(offset_bias, length):
    count = offset_bias.shape[0]
    padded = jnp.pad(offset_bias, ((0, 0), (0, 1)))
    tiled = jnp.tile(padded, (1, length))[:, : length * (2 * length - 1)]
    return tiled.reshape(count, length, 2 * length - 1)[:, :, length - 1 :]


def diagonal_sums(grid, length):
    count = grid.shape[0]
    wide = jnp.pad(grid, ((0, 0), (0, 0), (length - 1, 0))).reshape(
        count, length * (2 * length - 1)
    )
    wide = jnp.pad(wide, ((0, 0), (0, length)))
    return jnp.sum(wide.reshape(count, length, 2 * length), axis=1)[:, : 2 * length - 1]


def bucket_onehot(offset_start, length, buckets, bucket_count):
    reach = (buckets.shape[0] + 1) // 2
    offsets = offset_start + jnp.arange(2 * length - 1, dtype=jnp.int32) - (length - 1)
    spots = jnp.clip(offsets, 1 - reach, reach - 1) + (reach - 1)
    table_spots = jnp.arange(buckets.shape[0], dtype=jnp.int32)
    chosen = jnp.sum(jnp.where(spots[:, None] == table_spots[None, :], buckets[None, :], 0), axis=1)
    return chosen[:, None] == jnp.arange(bucket_count, dtype=jnp.int32)[None, :]


def block_scores(query3, keys3, table, onehot, key_live, length):
    scores = jnp.einsum("ihd,jhd->hij", query3, keys3, preferred_element_type=jnp.float32)
    offset_bias = jnp.einsum(
        "ob,bh->ho", onehot.astype(jnp.bfloat16), table, preferred_element_type=jnp.float32
    )
    scores = scores + skew_expand(offset_bias, length)
    return jnp.where(key_live[None, None, :], scores, MASKED)


def body(
    tokens,
    lengths,
    buckets,
    attention_gain,
    query_weight,
    key_weight,
    value_weight,
    output_weight,
    bias_table,
    feed_gain,
    gate_weight,
    up_weight,
    down_weight,
    cotangent,
):
    (
        gain_first,
        query_full,
        key_full,
        value_full,
        output_full,
        table_full,
        gain_second,
        gate_full,
        up_full,
        down_full,
    ) = (
        lax.all_gather(attention_gain, "wsh", axis=0, tiled=True),
        lax.all_gather(query_weight, "wsh", axis=0, tiled=True),
        lax.all_gather(key_weight, "wsh", axis=0, tiled=True),
        lax.all_gather(value_weight, "wsh", axis=0, tiled=True),
        lax.all_gather(output_weight, "wsh", axis=1, tiled=True),
        lax.all_gather(bias_table, "wsh", axis=0, tiled=True),
        lax.all_gather(feed_gain, "wsh", axis=0, tiled=True),
        lax.all_gather(gate_weight, "wsh", axis=1, tiled=True),
        lax.all_gather(up_weight, "wsh", axis=1, tiled=True),
        lax.all_gather(down_weight, "wsh", axis=0, tiled=True),
    )
    length = tokens.shape[1]
    heads = table_full.shape[1]
    bucket_count = table_full.shape[0]
    inner = query_full.shape[1]
    head_size = inner // heads
    seq_count = lengths.shape[1]
    wide_count = lax.axis_size("ctx")
    span = wide_count // seq_count
    here = lax.axis_index("ctx")
    my_seq = here % seq_count
    my_block = here // seq_count
    seq_pick = jnp.arange(seq_count, dtype=jnp.int32) == my_seq
    my_length = jnp.sum(jnp.where(seq_pick, lengths[0], 0))
    positions = jnp.arange(length, dtype=jnp.int32)
    live = (my_block * length + positions < my_length).astype(jnp.float32)[:, None]
    inputs = tokens[0].astype(jnp.float32)
    gain_one = gain_first.astype(jnp.float32)
    first = normalize(inputs, gain_one).astype(jnp.bfloat16)
    query = jnp.dot(first, query_full, preferred_element_type=jnp.float32).astype(jnp.bfloat16)
    keys = jnp.dot(first, key_full, preferred_element_type=jnp.float32).astype(jnp.bfloat16)
    values = jnp.dot(first, value_full, preferred_element_type=jnp.float32).astype(jnp.bfloat16)
    query3 = query.reshape(length, heads, head_size)

    def forward_step(carry, block_keys, block_values, key_block):
        run_max, run_total, running = carry
        onehot = bucket_onehot((key_block - my_block) * length, length, buckets, bucket_count)
        key_live = key_block * length + positions < my_length
        scores = block_scores(
            query3,
            block_keys.reshape(length, heads, head_size),
            table_full,
            onehot,
            key_live,
            length,
        )
        new_max = jnp.maximum(run_max, jnp.max(scores, axis=2))
        weights = jnp.exp(scores - new_max[:, :, None])
        factor = jnp.exp(run_max - new_max)
        run_total = run_total * factor + jnp.sum(weights, axis=2)
        update = jnp.einsum(
            "hij,jhd->ihd",
            weights.astype(jnp.bfloat16),
            block_values.reshape(length, heads, head_size),
            preferred_element_type=jnp.float32,
        )
        running = running * jnp.transpose(factor)[:, :, None] + update
        return (new_max, run_total, running)

    start_carry = (
        jnp.full((heads, length), MASKED, jnp.float32),
        jnp.zeros((heads, length), jnp.float32),
        jnp.zeros((length, heads, head_size), jnp.float32),
    )
    start_carry = forward_step(start_carry, keys, values, my_block)
    stored = ()

    def cycle_turn(turn, state):
        carry, block_keys, block_values, stored_blocks = state
        block_keys, block_values = shifted((block_keys, block_values), "ctx", seq_count)
        carry = forward_step(carry, block_keys, block_values, (my_block - turn) % span)
        return (carry, block_keys, block_values, stored_blocks)

    (run_max, run_total, running), _, _, stored = lax.fori_loop(
        1, span, cycle_turn, (start_carry, keys, values, stored)
    )
    log_total = run_max + jnp.log(run_total)
    attention = (running / jnp.transpose(run_total)[:, :, None]).reshape(length, inner)
    attention_low = attention.astype(jnp.bfloat16)
    branch = jnp.dot(attention_low, output_full, preferred_element_type=jnp.float32)
    middle = inputs + live * branch
    gain_two = gain_second.astype(jnp.float32)
    second = normalize(middle, gain_two).astype(jnp.bfloat16)
    gate = jnp.dot(second, gate_full, preferred_element_type=jnp.float32)
    up = jnp.dot(second, up_full, preferred_element_type=jnp.float32)
    hidden = (jax.nn.gelu(gate, approximate=True) * up).astype(jnp.bfloat16)
    feed = jnp.dot(hidden, down_full, preferred_element_type=jnp.float32)
    result = (middle + live * feed).astype(jnp.bfloat16)
    outer = live * cotangent[0].astype(jnp.float32)
    outer_low = outer.astype(jnp.bfloat16)
    down_grad = jnp.einsum("tf,td->fd", hidden, outer_low, preferred_element_type=jnp.float32)
    hidden_grad = jnp.einsum("td,fd->tf", outer_low, down_full, preferred_element_type=jnp.float32)

    def gated(gate_in, up_in):
        return jax.nn.gelu(gate_in, approximate=True) * up_in

    _, gate_pull = jax.vjp(gated, gate, up)
    gate_back, up_back = gate_pull(hidden_grad)
    gate_low = gate_back.astype(jnp.bfloat16)
    up_low = up_back.astype(jnp.bfloat16)
    gate_grad = jnp.einsum("td,tf->df", second, gate_low, preferred_element_type=jnp.float32)
    up_grad = jnp.einsum("td,tf->df", second, up_low, preferred_element_type=jnp.float32)
    second_grad = jnp.einsum(
        "tf,df->td", gate_low, gate_full, preferred_element_type=jnp.float32
    ) + jnp.einsum("tf,df->td", up_low, up_full, preferred_element_type=jnp.float32)
    _, norm_pull = jax.vjp(normalize, middle, gain_two)
    middle_back, gain_two_grad = norm_pull(second_grad)
    middle_grad = outer + middle_back
    branch_low = (live * middle_grad).astype(jnp.bfloat16)
    output_grad = jnp.einsum(
        "ti,td->id", attention_low, branch_low, preferred_element_type=jnp.float32
    )
    attention_grad = jnp.einsum(
        "td,id->ti", branch_low, output_full, preferred_element_type=jnp.float32
    ).astype(jnp.bfloat16)
    attention_grad3 = attention_grad.reshape(length, heads, head_size)
    delta = jnp.transpose(
        jnp.sum(
            (attention_grad.astype(jnp.float32) * attention).reshape(length, heads, head_size),
            axis=2,
        )
    )

    def backward_step(block_keys, block_values, key_block):
        keys3 = block_keys.reshape(length, heads, head_size)
        values3 = block_values.reshape(length, heads, head_size)
        onehot = bucket_onehot((key_block - my_block) * length, length, buckets, bucket_count)
        key_live = key_block * length + positions < my_length
        scores = block_scores(query3, keys3, table_full, onehot, key_live, length)
        probs = jnp.exp(scores - log_total[:, :, None])
        prob_grad = jnp.einsum(
            "ihd,jhd->hij", attention_grad3, values3, preferred_element_type=jnp.float32
        )
        score_grad = (probs * (prob_grad - delta[:, :, None])).astype(jnp.bfloat16)
        part_query = jnp.einsum(
            "hij,jhd->ihd", score_grad, keys3, preferred_element_type=jnp.float32
        )
        part_keys = jnp.einsum(
            "hij,ihd->jhd", score_grad, query3, preferred_element_type=jnp.float32
        )
        part_values = jnp.einsum(
            "hij,ihd->jhd",
            probs.astype(jnp.bfloat16),
            attention_grad3,
            preferred_element_type=jnp.float32,
        )
        part_table = jnp.einsum(
            "ho,ob->bh",
            diagonal_sums(score_grad.astype(jnp.float32), length),
            onehot.astype(jnp.float32),
            precision=HIGH,
        )
        return (
            part_query.reshape(length, inner),
            part_keys.reshape(length, inner),
            part_values.reshape(length, inner),
            part_table,
        )

    def back_turn(turn, state):
        block_keys, block_values, keys_sum, values_sum, query_sum, table_sum = state
        part_query, part_keys, part_values, part_table = backward_step(
            block_keys, block_values, (my_block - turn) % span
        )
        keys_next = keys_sum + part_keys
        values_next = values_sum + part_values
        keys_sum, values_sum = (
            shifted(keys_next.astype(jnp.bfloat16), "ctx", seq_count).astype(keys_next.dtype),
            shifted(values_next.astype(jnp.bfloat16), "ctx", seq_count).astype(values_next.dtype),
        )
        block_keys, block_values = shifted((block_keys, block_values), "ctx", seq_count)
        return (
            block_keys,
            block_values,
            keys_sum,
            values_sum,
            query_sum + part_query,
            table_sum + part_table,
        )

    zeros_rows = jnp.zeros((length, inner), jnp.float32)
    back_state = (
        keys,
        values,
        zeros_rows,
        zeros_rows,
        zeros_rows,
        jnp.zeros((bucket_count, heads), jnp.float32),
    )
    _, _, keys_sum, values_sum, query_sum, table_grad = lax.fori_loop(
        0, span, back_turn, back_state
    )
    query_low = query_sum.astype(jnp.bfloat16)
    keys_low = keys_sum.astype(jnp.bfloat16)
    values_low = values_sum.astype(jnp.bfloat16)
    query_grad = jnp.einsum("td,ti->di", first, query_low, preferred_element_type=jnp.float32)
    key_grad = jnp.einsum("td,ti->di", first, keys_low, preferred_element_type=jnp.float32)
    value_grad = jnp.einsum("td,ti->di", first, values_low, preferred_element_type=jnp.float32)
    first_grad = (
        jnp.einsum("ti,di->td", query_low, query_full, preferred_element_type=jnp.float32)
        + jnp.einsum("ti,di->td", keys_low, key_full, preferred_element_type=jnp.float32)
        + jnp.einsum("ti,di->td", values_low, value_full, preferred_element_type=jnp.float32)
    )
    _, first_pull = jax.vjp(normalize, inputs, gain_one)
    inputs_back, gain_one_grad = first_pull(first_grad)
    input_gradient = (middle_grad + inputs_back).astype(jnp.bfloat16)
    small = lax.psum((gain_one_grad, table_grad, gain_two_grad), "ctx")
    wide = (
        lax.psum_scatter(query_grad, "ctx", scatter_dimension=1, tiled=True),
        lax.psum_scatter(key_grad, "ctx", scatter_dimension=1, tiled=True),
        lax.psum_scatter(value_grad, "ctx", scatter_dimension=1, tiled=True),
        lax.psum_scatter(output_grad, "ctx", scatter_dimension=0, tiled=True),
        lax.psum_scatter(gate_grad, "ctx", scatter_dimension=1, tiled=True),
        lax.psum_scatter(up_grad, "ctx", scatter_dimension=1, tiled=True),
        lax.psum_scatter(down_grad, "ctx", scatter_dimension=0, tiled=True),
    )
    final = (
        lax.psum_scatter(
            small[0].astype(jnp.bfloat16), "wsh", scatter_dimension=0, tiled=True
        ).astype(jnp.float32),
        lax.psum_scatter(
            small[1].astype(jnp.bfloat16), "wsh", scatter_dimension=0, tiled=True
        ).astype(jnp.float32),
        lax.psum_scatter(
            small[2].astype(jnp.bfloat16), "wsh", scatter_dimension=0, tiled=True
        ).astype(jnp.float32),
        lax.psum_scatter(
            wide[0].astype(jnp.bfloat16), "wsh", scatter_dimension=0, tiled=True
        ).astype(jnp.float32),
        lax.psum_scatter(
            wide[1].astype(jnp.bfloat16), "wsh", scatter_dimension=0, tiled=True
        ).astype(jnp.float32),
        lax.psum_scatter(
            wide[2].astype(jnp.bfloat16), "wsh", scatter_dimension=0, tiled=True
        ).astype(jnp.float32),
        lax.psum_scatter(
            wide[3].astype(jnp.bfloat16), "wsh", scatter_dimension=1, tiled=True
        ).astype(jnp.float32),
        lax.psum_scatter(
            wide[4].astype(jnp.bfloat16), "wsh", scatter_dimension=1, tiled=True
        ).astype(jnp.float32),
        lax.psum_scatter(
            wide[5].astype(jnp.bfloat16), "wsh", scatter_dimension=1, tiled=True
        ).astype(jnp.float32),
        lax.psum_scatter(
            wide[6].astype(jnp.bfloat16), "wsh", scatter_dimension=0, tiled=True
        ).astype(jnp.float32),
    )
    gain_one_out, table_out, gain_two_out = (final[0], final[1], final[2])
    query_out, key_out, value_out, output_out = (final[3], final[4], final[5], final[6])
    gate_out, up_out, down_out = (final[7], final[8], final[9])
    return (
        result[None],
        input_gradient[None],
        gain_one_out,
        query_out,
        key_out,
        value_out,
        output_out,
        table_out,
        gain_two_out,
        gate_out,
        up_out,
        down_out,
    )


BLOCK = 256
PAIR = 128
SPAN_ROW = 1024
CONTRACT_LAST = (((1,), (1,)), ((), ()))
AXES = ("ctx", "wsh")
GELU_SCALE = 0.7978845608028654
GELU_CUBE = 0.044715
LEFT_LANE, RIGHT_LANE, DEAD_LANE = 125, 126, 127
NEAR, BEFORE, AFTER = 0, 1, 2


SHARE = 0.01


def estimate(flops, bytes_accessed, transcendentals):
    return pl.CostEstimate(
        flops=int(flops * SHARE),
        bytes_accessed=int(bytes_accessed * SHARE),
        transcendentals=int(transcendentals * SHARE),
    )


def lanes(rows=BLOCK):
    return lax.broadcasted_iota(jnp.int32, (rows, PAIR), 1)


def only_head(block, second):
    lane = lanes(block.shape[0])
    keep = lane >= PAIR // 2 if second else lane < PAIR // 2
    return jnp.where(keep, block, jnp.zeros_like(block))


def pair_select(first, second):
    return jnp.where(lanes(first.shape[0]) < PAIR // 2, first, second)


def contract_last(left, right):
    return lax.dot_general(left, right, CONTRACT_LAST, preferred_element_type=jnp.float32)


def stack_heads(block):
    return jnp.concatenate([only_head(block, False), only_head(block, True)], axis=0)


def dead_rows(start, limit):
    row = lax.broadcasted_iota(jnp.int32, (BLOCK, PAIR), 0)
    return start + row >= limit


def other_aux(start, limit, kind):
    lane = lanes()
    value = jnp.where(jnp.logical_and(lane < 48, lane % 8 < 6), 1.0, 0.0)
    value = jnp.where(jnp.logical_and(lane == LEFT_LANE, kind == BEFORE), 1.0, value)
    value = jnp.where(jnp.logical_and(lane == RIGHT_LANE, kind == AFTER), 1.0, value)
    value = jnp.where(jnp.logical_and(lane == DEAD_LANE, dead_rows(start, limit)), MASKED, value)
    return value.astype(jnp.bfloat16)


def own_lanes(far_ref, head, heads):
    lane = lanes()
    value = jnp.where(lane == DEAD_LANE, 1.0, 0.0)
    value = jnp.where(lane == LEFT_LANE, far_ref[head], value)
    return jnp.where(lane == RIGHT_LANE, far_ref[heads + head], value)


def parts_of(value):
    first = value.astype(jnp.bfloat16).astype(jnp.float32)
    second = (value - first).astype(jnp.bfloat16).astype(jnp.float32)
    return first, second, value - first - second


def place_parts(base, value, lane_start):
    lane = lanes()
    for spot, part in enumerate(parts_of(value)):
        base = jnp.where(lane == lane_start + spot, part, base)
    return base


def kind_of(block, own):
    return jnp.where(block < own, BEFORE, AFTER)


def tiles_kernel(row_ref, tile_ref, turned_ref):
    row = row_ref[0]
    wide = pltpu.roll(
        jnp.broadcast_to(row, (BLOCK, SPAN_ROW)), SPAN_ROW - 255, 1, stride=1, stride_axis=0
    )
    for spot in range(3):
        tile = wide[:, spot * BLOCK : (spot + 1) * BLOCK]
        tile_ref[0, spot] = tile.astype(jnp.bfloat16)
        turned_ref[0, spot] = jnp.transpose(tile).astype(jnp.bfloat16)


def bias_tiles(offset_rows):
    heads = offset_rows.shape[0]
    shape = jax.ShapeDtypeStruct((heads, 3, BLOCK, BLOCK), jnp.bfloat16)
    spec = pl.BlockSpec((1, 3, BLOCK, BLOCK), lambda h: (h, 0, 0, 0))
    return pl.pallas_call(
        tiles_kernel,
        grid=(heads,),
        out_shape=(shape, shape),
        in_specs=[pl.BlockSpec((1, 1, SPAN_ROW), lambda h: (h, 0, 0))],
        out_specs=(spec, spec),
        name="bias_tiles",
    )(offset_rows[:, None, :])


def view_spec(row, lane_block):
    return pl.BlockSpec((BLOCK, PAIR), lambda p, i, f: (row, lane_block(p)))


def tile_spec():
    return pl.BlockSpec((2, 3, BLOCK, BLOCK), lambda p, i, f: (p, 0, 0, 0))


def run_pairs(kernel, info, far, operands, in_specs, out_shape, out_specs, work, name):
    pairs = 3
    return pl.pallas_call(
        kernel,
        grid_spec=pltpu.PrefetchScalarGridSpec(
            num_scalar_prefetch=2, grid=(pairs,), in_specs=in_specs, out_specs=out_specs
        ),
        out_shape=out_shape,
        cost_estimate=estimate(
            flops=2 * pairs * work * BLOCK * BLOCK * BLOCK,
            bytes_accessed=pairs * work * BLOCK * PAIR * 2,
            transcendentals=pairs * work * BLOCK * BLOCK,
        ),
        name=name,
    )(info, far, *operands)


def forward_kernel(at, nears, first, last, heads, info_ref, far_ref, *refs):
    refs = list(refs)
    count = len(nears)
    query_ref = refs.pop(0)
    key_refs, refs = refs[:count], refs[count:]
    value_refs, refs = refs[:count], refs[count:]
    tile_ref = refs.pop(0) if any(nears) else None
    pair = pl.program_id(0)
    own = info_ref[0]
    query = query_ref[...]
    if first:
        old_max = jnp.full((BLOCK, PAIR), MASKED, jnp.float32)
        total = None
    else:
        max_ref, total_ref = refs.pop(0), refs.pop(0)
        old_max, total = max_ref[...], total_ref[...]
    keys = []
    for spot in range(count):
        block, limit = info_ref[at + 2 * spot], info_ref[at + 1 + 2 * spot]
        kind = NEAR if nears[spot] else kind_of(block, own)
        keys.append(
            jnp.concatenate([key_refs[spot][...], other_aux(block * BLOCK, limit, kind)], axis=1)
        )
    tops, weights = [], []
    for head in range(2):
        aux = own_lanes(far_ref, 2 * pair + head, heads).astype(jnp.bfloat16)
        left = jnp.concatenate([only_head(query, head == 1), aux], axis=1)
        scores = []
        for spot in range(count):
            score = contract_last(left, keys[spot])
            if nears[spot]:
                place = jnp.clip(info_ref[at + 2 * spot] - own, -1, 1) + 1
                score = score + tile_ref[head, place].astype(jnp.float32)
            scores.append(score)
        top = functools.reduce(jnp.maximum, scores)
        lane = head * (PAIR // 2)
        top = jnp.maximum(old_max[:, lane : lane + 1], jnp.max(top, axis=1, keepdims=True))
        tops.append(top)
        weights.append([jnp.exp(score - top).astype(jnp.bfloat16) for score in scores])
    new_max = pair_select(tops[0], tops[1])
    ones = stack_heads(jnp.ones((BLOCK, PAIR), jnp.bfloat16))
    update = None
    for spot in range(count):
        right = jnp.concatenate([stack_heads(value_refs[spot][...]), ones], axis=1)
        left = jnp.concatenate([weights[0][spot], weights[1][spot]], axis=1)
        part = jnp.dot(left, right, preferred_element_type=jnp.float32)
        update = part if update is None else update + part
    if not first:
        factor = jnp.exp(old_max - new_max)
        update = update + total * jnp.concatenate([factor, factor], axis=1)
    if last:
        out_ref, low_ref, aux_ref = refs
        out = update[:, :PAIR] / update[:, PAIR:]
        out_ref[...] = out
        low_ref[...] = out.astype(jnp.bfloat16)
        log = -(new_max + jnp.log(update[:, PAIR:]))
        base = jnp.where(lanes() >= LEFT_LANE, 1.0, 0.0)
        base = jnp.where(pair == 0, base, aux_ref[...])
        for head in range(2):
            lane = head * (PAIR // 2)
            base = place_parts(base, log[:, lane : lane + 1], 8 * (2 * pair + head) + 3)
        aux_ref[...] = base
    else:
        max_out, total_out = refs
        max_out[...] = new_max
        total_out[...] = update


def forward_call(info, far, query, blocks, tiles, nears, state, last):
    count, first = len(blocks), state is None
    inner = query.shape[1]
    pairs = inner // PAIR
    in_specs = [view_spec(0, lambda p: p)]
    in_specs += [view_spec(row, lambda p: p) for _, row in blocks]
    in_specs += [view_spec(row, lambda p: p + pairs) for _, row in blocks]
    operands = [query] + [array for array, _ in blocks] * 2
    if any(nears):
        in_specs.append(tile_spec())
        operands.append(tiles)
    block = view_spec(0, lambda p: p)
    double = pl.BlockSpec((BLOCK, 2 * PAIR), lambda p, i, f: (0, p))
    if not first:
        in_specs += [block, double]
        operands += list(state)
    f32 = functools.partial(jax.ShapeDtypeStruct, dtype=jnp.float32)
    if last:
        out_shape = (
            f32((BLOCK, inner)),
            jax.ShapeDtypeStruct((BLOCK, inner), jnp.bfloat16),
            f32((BLOCK, PAIR)),
        )
        out_specs = (block, block, view_spec(0, lambda p: 0))
    else:
        out_shape = (f32((BLOCK, inner)), f32((BLOCK, 2 * inner)))
        out_specs = (block, double)
    kernel = functools.partial(forward_kernel, info[1], nears, first, last, 2 * pairs)
    return run_pairs(
        kernel, info[0], far, operands, in_specs, out_shape, out_specs, 6 * count, "attention_forward"
    )


def head_aux(aux, head, start):
    lane = lanes()
    keep = jnp.logical_and(lane // 8 == head, jnp.logical_and(lane % 8 >= start, lane % 8 < start + 3))
    return jnp.where(jnp.logical_and(keep, lane < 48), aux, 0.0)


def query_kernel(at, count, near, first, last, heads, info_ref, far_ref, *refs):
    refs = list(refs)
    query_ref, grad_ref, aux_ref = refs.pop(0), refs.pop(0), refs.pop(0)
    key_refs, refs = refs[:count], refs[count:]
    value_refs, refs = refs[:count], refs[count:]
    tile_ref = refs.pop(0) if near else None
    pair = pl.program_id(0)
    own = info_ref[0]
    query, grad = query_ref[...], grad_ref[...]
    aux = aux_ref[...].astype(jnp.float32)
    total = None if first else refs.pop(0)[...]
    lefts, grads = [], []
    for head in range(2):
        which = 2 * pair + head
        mine = own_lanes(far_ref, which, heads) + head_aux(aux, which, 3)
        lefts.append(jnp.concatenate([only_head(query, head == 1), mine.astype(jnp.bfloat16)], axis=1))
        delta = head_aux(aux, which, 0).astype(jnp.bfloat16)
        grads.append(jnp.concatenate([only_head(grad, head == 1), delta], axis=1))
    if near:
        diag_ref = refs.pop()
        strips = [[jnp.zeros((BLOCK, BLOCK), jnp.float32)] * 3 for _ in range(2)]
    lane = lanes()
    for spot in range(count):
        block, limit = info_ref[at + 2 * spot], info_ref[at + 1 + 2 * spot]
        kind = NEAR if near else kind_of(block, own)
        key, value = key_refs[spot][...], value_refs[spot][...]
        side = other_aux(block * BLOCK, limit, kind)
        wide_key = jnp.concatenate([key, side], axis=1)
        wide_value = jnp.concatenate([value, jnp.where(lane < 48, side, jnp.zeros_like(side))], axis=1)
        place = jnp.clip(block - own, -1, 1) + 1
        pieces, counts = [], []
        for head in range(2):
            scores = contract_last(lefts[head], wide_key)
            if near:
                scores = scores + tile_ref[head, place].astype(jnp.float32)
            score_grad = jnp.exp(scores) * contract_last(grads[head], wide_value)
            if near:
                strips[head] = [
                    strip + jnp.where(place == spot_of, score_grad, 0.0)
                    for spot_of, strip in enumerate(strips[head])
                ]
            pieces.append(score_grad.astype(jnp.bfloat16))
            counts.append(jnp.where(lane == 4 * head + kind, 1.0, 0.0).astype(jnp.bfloat16))
        right = jnp.concatenate([stack_heads(key), jnp.concatenate(counts, axis=0)], axis=1)
        part = jnp.dot(jnp.concatenate(pieces, axis=1), right, preferred_element_type=jnp.float32)
        total = part if total is None else total + part
    if near:
        rows = []
        for head in range(2):
            wide = jnp.concatenate(strips[head] + [jnp.zeros((BLOCK, BLOCK), jnp.float32)], axis=1)
            eight = None
            for group in range(BLOCK // 8):
                turned = pltpu.roll(wide[8 * group : 8 * group + 8], (255 - 8 * group) % SPAN_ROW, 1)
                eight = turned if eight is None else eight + turned
            line = None
            for row in range(8):
                turned = pltpu.roll(eight, (SPAN_ROW - row) % SPAN_ROW, 1)[row : row + 1]
                line = turned if line is None else line + turned
            rows.append(line)
        diag_ref[0] = jnp.concatenate(rows + [jnp.zeros((6, SPAN_ROW), jnp.float32)], axis=0)
    if last:
        low_ref, sum_ref = refs
        low_ref[...] = total[:, :PAIR].astype(jnp.bfloat16)
        sum_ref[0] = jnp.broadcast_to(jnp.sum(total[:, PAIR:], axis=0, keepdims=True), (8, PAIR))
    else:
        (total_ref,) = refs
        total_ref[...] = total


def query_call(info, far, query, grads, blocks, tiles, state, last):
    count, near, first = len(blocks), tiles is not None, state is None
    inner = query.shape[1]
    pairs = inner // PAIR
    own = view_spec(0, lambda p: p)
    in_specs = [own, own, view_spec(0, lambda p: pairs)]
    in_specs += [view_spec(row, lambda p: p) for _, row in blocks]
    in_specs += [view_spec(row, lambda p: p + pairs) for _, row in blocks]
    operands = [query, grads, grads] + [array for array, _ in blocks] * 2
    if near:
        in_specs.append(tile_spec())
        operands.append(tiles)
    double = pl.BlockSpec((BLOCK, 2 * PAIR), lambda p, i, f: (0, p))
    if not first:
        in_specs.append(double)
        operands.append(state)
    f32 = functools.partial(jax.ShapeDtypeStruct, dtype=jnp.float32)
    if last:
        out_shape = [jax.ShapeDtypeStruct((BLOCK, inner), jnp.bfloat16), f32((pairs, 8, PAIR))]
        out_specs = [own, pl.BlockSpec((1, 8, PAIR), lambda p, i, f: (p, 0, 0))]
    else:
        out_shape, out_specs = [f32((BLOCK, 2 * inner))], [double]
    if near:
        out_shape.append(f32((pairs, 8, SPAN_ROW)))
        out_specs.append(pl.BlockSpec((1, 8, SPAN_ROW), lambda p, i, f: (p, 0, 0)))
    kernel = functools.partial(query_kernel, info[1], count, near, first, last, 2 * pairs)
    return run_pairs(
        kernel, info[0], far, operands, in_specs, out_shape, out_specs, 8 * count, "attention_query_grad"
    )


def key_kernel(at, count, near, first, last, heads, info_ref, far_ref, *refs):
    refs = list(refs)
    key_ref, value_ref = refs.pop(0), refs.pop(0)
    query_refs, refs = refs[:count], refs[count:]
    grad_refs, refs = refs[:count], refs[count:]
    aux_refs, refs = refs[:count], refs[count:]
    tile_ref = refs.pop(0) if near else None
    pair = pl.program_id(0)
    own = info_ref[0]
    key, value = key_ref[...], value_ref[...]
    key_sum = value_sum = None
    if not first:
        key_sum, value_sum = refs.pop(0)[...], refs.pop(0)[...]
    key_out, value_out = refs
    lane = lanes()
    keys = [only_head(key, False), only_head(key, True)]
    values = []
    for head in range(2):
        pick = jnp.logical_and(lane // 8 == 2 * pair + head, lane % 8 < 3)
        values.append(
            jnp.concatenate([only_head(value, head == 1), jnp.where(pick, 1.0, 0.0).astype(jnp.bfloat16)], axis=1)
        )
    for spot in range(count):
        block, limit = info_ref[at + 2 * spot], info_ref[at + 1 + 2 * spot]
        kind = NEAR if near else kind_of(own, block)
        query, grad, aux = query_refs[spot][...], grad_refs[spot][...], aux_refs[spot][...]
        wide_query = jnp.concatenate([query, aux], axis=1)
        wide_grad = jnp.concatenate([grad, aux], axis=1)
        place = jnp.clip(own - block, -1, 1) + 1
        dead = jnp.logical_and(lane == DEAD_LANE, dead_rows(own * BLOCK, limit))
        probs_low, slopes_low = [], []
        for head in range(2):
            which = 2 * pair + head
            pick = jnp.logical_and(lane // 8 == which, jnp.logical_and(lane % 8 >= 3, lane % 8 < 6))
            side = jnp.where(pick, 1.0, 0.0)
            if not near:
                constant = jnp.where(kind == BEFORE, far_ref[which], far_ref[heads + which])
                side = jnp.where(lane == RIGHT_LANE, constant, side)
            side = jnp.where(dead, MASKED, side).astype(jnp.bfloat16)
            scores = contract_last(jnp.concatenate([keys[head], side], axis=1), wide_query)
            if near:
                scores = scores + tile_ref[head, place].astype(jnp.float32)
            probs = jnp.exp(scores)
            slopes = probs * contract_last(values[head], wide_grad)
            probs_low.append(probs.astype(jnp.bfloat16))
            slopes_low.append(slopes.astype(jnp.bfloat16))
        part_value = jnp.dot(
            jnp.concatenate(probs_low, axis=1), stack_heads(grad), preferred_element_type=jnp.float32
        )
        part_key = jnp.dot(
            jnp.concatenate(slopes_low, axis=1), stack_heads(query), preferred_element_type=jnp.float32
        )
        key_sum = part_key if key_sum is None else key_sum + part_key
        value_sum = part_value if value_sum is None else value_sum + part_value
    key_out[...] = key_sum.astype(key_out.dtype)
    value_out[...] = value_sum.astype(value_out.dtype)


def key_call(info, far, joined, queries, grads, turned, state, last):
    count, near, first = len(queries), turned is not None, state is None
    inner = joined.shape[1] // 2
    pairs = inner // PAIR
    own = view_spec(0, lambda p: p)
    in_specs = [own, view_spec(0, lambda p: p + pairs)]
    in_specs += [view_spec(row, lambda p: p) for _, row in queries]
    in_specs += [view_spec(row, lambda p: p) for _, row in grads]
    in_specs += [view_spec(row, lambda p: pairs) for _, row in grads]
    arrays = [array for array, _ in grads]
    operands = [joined, joined] + [array for array, _ in queries] + arrays + arrays
    if near:
        in_specs.append(tile_spec())
        operands.append(turned)
    if not first:
        in_specs += [own, own]
        operands += list(state)
    shape = jax.ShapeDtypeStruct((BLOCK, inner), jnp.bfloat16 if last else jnp.float32)
    kernel = functools.partial(key_kernel, info[1], count, near, first, last, 2 * pairs)
    return run_pairs(
        kernel, info[0], far, operands, in_specs, (shape, shape), (own, own), 10 * count, "attention_key_grad"
    )


def grads_kernel(first_ref, second_ref, third_ref, out_ref, aux_ref, grad_ref):
    total = first_ref[...] + second_ref[...].astype(jnp.float32) + third_ref[...]
    low = total.astype(jnp.bfloat16)
    inner = low.shape[1]
    grad_ref[:, :inner] = low
    product = low.astype(jnp.float32) * out_ref[...]
    base = aux_ref[...]
    for pair in range(inner // PAIR):
        piece = product[:, pair * PAIR : (pair + 1) * PAIR]
        for head in range(2):
            delta = -jnp.sum(only_head(piece, head == 1), axis=1, keepdims=True)
            base = place_parts(base, delta, 8 * (2 * pair + head))
    grad_ref[:, inner:] = base.astype(jnp.bfloat16)


def finish_grads(first, second, third, out, aux):
    return pl.pallas_call(
        grads_kernel,
        out_shape=jax.ShapeDtypeStruct((BLOCK, out.shape[1] + PAIR), jnp.bfloat16),
        name="attention_out_grad",
    )(first, second, third, out, aux)

def feed_kernel(spot_ref, *refs):
    token_refs, cot_refs, mixed_refs = refs[:4], refs[4:8], refs[8:12]
    gain_ref, out_w_ref, gate_w_ref, up_w_ref, down_w_ref = refs[12:17]
    (
        second_ref,
        hidden_ref,
        gate_ref,
        up_ref,
        outer_ref,
        rows_ref,
        kept_ref,
        passed_ref,
        sent_ref,
        grad_kept_ref,
        grad_sent_ref,
        gain_sum_ref,
    ) = refs[17:29]
    token_all, cot_all, mixed_all, live_all = refs[29:]
    f32, bf16 = jnp.float32, jnp.bfloat16
    step = pl.program_id(0)
    gain = gain_ref[...]
    width = gain.shape[1]
    row = lax.broadcasted_iota(jnp.int32, (BLOCK, 1), 0)

    def load(which):
        for spot in range(2):
            at = slice(spot * BLOCK, (spot + 1) * BLOCK)
            token_all[at, :] = token_refs[2 * which + spot][:, :width]
            cot_all[at, :] = cot_refs[2 * which + spot][:, :width]
            mixed_all[at, :] = mixed_refs[2 * which + spot][...]
            block = spot_ref[1] if which == 0 else spot_ref[1] ^ 1
            alive = block * BLOCK + row < spot_ref[2 + spot]
            live_all[at, :] = jnp.broadcast_to(jnp.where(alive, 1.0, 0.0), (BLOCK, PAIR))

    @pl.when(step == 0)
    def _():
        load(0)

    @pl.when(step > 0)
    def _():
        load(1)

    live = live_all[:, 0:1]
    branch = contract_last(mixed_all[...], out_w_ref[...])
    rows = token_all[...].astype(f32) + live * branch
    scale = lax.rsqrt(jnp.mean(rows * rows, axis=-1, keepdims=True) + EPSILON)
    unit = rows * scale
    second = (unit * gain).astype(bf16)
    second_ref[...] = second
    outer = (cot_all[...].astype(f32) * live).astype(bf16)
    outer_ref[...] = outer
    count = gate_w_ref.shape[1]
    for start in range(0, count, 256):
        at = slice(start, min(start + 256, count))
        gate = jnp.dot(second, gate_w_ref[:, at], preferred_element_type=f32)
        up = jnp.dot(second, up_w_ref[:, at], preferred_element_type=f32)
        back = jnp.dot(outer, down_w_ref[:, at], preferred_element_type=f32)
        square = gate * gate
        bend = jnp.tanh(GELU_SCALE * gate * (1.0 + GELU_CUBE * square))
        curve = 0.5 * gate * (1.0 + bend)
        hidden_ref[:, at] = (curve * up).astype(bf16)
        rise = 0.5 * (1.0 + bend) + 0.5 * GELU_SCALE * gate * (1.0 - bend * bend) * (
            1.0 + 3.0 * GELU_CUBE * square
        )
        gate_ref[:, at] = (back * up * rise).astype(bf16)
        up_ref[:, at] = (back * curve).astype(bf16)
    second_grad = contract_last(gate_ref[...], gate_w_ref[...]) + contract_last(up_ref[...], up_w_ref[...])
    line = jnp.sum(second_grad * unit, axis=0, keepdims=True)

    @pl.when(step == 0)
    def _():
        gain_sum_ref[...] = line
        rows_ref[...] = rows[:BLOCK]

    @pl.when(step > 0)
    def _():
        gain_sum_ref[...] += line

    scaled = second_grad * gain
    middle = live * scale * (scaled - unit * jnp.mean(scaled * unit, axis=-1, keepdims=True))
    middle = middle.astype(bf16)
    grad = jnp.dot(middle, out_w_ref[...], preferred_element_type=f32).astype(bf16)
    feed = contract_last(hidden_ref[...], down_w_ref[...]).astype(bf16)

    @pl.when(step == 0)
    def _():
        kept_ref[0], kept_ref[1] = feed[:BLOCK], middle[:BLOCK]
        passed_ref[...] = jnp.zeros_like(passed_ref)
        passed_ref[0, :, :width], passed_ref[1, :, :width] = feed[BLOCK:], middle[BLOCK:]
        grad_kept_ref[...] = grad

    @pl.when(step > 0)
    def _():
        sent_ref[...] = jnp.zeros_like(sent_ref)
        sent_ref[0, :, :width], sent_ref[1, :, :width] = feed, middle
        grad_sent_ref[...] = grad


def feed_call(spots, tokens, cots, mixed, gain, out_w, gate_w, up_w, down_w):
    f32, bf16 = jnp.float32, jnp.bfloat16
    width, inner = out_w.shape
    wide = tokens[0][0].shape[1]
    units = gate_w.shape[1] // 2
    step, total = 2 * BLOCK, 4 * BLOCK
    once = pl.Buffered(1)

    def rows_of(row, lanes_of):
        return pl.BlockSpec((BLOCK, lanes_of), lambda s, i: (row, 0), pipeline_mode=once)

    def moving(lanes_of):
        return pl.BlockSpec((step, lanes_of), lambda s, i: (s, 0))

    def fixed(*shape):
        return pl.BlockSpec(shape, lambda s, i: (0,) * len(shape), pipeline_mode=once)

    shape = jax.ShapeDtypeStruct
    in_specs = [rows_of(row, array.shape[1]) for array, row in (*tokens, *cots, *mixed)]
    in_specs += [
        fixed(1, width),
        fixed(*out_w.shape),
        pl.BlockSpec((width, units), lambda s, i: (0, i[0]), pipeline_mode=once),
        pl.BlockSpec((width, units), lambda s, i: (0, i[0]), pipeline_mode=once),
        pl.BlockSpec((width, units), lambda s, i: (0, i[0]), pipeline_mode=once),
    ]
    return pl.pallas_call(
        feed_kernel,
        grid_spec=pltpu.PrefetchScalarGridSpec(
            num_scalar_prefetch=1,
            grid=(2,),
            in_specs=in_specs,
            out_specs=(
                moving(width),
                moving(units),
                moving(units),
                moving(units),
                moving(width),
                fixed(BLOCK, width),
                fixed(2, BLOCK, width),
                fixed(2, BLOCK, wide),
                fixed(2, step, wide),
                fixed(step, inner),
                fixed(step, inner),
                fixed(1, width),
            ),
            scratch_shapes=[
                pltpu.VMEM((step, width), bf16),
                pltpu.VMEM((step, width), bf16),
                pltpu.VMEM((step, inner), bf16),
                pltpu.VMEM((step, PAIR), f32),
            ],
        ),
        out_shape=(
            shape((total, width), bf16),
            shape((total, units), bf16),
            shape((total, units), bf16),
            shape((total, units), bf16),
            shape((total, width), bf16),
            shape((BLOCK, width), f32),
            shape((2, BLOCK, width), bf16),
            shape((2, BLOCK, wide), bf16),
            shape((2, step, wide), bf16),
            shape((step, inner), bf16),
            shape((step, inner), bf16),
            shape((1, width), f32),
        ),
        compiler_params=pltpu.CompilerParams(vmem_limit_bytes=63_000_000),
        cost_estimate=estimate(
            flops=2 * total * width * (6 * units + 2 * inner),
            bytes_accessed=2 * (3 * width * units + 8 * total * width),
            transcendentals=total * units,
        ),
        name="feed_forward",
    )(spots, *[array for array, _ in (*tokens, *cots, *mixed)], gain, out_w, gate_w, up_w, down_w)


def weight_kernel(spot_ref, left_ref, right_ref, kept_ref, sent_ref, product_ref):
    y, core, side = spot_ref[0], spot_ref[1], spot_ref[2]
    use = kept_ref.shape[2]
    product_ref[...] = lax.dot_general(
        left_ref[...], right_ref[...], (((0,), (0,)), ((), ())), preferred_element_type=jnp.float32
    )
    for out_ref, y_bit in ((kept_ref, y), (sent_ref, 1 - y)):
        for apart_x in range(2):
            for apart_k in range(2):
                k_bit = core if apart_k == 0 else 1 - core
                x_bit = side if apart_x == 0 else 1 - side
                block = y_bit * 4 + k_bit * 2 + x_bit
                rows = product_ref[pl.ds(pl.multiple_of(block * use, 16), use), :]
                out_ref[apart_x, apart_k] = rows.astype(jnp.bfloat16)


def weight_call(spots, left, right):
    width = right.shape[1]
    use = left.shape[1] // 8
    shape = jax.ShapeDtypeStruct((2, 2, use, width), jnp.bfloat16)
    return pl.pallas_call(
        weight_kernel,
        grid_spec=pltpu.PrefetchScalarGridSpec(
            num_scalar_prefetch=1,
            grid=(1,),
            in_specs=[
                pl.BlockSpec(left.shape, lambda s, i: (0, 0)),
                pl.BlockSpec(right.shape, lambda s, i: (0, 0)),
            ],
            out_specs=(
                pl.BlockSpec(shape.shape, lambda s, i: (0, 0, 0, 0)),
                pl.BlockSpec(shape.shape, lambda s, i: (0, 0, 0, 0)),
            ),
            scratch_shapes=[pltpu.VMEM((left.shape[1], width), jnp.float32)],
        ),
        out_shape=(shape, shape),
        compiler_params=pltpu.CompilerParams(vmem_limit_bytes=60_000_000),
        cost_estimate=estimate(
            flops=2 * left.shape[0] * left.shape[1] * width,
            bytes_accessed=2 * (left.size + right.size + 8 * use * width),
            transcendentals=0,
        ),
        name="feed_weight_grad",
    )(spots, left, right)


def projection_kernel(spot_ref, query_ref, key_ref, value_ref, mixed_ref, first_kept_ref, first_sent_ref, branch_kept_ref, branch_sent_ref, kept_ref, sent_ref):
    core, y, z_high, z_low = spot_ref[0], spot_ref[1], spot_ref[2], spot_ref[3]
    inner = query_ref.shape[1]
    columns = inner // 16
    size = inner // 2
    for out_ref, k_bit in ((kept_ref, core), (sent_ref, 1 - core)):
        target = lax.broadcasted_iota(jnp.int32, (inner, size), 1)
        group, inside = target // columns, target % columns
        z_bits = ((group // 2) % 2) ^ z_high, (group % 2) ^ z_low
        source = (((z_bits[0] * 2 + z_bits[1]) * 2 + ((group // 4) ^ y)) * 2 + k_bit) * columns + inside
        chooser = jnp.where(lax.broadcasted_iota(jnp.int32, (inner, size), 0) == source, 1.0, 0.0).astype(jnp.bfloat16)
        for spot, ref in enumerate((query_ref, key_ref, value_ref, mixed_ref)):
            picked = jnp.dot(ref[...], chooser, preferred_element_type=jnp.float32).astype(jnp.bfloat16)
            rights = (branch_kept_ref, branch_sent_ref) if spot == 3 else (first_kept_ref, first_sent_ref)
            for lane_half, right in enumerate(rights):
                out_ref[lane_half * 4 + spot] = lax.dot_general(
                    picked, right[...], (((0,), (0,)), ((), ())), preferred_element_type=jnp.float32
                ).astype(jnp.bfloat16)


def projection_call(spots, query, keys, values, mixed, first_lanes, branch_lanes):
    shape = jax.ShapeDtypeStruct((8, query.shape[1] // 2, first_lanes[0].shape[1]), jnp.bfloat16)
    operands = [query, keys, values, mixed, *first_lanes, *branch_lanes]
    return pl.pallas_call(
        projection_kernel,
        grid_spec=pltpu.PrefetchScalarGridSpec(
            num_scalar_prefetch=1,
            grid=(1,),
            in_specs=[pl.BlockSpec(a.shape, lambda s, i: (0, 0)) for a in operands],
            out_specs=[pl.BlockSpec(shape.shape, lambda s, i: (0, 0, 0))] * 2,
        ),
        out_shape=[shape, shape],
        cost_estimate=estimate(
            flops=2 * 4 * query.size * 2 * first_lanes[0].shape[1], bytes_accessed=8 * 2 * query.size, transcendentals=0
        ),
        name="projection_weight_grad",
    )(spots, *operands)


def grouped_body(
    tokens,
    lengths,
    buckets,
    attention_gain,
    query_weight,
    key_weight,
    value_weight,
    output_weight,
    bias_table,
    feed_gain,
    gate_weight,
    up_weight,
    down_weight,
    cotangent,
):
    bf16, f32 = jnp.bfloat16, jnp.float32
    places = lax.axis_size("ctx")
    chips = places // 2
    rows_of_chips = chips // 2
    here = lax.axis_index("ctx")
    side = lax.axis_index("wsh")
    core = here % 2
    chip = here // 2
    lane_y = chip % 2
    lane_z = chip // 2
    length = tokens.shape[1]
    half = tokens.shape[2] // 2
    heads = bias_table.shape[1]
    inner = query_weight.shape[1]
    nowhere = -(1 << 20)

    def spread(block, route):
        return lax.ppermute(block, AXES, route)

    def route_of(move):
        pairs = []
        for c in range(places):
            for w in range(2):
                target = move(c // 4, (c // 2) % 2, c % 2, w)
                if target is not None:
                    z, y, k, x = target
                    pairs.append((c * 2 + w, (((z * 2 + y) * 2) + k) * 2 + x))
        return pairs

    route_core = route_of(lambda z, y, k, x: (z, y, 1 - k, x))
    route_x = route_of(lambda z, y, k, x: (z, y, k, 1 - x))
    route_y = route_of(lambda z, y, k, x: (z, 1 - y, k, x))
    route_far = route_of(lambda z, y, k, x: (z ^ 2, y, k, x))
    route_near = route_of(lambda z, y, k, x: (z ^ 1, y, k, x))
    order = [(i, 0) for i in range(rows_of_chips)] + [
        (rows_of_chips - 1 - i, 1) for i in range(rows_of_chips)
    ]
    place = {spot: i for i, spot in enumerate(order)}
    route_ring = route_of(
        lambda z, y, k, x: (*order[(place[(z, y)] + 1 - 2 * k) % chips], k, x)
    )
    route_next = [
        ((c * 2 + w), (c + (1 if c % 2 else -1)) * 2 + w)
        for c in range(places)
        for w in range(2)
        if 0 <= c + (1 if c % 2 else -1) < places
    ]
    my_place = jnp.where(lane_y == 0, lane_z, 2 * rows_of_chips - 1 - lane_z)
    toward = jnp.where(core == 0, -1, 1)
    next_block = here - 1 + 2 * core
    has_next = jnp.logical_and(next_block >= 0, next_block < places)

    def chip_at(spot):
        spot = (spot + 2 * chips) % chips
        return jnp.where(
            spot < rows_of_chips, 2 * spot, 2 * (2 * rows_of_chips - 1 - spot) + 1
        )

    def swap_core(block):
        return spread(block, route_core)

    def swap_x(block):
        return spread(block, route_x)

    def both_sides(mine, other, axis):
        return jnp.where(
            side == 0,
            jnp.concatenate([mine, other], axis=axis),
            jnp.concatenate([other, mine], axis=axis),
        )

    def after(block, *others):
        return lax.optimization_barrier((block, *others))[0]

    live_count = jnp.minimum(lengths[0, 0], places * length)
    middle = chips // 2
    width = tokens.shape[2]

    def blocks_at(step):
        ahead = chip_at(my_place + toward * step)
        if step == middle:
            return [ahead * 2 + core, ahead * 2 + 1 - core]
        behind = chip_at(my_place - toward * step)
        return [ahead * 2 + core, ahead * 2 + 1 - core, behind * 2 + 1 - core, behind * 2 + core]

    def info_of(blocks, near):
        entries = []
        for block in blocks:
            limit = live_count
            if near:
                limit = jnp.where(jnp.logical_or(block != next_block, has_next), limit, nowhere)
            else:
                limit = jnp.where(block == next_block, nowhere, limit)
            entries += [block, limit]
        return entries

    marks = []

    def then(*blocks):
        if not marks:
            return blocks if len(blocks) > 1 else blocks[0]
        held = lax.optimization_barrier((*blocks, *marks))[: len(blocks)]
        return held if len(blocks) > 1 else held[0]

    def mark(*blocks):
        marks[:] = blocks

    def add_low(left, right):
        return (left.astype(f32) + right.astype(f32)).astype(bf16)

    quarter = half // 2

    def my_rows(block, which, count):
        return lax.dynamic_slice_in_dim(block, which * count, count, 0)

    def plain(block):
        return with_layout_constraint(block, Layout(tuple(range(block.ndim))))

    small = jnp.concatenate(
        [
            attention_gain,
            feed_gain,
            bias_table.reshape(-1),
            jnp.stack([live_count // 128, live_count % 128]).astype(bf16),
        ]
    )
    size_small = small.shape[0]
    small = jnp.pad(small, (0, -size_small % 2048)).reshape(-1, 128)
    small_other = swap_x(small).reshape(-1)
    projections = [key_weight, value_weight, query_weight]
    sent_rows = jnp.concatenate([my_rows(w, core, quarter) for w in projections], axis=1)
    sent_rows = after(sent_rows, small)
    part = swap_x(sent_rows)
    lanes_left = -width % PAIR

    def padded(block):
        return jnp.pad(block, ((0, 0), (0, lanes_left)))

    mine, cot = plain(padded(tokens[0])), plain(padded(cotangent[0]))
    tokens_core = swap_core(after(mine, sent_rows))
    output_turned = jnp.transpose(output_weight)
    gain_other = small_other[:half]
    feed_other = small_other[half : 2 * half]
    table_other = small_other[2 * half : size_small - 2].reshape(bias_table.shape)
    counts = small_other[size_small - 2 : size_small].astype(f32).astype(jnp.int32)
    count_other = counts[0] * 128 + counts[1]
    gain_one = both_sides(attention_gain, gain_other, 0).astype(f32)
    gain_two = both_sides(feed_gain, feed_other, 0).astype(f32)
    table = both_sides(bias_table, table_other, 0)
    bucket_count = table.shape[0]
    reach = (buckets.shape[0] + 1) // 2
    offsets = jnp.clip(jnp.arange(SPAN_ROW, dtype=jnp.int32) - 511, 1 - reach, reach - 1) + (reach - 1)
    spots = jnp.arange(buckets.shape[0], dtype=jnp.int32)
    chosen = jnp.sum(jnp.where(offsets[:, None] == spots[None, :], buckets[None, :], 0), axis=1)
    onehot = (chosen[:, None] == jnp.arange(bucket_count, dtype=jnp.int32)[None, :]).astype(f32)
    offset_rows = lax.dot_general(
        table.astype(f32), onehot, (((0,), (1,)), ((), ())), precision=HIGH, preferred_element_type=f32
    )
    tiles, turned = bias_tiles(offset_rows)
    far = jnp.concatenate([offset_rows[:, 0], offset_rows[:, SPAN_ROW - 2]])
    entries = [here] + info_of([here, here ^ 1, next_block], True)
    near_info, far_info = 1, []
    for step in range(1, middle + 1):
        far_info.append(len(entries))
        entries += info_of(blocks_at(step), False)
    entries += info_of([next_block], True)
    infos = jnp.stack(entries).astype(jnp.int32)

    inputs = mine[:, :width].astype(f32)
    scale_one = row_scale(inputs)
    first = (inputs * scale_one * gain_one).astype(bf16)
    partner_inputs = tokens_core[:, :width].astype(f32)
    first_partner = (partner_inputs * row_scale(partner_inputs) * gain_one).astype(bf16)
    first_pair = jnp.concatenate([first, first_partner], axis=0)

    def lanes_of(block):
        low_half, high_half = block[:, :half], block[:, half:]
        return (
            jnp.where(side == 0, low_half, high_half),
            jnp.where(side == 0, high_half, low_half),
        )

    pair_lanes = lanes_of(first_pair)
    first_lanes = [block[:length] for block in pair_lanes]
    weight_mine = jnp.concatenate(projections, axis=1)
    projected = jnp.dot(pair_lanes[0], weight_mine, preferred_element_type=f32)
    rows_own = jnp.concatenate([mine, cot], axis=0)
    held = lax.optimization_barrier((part, tiles, turned, far, infos, projected, pair_lanes[1], rows_own, weight_mine))
    part, tiles, turned, far, infos, projected, lanes_other, rows_own, weight_mine = held
    traded = swap_core(part)
    rows_side = swap_x(rows_own)

    def join_rows(part, traded):
        return jnp.where(
            core == 0,
            jnp.concatenate([part, traded], axis=0),
            jnp.concatenate([traded, part], axis=0),
        )

    weight_other = join_rows(part, traded)
    projected = (projected + jnp.dot(lanes_other, weight_other, preferred_element_type=f32)).astype(bf16)
    chunk, query_chunk = projected[:, : 2 * inner], projected[:, 2 * inner :]
    joined, query = chunk, query_chunk

    def start_ring(block):
        return jnp.concatenate([block, swap_core(block)], axis=0)

    def next_chunk(chunk, step):
        if step == middle:
            return spread(chunk[:length], route_ring)
        return spread(chunk, route_ring)

    def views(chunk):
        return [(chunk, row) for row in range(chunk.shape[0] // length)]

    received = next_chunk(chunk, 1)
    query_first = query_chunk
    query_received = next_chunk(query_chunk, 1)
    next_joined = spread(chunk[:length], route_next)
    query_next = spread(query_chunk[:length], route_next)
    near_views = views(chunk) + [(next_joined, 0)]
    state = forward_call((infos, near_info), far, query, near_views[:2], tiles, (True, True), None, False)
    far_views, query_views = [], []
    for step in range(1, middle + 1):
        received, _ = lax.optimization_barrier((received, state))
        following = next_chunk(received, step + 1) if step < middle else None
        partner = swap_core(received)
        now = views(received) + views(partner)
        far_views.append(now)
        if step > 1:
            query_partner = swap_core(query_received)
            query_views.append(views(query_received) + views(query_partner))
            forced = (query_received, query_partner)
            query_received = next_chunk(query_received, step)
            state = lax.optimization_barrier((*state, *forced))[:2]
        if step == 2:
            cot_core = swap_core(after(cot, state))
            rows_side = lax.optimization_barrier((rows_side, *state))[0]
            rows_both = swap_core(rows_side)
            out_part = swap_x(after(my_rows(output_turned, core, quarter), rows_side))
            state = lax.optimization_barrier((*state, rows_both, cot_core))
            rows_both, cot_core = state[2:]
            state = state[:2]
        if step == 4:
            out_traded = swap_core(after(out_part, state))
            output_full = both_sides(output_turned, join_rows(out_part, out_traded), 0)
            positions = here * length + jnp.arange(length, dtype=jnp.int32)
            live_own = (positions < live_count).astype(f32)[:, None]
            outer_own = cot[:, :width].astype(f32) * live_own
            grad_own = jnp.einsum(
                "td,di->ti", outer_own.astype(bf16), output_full, preferred_element_type=f32
            )
            state = lax.optimization_barrier((*state, output_full, grad_own))
            output_full, grad_own = state[2:]
            state = state[:2]
        if step == middle:
            blocks, nears = now + [near_views[2]], (False,) * len(now) + (True,)
        else:
            blocks, nears = now, (False,) * len(now)
        state = forward_call(
            (infos, far_info[step - 1]), far, query, blocks, tiles, nears, state, step == middle
        )
        query_received = lax.optimization_barrier((query_received, *state))[0]
        received = following
    attention, attention_low, aux = state
    query_partner = swap_core(query_received)

    mixed_side = swap_x(attention_low)
    mixed_core = swap_core(attention_low)
    mixed_both = swap_core(mixed_side)
    mixed_both, query_received, query_partner = lax.optimization_barrier((mixed_both, query_received, query_partner))
    query_views.append(views(query_received) + views(query_partner))
    feed_spots = jnp.stack([core, here, live_count, count_other]).astype(jnp.int32)
    (
        second,
        hidden,
        gate_low,
        up_low,
        outer_low,
        middle_own,
        both_kept,
        both_passed,
        both_sent,
        grad_kept,
        grad_sent,
        feed_gain_part,
    ) = feed_call(
        feed_spots,
        [(mine, 0), (rows_side, 0), (tokens_core, 0), (rows_both, 0)],
        [(cot, 0), (rows_side, 1), (cot_core, 0), (rows_both, 1)],
        [(attention_low, 0), (mixed_side, 0), (mixed_core, 0), (mixed_both, 0)],
        gain_two[None, :],
        output_full,
        gate_weight,
        up_weight,
        jnp.transpose(down_weight),
    )

    outer_chips = [0, rows_of_chips - 1]
    route_inward = route_of(
        lambda z, y, k, x: ((1 if z == 0 else 2), y, k, x) if z in outer_chips else None
    )
    route_across = route_of(lambda z, y, k, x: (3 - z, y, k, x) if z in (1, 2) else None)
    route_third = route_of(lambda z, y, k, x: (z ^ 1, y, k, x) if z % 2 != k else None)
    route_fourth = route_of(lambda z, y, k, x: (z, y, 1 - k, x) if z % 2 == k else None)
    z_low = lane_z % 2
    upper = lane_z // 2

    def split_x(kept, got):
        total = add_low(kept, got)
        return total[0], total[1]

    def join_x(kept, got):
        return jnp.where(side == upper, kept, got), jnp.where(side == upper, got, kept)

    def reduce_last(block):
        return jnp.where(z_low == core, block[0], spread(block[1], route_fourth)).astype(f32)

    weight_spots = jnp.stack([lane_y, core, side]).astype(jnp.int32)
    grad_got = swap_core(grad_sent)
    down_kept, down_sent = weight_call(weight_spots, hidden, outer_low)
    mark(down_sent)
    grad_kept, grad_got = then(grad_kept, grad_got)
    grad_sum = grad_kept.astype(f32) + grad_got.astype(f32)
    grad_passed = grad_sum[length:].astype(bf16)
    grad_side = swap_x(grad_passed)
    mark(grad_passed)
    gate_kept, gate_sent = weight_call(weight_spots, then(gate_low), second)
    mark(gate_sent)
    grad_side = then(grad_side)
    grads = finish_grads(grad_sum[:length], grad_side, grad_own, attention, aux)

    grad_chunk = start_ring(grads)
    received = next_chunk(grad_chunk, 1)
    grad_next = spread(grads, route_next)
    both_got = swap_core(after(both_sent, grad_chunk))
    query_state, diagonals = query_call((infos, near_info), far, query, after(grads, grad_chunk), near_views, tiles, None, False)
    mark(query_state)
    both_passed, both_got = then(both_passed, both_got)
    both_passed = add_low(both_passed, both_got[:, length:])
    both_side = swap_x(both_passed)
    mark(query_state, both_passed)
    grad_views = []
    for step in range(1, middle + 1):
        received = then(received)
        following = next_chunk(received, step + 1) if step < middle else None
        partner = swap_core(received)
        grad_views.append(views(received) + views(partner))
        outs = query_call(
            (infos, far_info[step - 1]), far, query, after(grads, received), far_views[step - 1], None, query_state, step == middle
        )
        query_state = outs[0]
        mark(query_state)
        if step == 2:
            grad_next, query_next = then(grad_next, query_next)
            mark(query_state, grad_next, query_next)
        if step == middle:
            down_got = spread(after(down_sent, received), route_y)
            gate_got = spread(after(gate_sent, received), route_y)
        received = following
    query_low, far_sums = outs

    def key_step(step, state):
        if step == 0:
            queries = views(query_first) + [(query_next, 0)]
            outs = key_call(
                (infos, near_info), far, then(chunk), queries, views(grad_chunk) + [(grad_next, 0)], turned, None, False
            )
        else:
            outs = key_call(
                (infos, far_info[step - 1]), far, then(chunk), query_views[step - 1], grad_views[step - 1], None, state, step == middle
            )
        mark(outs[0])
        return outs

    key_state = key_step(0, None)
    up_kept, up_sent = weight_call(weight_spots, then(up_low), second)
    mark(up_sent)
    down_x, down_sent = split_x(*then(down_kept, down_got))
    down_got = swap_x(down_sent)
    up_got = spread(after(up_sent, down_sent), route_y)
    mark(down_sent)
    key_state = key_step(1, key_state)
    key_state = key_step(2, key_state)
    down_stays, down_leaves = join_x(*then(down_x, down_got))
    down_got = spread(down_leaves, route_inward)
    mark(down_leaves)
    key_state = key_step(3, key_state)
    gate_x, gate_sent = split_x(*then(gate_kept, gate_got))
    gate_got = swap_x(gate_sent)
    mark(gate_sent)
    key_state = key_step(4, key_state)
    keys_low, values_low = key_state
    down_leaves = add_low(*then(down_leaves, down_got))
    down_got = spread(down_leaves, route_across)
    mark(down_leaves)

    both_kept, both_got, both_side = then(both_kept, both_got, both_side)
    both_total = both_kept.astype(f32) + both_got[:, :length, :width].astype(f32) + both_side[:, :, :width].astype(f32)
    result = (middle_own + live_own * both_total[0]).astype(bf16)
    middle_grad = outer_own + both_total[1]
    branch_low = (live_own * middle_grad).astype(bf16)
    mark(branch_low)

    projection_spots = jnp.stack([core, lane_y, upper, z_low]).astype(jnp.int32)
    kept_core, sent_core = projection_call(
        projection_spots, query_low, keys_low, values_low, attention_low, first_lanes, lanes_of(branch_low)
    )
    got_core = swap_core(sent_core)
    mark(sent_core)
    gate_stays, gate_leaves = join_x(*then(gate_x, gate_got))
    gate_got = spread(gate_leaves, route_inward)
    mark(gate_leaves)
    kept_core, got_core = then(kept_core, got_core)
    core_sum = kept_core.astype(f32) + got_core.astype(f32)
    passed = core_sum[4:].astype(bf16)
    got_x = swap_x(passed)
    mark(passed)
    up_x, up_sent = split_x(*then(up_kept, up_got))
    up_got = swap_x(up_sent)
    mark(up_sent)
    down_stays = add_low(*then(down_stays, down_got))
    down_got = spread(down_stays, route_third)
    mark(down_stays)

    gradients = then(jnp.concatenate([keys_low, values_low, query_low], axis=1))
    first_grad = both_sides(contract_last(gradients, weight_mine), contract_last(gradients, weight_other), 1)
    unit_one = inputs * scale_one
    gain_one_part = jnp.sum(first_grad * unit_one, axis=0)
    scaled_one = first_grad * gain_one
    input_gradient = (
        middle_grad
        + scale_one * (scaled_one - unit_one * jnp.mean(scaled_one * unit_one, axis=-1, keepdims=True))
    ).astype(bf16)
    mark(input_gradient)

    lines = diagonals[:, :2].reshape(heads, SPAN_ROW)
    outside = far_sums[:, 0].reshape(heads // 2, PAIR)[:, :8].reshape(heads, 4)
    lines = lines.at[:, 0].add(outside[:, BEFORE]).at[:, SPAN_ROW - 2].add(outside[:, AFTER])
    table_part = lax.dot_general(
        onehot, lines, (((0,), (1,)), ((), ())), precision=HIGH, preferred_element_type=f32
    )
    flat = jnp.concatenate([gain_one_part, feed_gain_part[0], table_part.reshape(-1)])
    used = flat.shape[0]
    flat = jnp.pad(flat, (0, -used % 1024)).reshape(-1, 128)
    flat = flat + spread(flat, route_core)
    flat_got = spread(flat, route_near)
    mark(flat)
    gate_leaves = add_low(*then(gate_leaves, gate_got))
    gate_got = spread(gate_leaves, route_across)
    mark(gate_leaves)
    flat, flat_got = then(flat, flat_got)
    flat = flat + flat_got
    flat_got = spread(flat, route_far)
    kept_x, got_x = then(core_sum[:4], got_x)
    total = (kept_x + got_x.astype(f32)).astype(bf16)
    size = total.shape[1] // 2
    got = spread(total[:, size:], route_y)
    mark(total)
    up_stays, up_leaves = join_x(*then(up_x, up_got))
    up_got = spread(up_leaves, route_inward)
    mark(up_leaves)
    down_last = add_low(*then(down_stays, down_got))
    down_out = reduce_last(down_last)
    flat, flat_got = then(flat, flat_got)
    flat = flat + flat_got
    flat_got = spread(flat, route_y)
    mark(flat)
    total, got = then(total, got)
    total = add_low(total[:, :size], got)
    size = size // 2
    got = spread(total[:, size:], route_far)
    mark(total)
    gate_stays = add_low(*then(gate_stays, gate_got))
    gate_got = spread(gate_stays, route_third)
    mark(gate_stays)
    up_leaves = add_low(*then(up_leaves, up_got))
    up_got = spread(up_leaves, route_across)
    mark(up_leaves)
    flat, flat_got = then(flat, flat_got)
    flat = flat + flat_got
    flat_got = spread(flat, route_x)
    total, got = then(total, got)
    total = add_low(total[:, :size], got)
    size = size // 2
    got = spread(total[:, size:], route_near)
    mark(total)
    gate_out = jnp.transpose(reduce_last(add_low(*then(gate_stays, gate_got))))
    up_stays = add_low(*then(up_stays, up_got))
    up_got = spread(up_stays, route_third)
    mark(up_stays)
    total, got = then(total, got)
    total = add_low(total[:, :size], got).astype(f32)
    projection_out = jnp.transpose(total[:3], (0, 2, 1))
    flat, flat_got = then(flat, flat_got)
    flat = (flat + flat_got).reshape(-1)
    mark(total)
    up_out = jnp.transpose(reduce_last(add_low(*then(up_stays, up_got))))
    gain_one_sum = flat[:width]
    feed_gain_sum = flat[width : 2 * width]
    table_sum = flat[2 * width : used].reshape(bucket_count, heads)

    def my_half(block):
        size = block.shape[0] // 2
        return lax.dynamic_slice_in_dim(block, side * size, size, 0)

    return (
        result[None],
        input_gradient[None],
        my_half(gain_one_sum),
        projection_out[0],
        projection_out[1],
        projection_out[2],
        total[3],
        my_half(table_sum),
        my_half(feed_gain_sum),
        gate_out,
        up_out,
        down_out,
    )


def solution(mesh):
    placed = (
        P("wsh", "ctx", None),
        P("wsh", None),
        P(),
        P("wsh"),
        P("wsh", None),
        P("wsh", None),
        P("wsh", None),
        P(None, "wsh"),
        P("wsh", None),
        P("wsh"),
        P(None, "wsh"),
        P(None, "wsh"),
        P("wsh", None),
        P("wsh", "ctx", None),
    )
    step = grouped_body if mesh.shape["ctx"] == 16 else body
    return jax.shard_map(
        step,
        mesh=mesh,
        in_specs=placed,
        out_specs=(
            P("wsh", "ctx", None),
            P("wsh", "ctx", None),
            P("wsh"),
            P("wsh", "ctx"),
            P("wsh", "ctx"),
            P("wsh", "ctx"),
            P("ctx", "wsh"),
            P("wsh", None),
            P("wsh"),
            P(None, ("ctx", "wsh")),
            P(None, ("ctx", "wsh")),
            P(("ctx", "wsh"), None),
        ),
        check_vma=False,
    )
```

```python
import functools

import jax
import jax.numpy as jnp
from jax import lax
from jax.experimental import pallas as pl
from jax.experimental.layout import Layout, with_layout_constraint
from jax.experimental.pallas import tpu as pltpu
from jax.sharding import PartitionSpec as P

EPSILON = 1e-06
MASKED = -1e30
HIGH = lax.Precision.HIGHEST


def shifted(block, axis, distance):
    devices = range(lax.axis_size(axis))
    route = [((i - distance) % len(devices), i) for i in devices]
    return lax.ppermute(block, axis, route)


def row_scale(values):
    return lax.rsqrt(jnp.mean(values * values, axis=-1, keepdims=True) + EPSILON)


def normalize(values, gain):
    return values * row_scale(values) * gain


def skew_expand(offset_bias, length):
    count = offset_bias.shape[0]
    padded = jnp.pad(offset_bias, ((0, 0), (0, 1)))
    tiled = jnp.tile(padded, (1, length))[:, : length * (2 * length - 1)]
    return tiled.reshape(count, length, 2 * length - 1)[:, :, length - 1 :]


def diagonal_sums(grid, length):
    count = grid.shape[0]
    wide = jnp.pad(grid, ((0, 0), (0, 0), (length - 1, 0))).reshape(
        count, length * (2 * length - 1)
    )
    wide = jnp.pad(wide, ((0, 0), (0, length)))
    return jnp.sum(wide.reshape(count, length, 2 * length), axis=1)[:, : 2 * length - 1]


def bucket_onehot(offset_start, length, buckets, bucket_count):
    reach = (buckets.shape[0] + 1) // 2
    offsets = offset_start + jnp.arange(2 * length - 1, dtype=jnp.int32) - (length - 1)
    spots = jnp.clip(offsets, 1 - reach, reach - 1) + (reach - 1)
    table_spots = jnp.arange(buckets.shape[0], dtype=jnp.int32)
    chosen = jnp.sum(jnp.where(spots[:, None] == table_spots[None, :], buckets[None, :], 0), axis=1)
    return chosen[:, None] == jnp.arange(bucket_count, dtype=jnp.int32)[None, :]


def block_scores(query3, keys3, table, onehot, key_live, length):
    scores = jnp.einsum("ihd,jhd->hij", query3, keys3, preferred_element_type=jnp.float32)
    offset_bias = jnp.einsum(
        "ob,bh->ho", onehot.astype(jnp.bfloat16), table, preferred_element_type=jnp.float32
    )
    scores = scores + skew_expand(offset_bias, length)
    return jnp.where(key_live[None, None, :], scores, MASKED)


def body(
    tokens,
    lengths,
    buckets,
    attention_gain,
    query_weight,
    key_weight,
    value_weight,
    output_weight,
    bias_table,
    feed_gain,
    gate_weight,
    up_weight,
    down_weight,
    cotangent,
):
    (
        gain_first,
        query_full,
        key_full,
        value_full,
        output_full,
        table_full,
        gain_second,
        gate_full,
        up_full,
        down_full,
    ) = (
        lax.all_gather(attention_gain, "wsh", axis=0, tiled=True),
        lax.all_gather(query_weight, "wsh", axis=0, tiled=True),
        lax.all_gather(key_weight, "wsh", axis=0, tiled=True),
        lax.all_gather(value_weight, "wsh", axis=0, tiled=True),
        lax.all_gather(output_weight, "wsh", axis=1, tiled=True),
        lax.all_gather(bias_table, "wsh", axis=0, tiled=True),
        lax.all_gather(feed_gain, "wsh", axis=0, tiled=True),
        lax.all_gather(gate_weight, "wsh", axis=1, tiled=True),
        lax.all_gather(up_weight, "wsh", axis=1, tiled=True),
        lax.all_gather(down_weight, "wsh", axis=0, tiled=True),
    )
    length = tokens.shape[1]
    heads = table_full.shape[1]
    bucket_count = table_full.shape[0]
    inner = query_full.shape[1]
    head_size = inner // heads
    seq_count = lengths.shape[1]
    wide_count = lax.axis_size("ctx")
    span = wide_count // seq_count
    here = lax.axis_index("ctx")
    my_seq = here % seq_count
    my_block = here // seq_count
    seq_pick = jnp.arange(seq_count, dtype=jnp.int32) == my_seq
    my_length = jnp.sum(jnp.where(seq_pick, lengths[0], 0))
    positions = jnp.arange(length, dtype=jnp.int32)
    live = (my_block * length + positions < my_length).astype(jnp.float32)[:, None]
    inputs = tokens[0].astype(jnp.float32)
    gain_one = gain_first.astype(jnp.float32)
    first = normalize(inputs, gain_one).astype(jnp.bfloat16)
    query = jnp.dot(first, query_full, preferred_element_type=jnp.float32).astype(jnp.bfloat16)
    keys = jnp.dot(first, key_full, preferred_element_type=jnp.float32).astype(jnp.bfloat16)
    values = jnp.dot(first, value_full, preferred_element_type=jnp.float32).astype(jnp.bfloat16)
    query3 = query.reshape(length, heads, head_size)

    def forward_step(carry, block_keys, block_values, key_block):
        run_max, run_total, running = carry
        onehot = bucket_onehot((key_block - my_block) * length, length, buckets, bucket_count)
        key_live = key_block * length + positions < my_length
        scores = block_scores(
            query3,
            block_keys.reshape(length, heads, head_size),
            table_full,
            onehot,
            key_live,
            length,
        )
        new_max = jnp.maximum(run_max, jnp.max(scores, axis=2))
        weights = jnp.exp(scores - new_max[:, :, None])
        factor = jnp.exp(run_max - new_max)
        run_total = run_total * factor + jnp.sum(weights, axis=2)
        update = jnp.einsum(
            "hij,jhd->ihd",
            weights.astype(jnp.bfloat16),
            block_values.reshape(length, heads, head_size),
            preferred_element_type=jnp.float32,
        )
        running = running * jnp.transpose(factor)[:, :, None] + update
        return (new_max, run_total, running)

    start_carry = (
        jnp.full((heads, length), MASKED, jnp.float32),
        jnp.zeros((heads, length), jnp.float32),
        jnp.zeros((length, heads, head_size), jnp.float32),
    )
    start_carry = forward_step(start_carry, keys, values, my_block)
    stored = ()

    def cycle_turn(turn, state):
        carry, block_keys, block_values, stored_blocks = state
        block_keys, block_values = shifted((block_keys, block_values), "ctx", seq_count)
        carry = forward_step(carry, block_keys, block_values, (my_block - turn) % span)
        return (carry, block_keys, block_values, stored_blocks)

    (run_max, run_total, running), _, _, stored = lax.fori_loop(
        1, span, cycle_turn, (start_carry, keys, values, stored)
    )
    log_total = run_max + jnp.log(run_total)
    attention = (running / jnp.transpose(run_total)[:, :, None]).reshape(length, inner)
    attention_low = attention.astype(jnp.bfloat16)
    branch = jnp.dot(attention_low, output_full, preferred_element_type=jnp.float32)
    middle = inputs + live * branch
    gain_two = gain_second.astype(jnp.float32)
    second = normalize(middle, gain_two).astype(jnp.bfloat16)
    gate = jnp.dot(second, gate_full, preferred_element_type=jnp.float32)
    up = jnp.dot(second, up_full, preferred_element_type=jnp.float32)
    hidden = (jax.nn.gelu(gate, approximate=True) * up).astype(jnp.bfloat16)
    feed = jnp.dot(hidden, down_full, preferred_element_type=jnp.float32)
    result = (middle + live * feed).astype(jnp.bfloat16)
    outer = live * cotangent[0].astype(jnp.float32)
    outer_low = outer.astype(jnp.bfloat16)
    down_grad = jnp.einsum("tf,td->fd", hidden, outer_low, preferred_element_type=jnp.float32)
    hidden_grad = jnp.einsum("td,fd->tf", outer_low, down_full, preferred_element_type=jnp.float32)

    def gated(gate_in, up_in):
        return jax.nn.gelu(gate_in, approximate=True) * up_in

    _, gate_pull = jax.vjp(gated, gate, up)
    gate_back, up_back = gate_pull(hidden_grad)
    gate_low = gate_back.astype(jnp.bfloat16)
    up_low = up_back.astype(jnp.bfloat16)
    gate_grad = jnp.einsum("td,tf->df", second, gate_low, preferred_element_type=jnp.float32)
    up_grad = jnp.einsum("td,tf->df", second, up_low, preferred_element_type=jnp.float32)
    second_grad = jnp.einsum(
        "tf,df->td", gate_low, gate_full, preferred_element_type=jnp.float32
    ) + jnp.einsum("tf,df->td", up_low, up_full, preferred_element_type=jnp.float32)
    _, norm_pull = jax.vjp(normalize, middle, gain_two)
    middle_back, gain_two_grad = norm_pull(second_grad)
    middle_grad = outer + middle_back
    branch_low = (live * middle_grad).astype(jnp.bfloat16)
    output_grad = jnp.einsum(
        "ti,td->id", attention_low, branch_low, preferred_element_type=jnp.float32
    )
    attention_grad = jnp.einsum(
        "td,id->ti", branch_low, output_full, preferred_element_type=jnp.float32
    ).astype(jnp.bfloat16)
    attention_grad3 = attention_grad.reshape(length, heads, head_size)
    delta = jnp.transpose(
        jnp.sum(
            (attention_grad.astype(jnp.float32) * attention).reshape(length, heads, head_size),
            axis=2,
        )
    )

    def backward_step(block_keys, block_values, key_block):
        keys3 = block_keys.reshape(length, heads, head_size)
        values3 = block_values.reshape(length, heads, head_size)
        onehot = bucket_onehot((key_block - my_block) * length, length, buckets, bucket_count)
        key_live = key_block * length + positions < my_length
        scores = block_scores(query3, keys3, table_full, onehot, key_live, length)
        probs = jnp.exp(scores - log_total[:, :, None])
        prob_grad = jnp.einsum(
            "ihd,jhd->hij", attention_grad3, values3, preferred_element_type=jnp.float32
        )
        score_grad = (probs * (prob_grad - delta[:, :, None])).astype(jnp.bfloat16)
        part_query = jnp.einsum(
            "hij,jhd->ihd", score_grad, keys3, preferred_element_type=jnp.float32
        )
        part_keys = jnp.einsum(
            "hij,ihd->jhd", score_grad, query3, preferred_element_type=jnp.float32
        )
        part_values = jnp.einsum(
            "hij,ihd->jhd",
            probs.astype(jnp.bfloat16),
            attention_grad3,
            preferred_element_type=jnp.float32,
        )
        part_table = jnp.einsum(
            "ho,ob->bh",
            diagonal_sums(score_grad.astype(jnp.float32), length),
            onehot.astype(jnp.float32),
            precision=HIGH,
        )
        return (
            part_query.reshape(length, inner),
            part_keys.reshape(length, inner),
            part_values.reshape(length, inner),
            part_table,
        )

    def back_turn(turn, state):
        block_keys, block_values, keys_sum, values_sum, query_sum, table_sum = state
        part_query, part_keys, part_values, part_table = backward_step(
            block_keys, block_values, (my_block - turn) % span
        )
        keys_next = keys_sum + part_keys
        values_next = values_sum + part_values
        keys_sum, values_sum = (
            shifted(keys_next.astype(jnp.bfloat16), "ctx", seq_count).astype(keys_next.dtype),
            shifted(values_next.astype(jnp.bfloat16), "ctx", seq_count).astype(values_next.dtype),
        )
        block_keys, block_values = shifted((block_keys, block_values), "ctx", seq_count)
        return (
            block_keys,
            block_values,
            keys_sum,
            values_sum,
            query_sum + part_query,
            table_sum + part_table,
        )

    zeros_rows = jnp.zeros((length, inner), jnp.float32)
    back_state = (
        keys,
        values,
        zeros_rows,
        zeros_rows,
        zeros_rows,
        jnp.zeros((bucket_count, heads), jnp.float32),
    )
    _, _, keys_sum, values_sum, query_sum, table_grad = lax.fori_loop(
        0, span, back_turn, back_state
    )
    query_low = query_sum.astype(jnp.bfloat16)
    keys_low = keys_sum.astype(jnp.bfloat16)
    values_low = values_sum.astype(jnp.bfloat16)
    query_grad = jnp.einsum("td,ti->di", first, query_low, preferred_element_type=jnp.float32)
    key_grad = jnp.einsum("td,ti->di", first, keys_low, preferred_element_type=jnp.float32)
    value_grad = jnp.einsum("td,ti->di", first, values_low, preferred_element_type=jnp.float32)
    first_grad = (
        jnp.einsum("ti,di->td", query_low, query_full, preferred_element_type=jnp.float32)
        + jnp.einsum("ti,di->td", keys_low, key_full, preferred_element_type=jnp.float32)
        + jnp.einsum("ti,di->td", values_low, value_full, preferred_element_type=jnp.float32)
    )
    _, first_pull = jax.vjp(normalize, inputs, gain_one)
    inputs_back, gain_one_grad = first_pull(first_grad)
    input_gradient = (middle_grad + inputs_back).astype(jnp.bfloat16)
    small = lax.psum((gain_one_grad, table_grad, gain_two_grad), "ctx")
    wide = (
        lax.psum_scatter(query_grad, "ctx", scatter_dimension=1, tiled=True),
        lax.psum_scatter(key_grad, "ctx", scatter_dimension=1, tiled=True),
        lax.psum_scatter(value_grad, "ctx", scatter_dimension=1, tiled=True),
        lax.psum_scatter(output_grad, "ctx", scatter_dimension=0, tiled=True),
        lax.psum_scatter(gate_grad, "ctx", scatter_dimension=1, tiled=True),
        lax.psum_scatter(up_grad, "ctx", scatter_dimension=1, tiled=True),
        lax.psum_scatter(down_grad, "ctx", scatter_dimension=0, tiled=True),
    )
    final = (
        lax.psum_scatter(
            small[0].astype(jnp.bfloat16), "wsh", scatter_dimension=0, tiled=True
        ).astype(jnp.float32),
        lax.psum_scatter(
            small[1].astype(jnp.bfloat16), "wsh", scatter_dimension=0, tiled=True
        ).astype(jnp.float32),
        lax.psum_scatter(
            small[2].astype(jnp.bfloat16), "wsh", scatter_dimension=0, tiled=True
        ).astype(jnp.float32),
        lax.psum_scatter(
            wide[0].astype(jnp.bfloat16), "wsh", scatter_dimension=0, tiled=True
        ).astype(jnp.float32),
        lax.psum_scatter(
            wide[1].astype(jnp.bfloat16), "wsh", scatter_dimension=0, tiled=True
        ).astype(jnp.float32),
        lax.psum_scatter(
            wide[2].astype(jnp.bfloat16), "wsh", scatter_dimension=0, tiled=True
        ).astype(jnp.float32),
        lax.psum_scatter(
            wide[3].astype(jnp.bfloat16), "wsh", scatter_dimension=1, tiled=True
        ).astype(jnp.float32),
        lax.psum_scatter(
            wide[4].astype(jnp.bfloat16), "wsh", scatter_dimension=1, tiled=True
        ).astype(jnp.float32),
        lax.psum_scatter(
            wide[5].astype(jnp.bfloat16), "wsh", scatter_dimension=1, tiled=True
        ).astype(jnp.float32),
        lax.psum_scatter(
            wide[6].astype(jnp.bfloat16), "wsh", scatter_dimension=0, tiled=True
        ).astype(jnp.float32),
    )
    gain_one_out, table_out, gain_two_out = (final[0], final[1], final[2])
    query_out, key_out, value_out, output_out = (final[3], final[4], final[5], final[6])
    gate_out, up_out, down_out = (final[7], final[8], final[9])
    return (
        result[None],
        input_gradient[None],
        gain_one_out,
        query_out,
        key_out,
        value_out,
        output_out,
        table_out,
        gain_two_out,
        gate_out,
        up_out,
        down_out,
    )


BLOCK = 256
PAIR = 128
SPAN_ROW = 1024
CONTRACT_LAST = (((1,), (1,)), ((), ()))
AXES = ("ctx", "wsh")
GELU_SCALE = 0.7978845608028654
GELU_CUBE = 0.044715
LEFT_LANE, RIGHT_LANE, DEAD_LANE = 125, 126, 127
NEAR, BEFORE, AFTER = 0, 1, 2


SHARE = 0.01
RING_SHARE = 1.0
RINGED = ("attention_forward", "attention_query_grad")


def estimate(flops, bytes_accessed, transcendentals, share=SHARE):
    return pl.CostEstimate(
        flops=int(flops * share),
        bytes_accessed=int(bytes_accessed * share),
        transcendentals=int(transcendentals * share),
    )


def lanes(rows=BLOCK):
    return lax.broadcasted_iota(jnp.int32, (rows, PAIR), 1)


def only_head(block, second):
    lane = lanes(block.shape[0])
    keep = lane >= PAIR // 2 if second else lane < PAIR // 2
    return jnp.where(keep, block, jnp.zeros_like(block))


def pair_select(first, second):
    return jnp.where(lanes(first.shape[0]) < PAIR // 2, first, second)


def contract_last(left, right):
    return lax.dot_general(left, right, CONTRACT_LAST, preferred_element_type=jnp.float32)


def stack_heads(block):
    return jnp.concatenate([only_head(block, False), only_head(block, True)], axis=0)


def dead_rows(start, limit):
    row = lax.broadcasted_iota(jnp.int32, (BLOCK, PAIR), 0)
    return start + row >= limit


def other_aux(start, limit, kind):
    lane = lanes()
    value = jnp.where(jnp.logical_and(lane < 48, lane % 8 < 6), 1.0, 0.0)
    value = jnp.where(jnp.logical_and(lane == LEFT_LANE, kind == BEFORE), 1.0, value)
    value = jnp.where(jnp.logical_and(lane == RIGHT_LANE, kind == AFTER), 1.0, value)
    value = jnp.where(jnp.logical_and(lane == DEAD_LANE, dead_rows(start, limit)), MASKED, value)
    return value.astype(jnp.bfloat16)


def own_lanes(far_ref, head, heads):
    lane = lanes()
    value = jnp.where(lane == DEAD_LANE, 1.0, 0.0)
    value = jnp.where(lane == LEFT_LANE, far_ref[head], value)
    return jnp.where(lane == RIGHT_LANE, far_ref[heads + head], value)


def parts_of(value):
    first = value.astype(jnp.bfloat16).astype(jnp.float32)
    second = (value - first).astype(jnp.bfloat16).astype(jnp.float32)
    return first, second, value - first - second


def place_parts(base, value, lane_start):
    lane = lanes()
    for spot, part in enumerate(parts_of(value)):
        base = jnp.where(lane == lane_start + spot, part, base)
    return base


def kind_of(block, own):
    return jnp.where(block < own, BEFORE, AFTER)


def tiles_kernel(row_ref, tile_ref, turned_ref):
    row = row_ref[0]
    wide = pltpu.roll(
        jnp.broadcast_to(row, (BLOCK, SPAN_ROW)), SPAN_ROW - 255, 1, stride=1, stride_axis=0
    )
    for spot in range(3):
        tile = wide[:, spot * BLOCK : (spot + 1) * BLOCK]
        tile_ref[0, spot] = tile.astype(jnp.bfloat16)
        turned_ref[0, spot] = jnp.transpose(tile).astype(jnp.bfloat16)


def bias_tiles(offset_rows):
    heads = offset_rows.shape[0]
    shape = jax.ShapeDtypeStruct((heads, 3, BLOCK, BLOCK), jnp.bfloat16)
    spec = pl.BlockSpec((1, 3, BLOCK, BLOCK), lambda h: (h, 0, 0, 0))
    return pl.pallas_call(
        tiles_kernel,
        grid=(heads,),
        out_shape=(shape, shape),
        in_specs=[pl.BlockSpec((1, 1, SPAN_ROW), lambda h: (h, 0, 0))],
        out_specs=(spec, spec),
        name="bias_tiles",
    )(offset_rows[:, None, :])


def view_spec(row, lane_block):
    return pl.BlockSpec((BLOCK, PAIR), lambda p, i, f: (row, lane_block(p)))


def tile_spec():
    return pl.BlockSpec((2, 3, BLOCK, BLOCK), lambda p, i, f: (p, 0, 0, 0))


def run_pairs(kernel, info, far, operands, in_specs, out_shape, out_specs, work, name):
    pairs = 3
    return pl.pallas_call(
        kernel,
        grid_spec=pltpu.PrefetchScalarGridSpec(
            num_scalar_prefetch=2, grid=(pairs,), in_specs=in_specs, out_specs=out_specs
        ),
        out_shape=out_shape,
        cost_estimate=estimate(
            flops=2 * pairs * work * BLOCK * BLOCK * BLOCK,
            bytes_accessed=pairs * work * BLOCK * PAIR * 2,
            transcendentals=pairs * work * BLOCK * BLOCK,
            share=RING_SHARE if name in RINGED else SHARE,
        ),
        name=name,
    )(info, far, *operands)


def forward_kernel(at, nears, first, last, heads, info_ref, far_ref, *refs):
    refs = list(refs)
    count = len(nears)
    query_ref = refs.pop(0)
    key_refs, refs = refs[:count], refs[count:]
    value_refs, refs = refs[:count], refs[count:]
    tile_ref = refs.pop(0) if any(nears) else None
    pair = pl.program_id(0)
    own = info_ref[0]
    query = query_ref[...]
    if first:
        old_max = jnp.full((BLOCK, PAIR), MASKED, jnp.float32)
        total = None
    else:
        max_ref, total_ref = refs.pop(0), refs.pop(0)
        old_max, total = max_ref[...], total_ref[...]
    keys = []
    for spot in range(count):
        block, limit = info_ref[at + 2 * spot], info_ref[at + 1 + 2 * spot]
        kind = NEAR if nears[spot] else kind_of(block, own)
        keys.append(
            jnp.concatenate([key_refs[spot][...], other_aux(block * BLOCK, limit, kind)], axis=1)
        )
    tops, weights = [], []
    for head in range(2):
        aux = own_lanes(far_ref, 2 * pair + head, heads).astype(jnp.bfloat16)
        left = jnp.concatenate([only_head(query, head == 1), aux], axis=1)
        scores = []
        for spot in range(count):
            score = contract_last(left, keys[spot])
            if nears[spot]:
                place = jnp.clip(info_ref[at + 2 * spot] - own, -1, 1) + 1
                score = score + tile_ref[head, place].astype(jnp.float32)
            scores.append(score)
        top = functools.reduce(jnp.maximum, scores)
        lane = head * (PAIR // 2)
        top = jnp.maximum(old_max[:, lane : lane + 1], jnp.max(top, axis=1, keepdims=True))
        tops.append(top)
        weights.append([jnp.exp(score - top).astype(jnp.bfloat16) for score in scores])
    new_max = pair_select(tops[0], tops[1])
    ones = stack_heads(jnp.ones((BLOCK, PAIR), jnp.bfloat16))
    update = None
    for spot in range(count):
        right = jnp.concatenate([stack_heads(value_refs[spot][...]), ones], axis=1)
        left = jnp.concatenate([weights[0][spot], weights[1][spot]], axis=1)
        part = jnp.dot(left, right, preferred_element_type=jnp.float32)
        update = part if update is None else update + part
    if not first:
        factor = jnp.exp(old_max - new_max)
        update = update + total * jnp.concatenate([factor, factor], axis=1)
    if last:
        out_ref, low_ref, aux_ref = refs
        out = update[:, :PAIR] / update[:, PAIR:]
        out_ref[...] = out
        low_ref[...] = out.astype(jnp.bfloat16)
        log = -(new_max + jnp.log(update[:, PAIR:]))
        base = jnp.where(lanes() >= LEFT_LANE, 1.0, 0.0)
        base = jnp.where(pair == 0, base, aux_ref[...])
        for head in range(2):
            lane = head * (PAIR // 2)
            base = place_parts(base, log[:, lane : lane + 1], 8 * (2 * pair + head) + 3)
        aux_ref[...] = base
    else:
        max_out, total_out = refs
        max_out[...] = new_max
        total_out[...] = update


def forward_call(info, far, query, blocks, tiles, nears, state, last):
    count, first = len(blocks), state is None
    inner = query.shape[1]
    pairs = inner // PAIR
    in_specs = [view_spec(0, lambda p: p)]
    in_specs += [view_spec(row, lambda p: p) for _, row in blocks]
    in_specs += [view_spec(row, lambda p: p + pairs) for _, row in blocks]
    operands = [query] + [array for array, _ in blocks] * 2
    if any(nears):
        in_specs.append(tile_spec())
        operands.append(tiles)
    block = view_spec(0, lambda p: p)
    double = pl.BlockSpec((BLOCK, 2 * PAIR), lambda p, i, f: (0, p))
    if not first:
        in_specs += [block, double]
        operands += list(state)
    f32 = functools.partial(jax.ShapeDtypeStruct, dtype=jnp.float32)
    if last:
        out_shape = (
            f32((BLOCK, inner)),
            jax.ShapeDtypeStruct((BLOCK, inner), jnp.bfloat16),
            f32((BLOCK, PAIR)),
        )
        out_specs = (block, block, view_spec(0, lambda p: 0))
    else:
        out_shape = (f32((BLOCK, inner)), f32((BLOCK, 2 * inner)))
        out_specs = (block, double)
    kernel = functools.partial(forward_kernel, info[1], nears, first, last, 2 * pairs)
    return run_pairs(
        kernel, info[0], far, operands, in_specs, out_shape, out_specs, 6 * count, "attention_forward"
    )


def head_aux(aux, head, start):
    lane = lanes()
    keep = jnp.logical_and(lane // 8 == head, jnp.logical_and(lane % 8 >= start, lane % 8 < start + 3))
    return jnp.where(jnp.logical_and(keep, lane < 48), aux, 0.0)


def query_kernel(at, count, near, first, last, heads, info_ref, far_ref, *refs):
    refs = list(refs)
    query_ref, grad_ref, aux_ref = refs.pop(0), refs.pop(0), refs.pop(0)
    key_refs, refs = refs[:count], refs[count:]
    value_refs, refs = refs[:count], refs[count:]
    tile_ref = refs.pop(0) if near else None
    pair = pl.program_id(0)
    own = info_ref[0]
    query, grad = query_ref[...], grad_ref[...]
    aux = aux_ref[...].astype(jnp.float32)
    total = None if first else refs.pop(0)[...]
    lefts, grads = [], []
    for head in range(2):
        which = 2 * pair + head
        mine = own_lanes(far_ref, which, heads) + head_aux(aux, which, 3)
        lefts.append(jnp.concatenate([only_head(query, head == 1), mine.astype(jnp.bfloat16)], axis=1))
        delta = head_aux(aux, which, 0).astype(jnp.bfloat16)
        grads.append(jnp.concatenate([only_head(grad, head == 1), delta], axis=1))
    if near:
        diag_ref = refs.pop()
        strips = [[jnp.zeros((BLOCK, BLOCK), jnp.float32)] * 3 for _ in range(2)]
    lane = lanes()
    for spot in range(count):
        block, limit = info_ref[at + 2 * spot], info_ref[at + 1 + 2 * spot]
        kind = NEAR if near else kind_of(block, own)
        key, value = key_refs[spot][...], value_refs[spot][...]
        side = other_aux(block * BLOCK, limit, kind)
        wide_key = jnp.concatenate([key, side], axis=1)
        wide_value = jnp.concatenate([value, jnp.where(lane < 48, side, jnp.zeros_like(side))], axis=1)
        place = jnp.clip(block - own, -1, 1) + 1
        pieces, counts = [], []
        for head in range(2):
            scores = contract_last(lefts[head], wide_key)
            if near:
                scores = scores + tile_ref[head, place].astype(jnp.float32)
            score_grad = jnp.exp(scores) * contract_last(grads[head], wide_value)
            if near:
                strips[head] = [
                    strip + jnp.where(place == spot_of, score_grad, 0.0)
                    for spot_of, strip in enumerate(strips[head])
                ]
            pieces.append(score_grad.astype(jnp.bfloat16))
            counts.append(jnp.where(lane == 4 * head + kind, 1.0, 0.0).astype(jnp.bfloat16))
        right = jnp.concatenate([stack_heads(key), jnp.concatenate(counts, axis=0)], axis=1)
        part = jnp.dot(jnp.concatenate(pieces, axis=1), right, preferred_element_type=jnp.float32)
        total = part if total is None else total + part
    if near:
        rows = []
        for head in range(2):
            wide = jnp.concatenate(strips[head] + [jnp.zeros((BLOCK, BLOCK), jnp.float32)], axis=1)
            eight = None
            for group in range(BLOCK // 8):
                turned = pltpu.roll(wide[8 * group : 8 * group + 8], (255 - 8 * group) % SPAN_ROW, 1)
                eight = turned if eight is None else eight + turned
            line = None
            for row in range(8):
                turned = pltpu.roll(eight, (SPAN_ROW - row) % SPAN_ROW, 1)[row : row + 1]
                line = turned if line is None else line + turned
            rows.append(line)
        diag_ref[0] = jnp.concatenate(rows + [jnp.zeros((6, SPAN_ROW), jnp.float32)], axis=0)
    if last:
        low_ref, sum_ref = refs
        low_ref[...] = total[:, :PAIR].astype(jnp.bfloat16)
        sum_ref[0] = jnp.broadcast_to(jnp.sum(total[:, PAIR:], axis=0, keepdims=True), (8, PAIR))
    else:
        (total_ref,) = refs
        total_ref[...] = total


def query_call(info, far, query, grads, blocks, tiles, state, last):
    count, near, first = len(blocks), tiles is not None, state is None
    inner = query.shape[1]
    pairs = inner // PAIR
    own = view_spec(0, lambda p: p)
    in_specs = [own, own, view_spec(0, lambda p: pairs)]
    in_specs += [view_spec(row, lambda p: p) for _, row in blocks]
    in_specs += [view_spec(row, lambda p: p + pairs) for _, row in blocks]
    operands = [query, grads, grads] + [array for array, _ in blocks] * 2
    if near:
        in_specs.append(tile_spec())
        operands.append(tiles)
    double = pl.BlockSpec((BLOCK, 2 * PAIR), lambda p, i, f: (0, p))
    if not first:
        in_specs.append(double)
        operands.append(state)
    f32 = functools.partial(jax.ShapeDtypeStruct, dtype=jnp.float32)
    if last:
        out_shape = [jax.ShapeDtypeStruct((BLOCK, inner), jnp.bfloat16), f32((pairs, 8, PAIR))]
        out_specs = [own, pl.BlockSpec((1, 8, PAIR), lambda p, i, f: (p, 0, 0))]
    else:
        out_shape, out_specs = [f32((BLOCK, 2 * inner))], [double]
    if near:
        out_shape.append(f32((pairs, 8, SPAN_ROW)))
        out_specs.append(pl.BlockSpec((1, 8, SPAN_ROW), lambda p, i, f: (p, 0, 0)))
    kernel = functools.partial(query_kernel, info[1], count, near, first, last, 2 * pairs)
    return run_pairs(
        kernel, info[0], far, operands, in_specs, out_shape, out_specs, 8 * count, "attention_query_grad"
    )


def key_kernel(at, count, near, first, last, heads, info_ref, far_ref, *refs):
    refs = list(refs)
    key_ref, value_ref = refs.pop(0), refs.pop(0)
    query_refs, refs = refs[:count], refs[count:]
    grad_refs, refs = refs[:count], refs[count:]
    aux_refs, refs = refs[:count], refs[count:]
    tile_ref = refs.pop(0) if near else None
    pair = pl.program_id(0)
    own = info_ref[0]
    key, value = key_ref[...], value_ref[...]
    key_sum = value_sum = None
    if not first:
        key_sum, value_sum = refs.pop(0)[...], refs.pop(0)[...]
    key_out, value_out = refs
    lane = lanes()
    keys = [only_head(key, False), only_head(key, True)]
    values = []
    for head in range(2):
        pick = jnp.logical_and(lane // 8 == 2 * pair + head, lane % 8 < 3)
        values.append(
            jnp.concatenate([only_head(value, head == 1), jnp.where(pick, 1.0, 0.0).astype(jnp.bfloat16)], axis=1)
        )
    for spot in range(count):
        block, limit = info_ref[at + 2 * spot], info_ref[at + 1 + 2 * spot]
        kind = NEAR if near else kind_of(own, block)
        query, grad, aux = query_refs[spot][...], grad_refs[spot][...], aux_refs[spot][...]
        wide_query = jnp.concatenate([query, aux], axis=1)
        wide_grad = jnp.concatenate([grad, aux], axis=1)
        place = jnp.clip(own - block, -1, 1) + 1
        dead = jnp.logical_and(lane == DEAD_LANE, dead_rows(own * BLOCK, limit))
        probs_low, slopes_low = [], []
        for head in range(2):
            which = 2 * pair + head
            pick = jnp.logical_and(lane // 8 == which, jnp.logical_and(lane % 8 >= 3, lane % 8 < 6))
            side = jnp.where(pick, 1.0, 0.0)
            if not near:
                constant = jnp.where(kind == BEFORE, far_ref[which], far_ref[heads + which])
                side = jnp.where(lane == RIGHT_LANE, constant, side)
            side = jnp.where(dead, MASKED, side).astype(jnp.bfloat16)
            scores = contract_last(jnp.concatenate([keys[head], side], axis=1), wide_query)
            if near:
                scores = scores + tile_ref[head, place].astype(jnp.float32)
            probs = jnp.exp(scores)
            slopes = probs * contract_last(values[head], wide_grad)
            probs_low.append(probs.astype(jnp.bfloat16))
            slopes_low.append(slopes.astype(jnp.bfloat16))
        part_value = jnp.dot(
            jnp.concatenate(probs_low, axis=1), stack_heads(grad), preferred_element_type=jnp.float32
        )
        part_key = jnp.dot(
            jnp.concatenate(slopes_low, axis=1), stack_heads(query), preferred_element_type=jnp.float32
        )
        key_sum = part_key if key_sum is None else key_sum + part_key
        value_sum = part_value if value_sum is None else value_sum + part_value
    key_out[...] = key_sum.astype(key_out.dtype)
    value_out[...] = value_sum.astype(value_out.dtype)


def key_call(info, far, joined, queries, grads, turned, state, last):
    count, near, first = len(queries), turned is not None, state is None
    inner = joined.shape[1] // 2
    pairs = inner // PAIR
    own = view_spec(0, lambda p: p)
    in_specs = [own, view_spec(0, lambda p: p + pairs)]
    in_specs += [view_spec(row, lambda p: p) for _, row in queries]
    in_specs += [view_spec(row, lambda p: p) for _, row in grads]
    in_specs += [view_spec(row, lambda p: pairs) for _, row in grads]
    arrays = [array for array, _ in grads]
    operands = [joined, joined] + [array for array, _ in queries] + arrays + arrays
    if near:
        in_specs.append(tile_spec())
        operands.append(turned)
    if not first:
        in_specs += [own, own]
        operands += list(state)
    shape = jax.ShapeDtypeStruct((BLOCK, inner), jnp.bfloat16 if last else jnp.float32)
    kernel = functools.partial(key_kernel, info[1], count, near, first, last, 2 * pairs)
    return run_pairs(
        kernel, info[0], far, operands, in_specs, (shape, shape), (own, own), 10 * count, "attention_key_grad"
    )


def grads_kernel(first_ref, second_ref, third_ref, out_ref, aux_ref, grad_ref):
    total = first_ref[...] + second_ref[...].astype(jnp.float32) + third_ref[...]
    low = total.astype(jnp.bfloat16)
    inner = low.shape[1]
    grad_ref[:, :inner] = low
    product = low.astype(jnp.float32) * out_ref[...]
    base = aux_ref[...]
    for pair in range(inner // PAIR):
        piece = product[:, pair * PAIR : (pair + 1) * PAIR]
        for head in range(2):
            delta = -jnp.sum(only_head(piece, head == 1), axis=1, keepdims=True)
            base = place_parts(base, delta, 8 * (2 * pair + head))
    grad_ref[:, inner:] = base.astype(jnp.bfloat16)


def finish_grads(first, second, third, out, aux):
    return pl.pallas_call(
        grads_kernel,
        out_shape=jax.ShapeDtypeStruct((BLOCK, out.shape[1] + PAIR), jnp.bfloat16),
        name="attention_out_grad",
    )(first, second, third, out, aux)

def feed_kernel(spot_ref, *refs):
    token_refs, cot_refs, mixed_refs = refs[:4], refs[4:8], refs[8:12]
    gain_ref, out_w_ref, gate_w_ref, up_w_ref, down_w_ref = refs[12:17]
    (
        second_ref,
        hidden_ref,
        gate_ref,
        up_ref,
        outer_ref,
        rows_ref,
        kept_ref,
        passed_ref,
        sent_ref,
        grad_kept_ref,
        grad_sent_ref,
        gain_sum_ref,
    ) = refs[17:29]
    token_all, cot_all, mixed_all, live_all = refs[29:]
    f32, bf16 = jnp.float32, jnp.bfloat16
    step = pl.program_id(0)
    gain = gain_ref[...]
    width = gain.shape[1]
    row = lax.broadcasted_iota(jnp.int32, (BLOCK, 1), 0)

    def load(which):
        for spot in range(2):
            at = slice(spot * BLOCK, (spot + 1) * BLOCK)
            token_all[at, :] = token_refs[2 * which + spot][:, :width]
            cot_all[at, :] = cot_refs[2 * which + spot][:, :width]
            mixed_all[at, :] = mixed_refs[2 * which + spot][...]
            block = spot_ref[1] if which == 0 else spot_ref[1] ^ 1
            alive = block * BLOCK + row < spot_ref[2 + spot]
            live_all[at, :] = jnp.broadcast_to(jnp.where(alive, 1.0, 0.0), (BLOCK, PAIR))

    @pl.when(step == 0)
    def _():
        load(0)

    @pl.when(step > 0)
    def _():
        load(1)

    live = live_all[:, 0:1]
    branch = contract_last(mixed_all[...], out_w_ref[...])
    rows = token_all[...].astype(f32) + live * branch
    scale = lax.rsqrt(jnp.mean(rows * rows, axis=-1, keepdims=True) + EPSILON)
    unit = rows * scale
    second = (unit * gain).astype(bf16)
    second_ref[...] = second
    outer = (cot_all[...].astype(f32) * live).astype(bf16)
    outer_ref[...] = outer
    count = gate_w_ref.shape[1]
    for start in range(0, count, 256):
        at = slice(start, min(start + 256, count))
        gate = jnp.dot(second, gate_w_ref[:, at], preferred_element_type=f32)
        up = jnp.dot(second, up_w_ref[:, at], preferred_element_type=f32)
        back = jnp.dot(outer, down_w_ref[:, at], preferred_element_type=f32)
        square = gate * gate
        bend = jnp.tanh(GELU_SCALE * gate * (1.0 + GELU_CUBE * square))
        curve = 0.5 * gate * (1.0 + bend)
        hidden_ref[:, at] = (curve * up).astype(bf16)
        rise = 0.5 * (1.0 + bend) + 0.5 * GELU_SCALE * gate * (1.0 - bend * bend) * (
            1.0 + 3.0 * GELU_CUBE * square
        )
        gate_ref[:, at] = (back * up * rise).astype(bf16)
        up_ref[:, at] = (back * curve).astype(bf16)
    second_grad = contract_last(gate_ref[...], gate_w_ref[...]) + contract_last(up_ref[...], up_w_ref[...])
    line = jnp.sum(second_grad * unit, axis=0, keepdims=True)

    @pl.when(step == 0)
    def _():
        gain_sum_ref[...] = line
        rows_ref[...] = rows[:BLOCK]

    @pl.when(step > 0)
    def _():
        gain_sum_ref[...] += line

    scaled = second_grad * gain
    middle = live * scale * (scaled - unit * jnp.mean(scaled * unit, axis=-1, keepdims=True))
    middle = middle.astype(bf16)
    grad = jnp.dot(middle, out_w_ref[...], preferred_element_type=f32).astype(bf16)
    feed = contract_last(hidden_ref[...], down_w_ref[...]).astype(bf16)

    @pl.when(step == 0)
    def _():
        kept_ref[0], kept_ref[1] = feed[:BLOCK], middle[:BLOCK]
        passed_ref[...] = jnp.zeros_like(passed_ref)
        passed_ref[0, :, :width], passed_ref[1, :, :width] = feed[BLOCK:], middle[BLOCK:]
        grad_kept_ref[...] = grad

    @pl.when(step > 0)
    def _():
        sent_ref[...] = jnp.zeros_like(sent_ref)
        sent_ref[0, :, :width], sent_ref[1, :, :width] = feed, middle
        grad_sent_ref[...] = grad


def feed_call(spots, tokens, cots, mixed, gain, out_w, gate_w, up_w, down_w):
    f32, bf16 = jnp.float32, jnp.bfloat16
    width, inner = out_w.shape
    wide = tokens[0][0].shape[1]
    units = gate_w.shape[1] // 2
    step, total = 2 * BLOCK, 4 * BLOCK
    once = pl.Buffered(1)

    def rows_of(row, lanes_of):
        return pl.BlockSpec((BLOCK, lanes_of), lambda s, i: (row, 0), pipeline_mode=once)

    def moving(lanes_of):
        return pl.BlockSpec((step, lanes_of), lambda s, i: (s, 0))

    def fixed(*shape):
        return pl.BlockSpec(shape, lambda s, i: (0,) * len(shape), pipeline_mode=once)

    shape = jax.ShapeDtypeStruct
    in_specs = [rows_of(row, array.shape[1]) for array, row in (*tokens, *cots, *mixed)]
    in_specs += [
        fixed(1, width),
        fixed(*out_w.shape),
        pl.BlockSpec((width, units), lambda s, i: (0, i[0]), pipeline_mode=once),
        pl.BlockSpec((width, units), lambda s, i: (0, i[0]), pipeline_mode=once),
        pl.BlockSpec((width, units), lambda s, i: (0, i[0]), pipeline_mode=once),
    ]
    return pl.pallas_call(
        feed_kernel,
        grid_spec=pltpu.PrefetchScalarGridSpec(
            num_scalar_prefetch=1,
            grid=(2,),
            in_specs=in_specs,
            out_specs=(
                moving(width),
                moving(units),
                moving(units),
                moving(units),
                moving(width),
                fixed(BLOCK, width),
                fixed(2, BLOCK, width),
                fixed(2, BLOCK, wide),
                fixed(2, step, wide),
                fixed(step, inner),
                fixed(step, inner),
                fixed(1, width),
            ),
            scratch_shapes=[
                pltpu.VMEM((step, width), bf16),
                pltpu.VMEM((step, width), bf16),
                pltpu.VMEM((step, inner), bf16),
                pltpu.VMEM((step, PAIR), f32),
            ],
        ),
        out_shape=(
            shape((total, width), bf16),
            shape((total, units), bf16),
            shape((total, units), bf16),
            shape((total, units), bf16),
            shape((total, width), bf16),
            shape((BLOCK, width), f32),
            shape((2, BLOCK, width), bf16),
            shape((2, BLOCK, wide), bf16),
            shape((2, step, wide), bf16),
            shape((step, inner), bf16),
            shape((step, inner), bf16),
            shape((1, width), f32),
        ),
        compiler_params=pltpu.CompilerParams(vmem_limit_bytes=63_000_000),
        cost_estimate=estimate(
            flops=2 * total * width * (6 * units + 2 * inner),
            bytes_accessed=2 * (3 * width * units + 8 * total * width),
            transcendentals=total * units,
        ),
        name="feed_forward",
    )(spots, *[array for array, _ in (*tokens, *cots, *mixed)], gain, out_w, gate_w, up_w, down_w)


def weight_kernel(spot_ref, left_ref, right_ref, kept_ref, apart_ref, here_ref, product_ref):
    y, core, side = spot_ref[0], spot_ref[1], spot_ref[2]
    use = kept_ref.shape[2]
    product_ref[...] = lax.dot_general(
        left_ref[...], right_ref[...], (((0,), (0,)), ((), ())), preferred_element_type=jnp.float32
    )

    def block_of(y_bit, apart_x, apart_k):
        k_bit = core if apart_k == 0 else 1 - core
        x_bit = side if apart_x == 0 else 1 - side
        block = y_bit * 4 + k_bit * 2 + x_bit
        return product_ref[pl.ds(pl.multiple_of(block * use, 16), use), :].astype(jnp.bfloat16)

    for apart_k in range(2):
        for apart_x in range(2):
            kept_ref[apart_x, apart_k] = block_of(y, apart_x, apart_k)
        apart_ref[apart_k] = block_of(1 - y, 1, apart_k)
        here_ref[apart_k] = block_of(1 - y, 0, apart_k)


def weight_call(spots, left, right):
    width = right.shape[1]
    use = left.shape[1] // 8
    whole = jax.ShapeDtypeStruct((2, 2, use, width), jnp.bfloat16)
    part = jax.ShapeDtypeStruct((2, use, width), jnp.bfloat16)
    part_spec = pl.BlockSpec(part.shape, lambda s, i: (0, 0, 0))
    return pl.pallas_call(
        weight_kernel,
        grid_spec=pltpu.PrefetchScalarGridSpec(
            num_scalar_prefetch=1,
            grid=(1,),
            in_specs=[
                pl.BlockSpec(left.shape, lambda s, i: (0, 0)),
                pl.BlockSpec(right.shape, lambda s, i: (0, 0)),
            ],
            out_specs=(pl.BlockSpec(whole.shape, lambda s, i: (0, 0, 0, 0)), part_spec, part_spec),
            scratch_shapes=[pltpu.VMEM((left.shape[1], width), jnp.float32)],
        ),
        out_shape=(whole, part, part),
        compiler_params=pltpu.CompilerParams(vmem_limit_bytes=60_000_000),
        cost_estimate=estimate(
            flops=2 * left.shape[0] * left.shape[1] * width,
            bytes_accessed=2 * (left.size + right.size + 8 * use * width),
            transcendentals=0,
        ),
        name="feed_weight_grad",
    )(spots, left, right)


def projection_kernel(spot_ref, query_ref, key_ref, value_ref, mixed_ref, first_kept_ref, first_sent_ref, branch_kept_ref, branch_sent_ref, kept_ref, sent_ref):
    core, y, z_high, z_low = spot_ref[0], spot_ref[1], spot_ref[2], spot_ref[3]
    inner = query_ref.shape[1]
    columns = inner // 16
    size = inner // 2
    for out_ref, k_bit in ((kept_ref, core), (sent_ref, 1 - core)):
        target = lax.broadcasted_iota(jnp.int32, (inner, size), 1)
        group, inside = target // columns, target % columns
        z_bits = ((group // 2) % 2) ^ z_high, (group % 2) ^ z_low
        source = (((z_bits[0] * 2 + z_bits[1]) * 2 + ((group // 4) ^ y)) * 2 + k_bit) * columns + inside
        chooser = jnp.where(lax.broadcasted_iota(jnp.int32, (inner, size), 0) == source, 1.0, 0.0).astype(jnp.bfloat16)
        for spot, ref in enumerate((query_ref, key_ref, value_ref, mixed_ref)):
            picked = jnp.dot(ref[...], chooser, preferred_element_type=jnp.float32).astype(jnp.bfloat16)
            rights = (branch_kept_ref, branch_sent_ref) if spot == 3 else (first_kept_ref, first_sent_ref)
            for lane_half, right in enumerate(rights):
                out_ref[lane_half * 4 + spot] = lax.dot_general(
                    picked, right[...], (((0,), (0,)), ((), ())), preferred_element_type=jnp.float32
                ).astype(jnp.bfloat16)


def projection_call(spots, query, keys, values, mixed, first_lanes, branch_lanes):
    shape = jax.ShapeDtypeStruct((8, query.shape[1] // 2, first_lanes[0].shape[1]), jnp.bfloat16)
    operands = [query, keys, values, mixed, *first_lanes, *branch_lanes]
    return pl.pallas_call(
        projection_kernel,
        grid_spec=pltpu.PrefetchScalarGridSpec(
            num_scalar_prefetch=1,
            grid=(1,),
            in_specs=[pl.BlockSpec(a.shape, lambda s, i: (0, 0)) for a in operands],
            out_specs=[pl.BlockSpec(shape.shape, lambda s, i: (0, 0, 0))] * 2,
        ),
        out_shape=[shape, shape],
        cost_estimate=estimate(
            flops=2 * 4 * query.size * 2 * first_lanes[0].shape[1], bytes_accessed=8 * 2 * query.size, transcendentals=0
        ),
        name="projection_weight_grad",
    )(spots, *operands)


def grouped_body(
    tokens,
    lengths,
    buckets,
    attention_gain,
    query_weight,
    key_weight,
    value_weight,
    output_weight,
    bias_table,
    feed_gain,
    gate_weight,
    up_weight,
    down_weight,
    cotangent,
):
    bf16, f32 = jnp.bfloat16, jnp.float32
    places = lax.axis_size("ctx")
    chips = places // 2
    rows_of_chips = chips // 2
    here = lax.axis_index("ctx")
    side = lax.axis_index("wsh")
    core = here % 2
    chip = here // 2
    lane_y = chip % 2
    lane_z = chip // 2
    length = tokens.shape[1]
    half = tokens.shape[2] // 2
    heads = bias_table.shape[1]
    inner = query_weight.shape[1]
    nowhere = -(1 << 20)

    def spread(block, route):
        return lax.ppermute(block, AXES, route)

    def route_of(move):
        pairs = []
        for c in range(places):
            for w in range(2):
                target = move(c // 4, (c // 2) % 2, c % 2, w)
                if target is not None:
                    z, y, k, x = target
                    pairs.append((c * 2 + w, (((z * 2 + y) * 2) + k) * 2 + x))
        return pairs

    route_core = route_of(lambda z, y, k, x: (z, y, 1 - k, x))
    route_x = route_of(lambda z, y, k, x: (z, y, k, 1 - x))
    route_y = route_of(lambda z, y, k, x: (z, 1 - y, k, x))
    route_far = route_of(lambda z, y, k, x: (z ^ 2, y, k, x))
    route_near = route_of(lambda z, y, k, x: (z ^ 1, y, k, x))
    order = [(i, 0) for i in range(rows_of_chips)] + [
        (rows_of_chips - 1 - i, 1) for i in range(rows_of_chips)
    ]
    place = {spot: i for i, spot in enumerate(order)}
    route_ring = route_of(
        lambda z, y, k, x: (*order[(place[(z, y)] + 1 - 2 * k) % chips], k, x)
    )
    route_next = [
        ((c * 2 + w), (c + (1 if c % 2 else -1)) * 2 + w)
        for c in range(places)
        for w in range(2)
        if 0 <= c + (1 if c % 2 else -1) < places
    ]
    my_place = jnp.where(lane_y == 0, lane_z, 2 * rows_of_chips - 1 - lane_z)
    toward = jnp.where(core == 0, -1, 1)
    next_block = here - 1 + 2 * core
    has_next = jnp.logical_and(next_block >= 0, next_block < places)

    def chip_at(spot):
        spot = (spot + 2 * chips) % chips
        return jnp.where(
            spot < rows_of_chips, 2 * spot, 2 * (2 * rows_of_chips - 1 - spot) + 1
        )

    def swap_core(block):
        return spread(block, route_core)

    def swap_x(block):
        return spread(block, route_x)

    def both_sides(mine, other, axis):
        return jnp.where(
            side == 0,
            jnp.concatenate([mine, other], axis=axis),
            jnp.concatenate([other, mine], axis=axis),
        )

    def after(block, *others):
        return lax.optimization_barrier((block, *others))[0]

    live_count = jnp.minimum(lengths[0, 0], places * length)
    middle = chips // 2
    width = tokens.shape[2]

    def blocks_at(step):
        ahead = chip_at(my_place + toward * step)
        if step == middle:
            return [ahead * 2 + core, ahead * 2 + 1 - core]
        behind = chip_at(my_place - toward * step)
        return [ahead * 2 + core, ahead * 2 + 1 - core, behind * 2 + 1 - core, behind * 2 + core]

    def info_of(blocks, near):
        entries = []
        for block in blocks:
            limit = live_count
            if near:
                limit = jnp.where(jnp.logical_or(block != next_block, has_next), limit, nowhere)
            else:
                limit = jnp.where(block == next_block, nowhere, limit)
            entries += [block, limit]
        return entries

    marks = []

    def then(*blocks):
        if not marks:
            return blocks if len(blocks) > 1 else blocks[0]
        held = lax.optimization_barrier((*blocks, *marks))[: len(blocks)]
        return held if len(blocks) > 1 else held[0]

    def mark(*blocks):
        marks[:] = blocks

    def add_low(left, right):
        return (left.astype(f32) + right.astype(f32)).astype(bf16)

    quarter = half // 2

    def my_rows(block, which, count):
        return lax.dynamic_slice_in_dim(block, which * count, count, 0)

    def plain(block):
        return with_layout_constraint(block, Layout(tuple(range(block.ndim))))

    small = jnp.concatenate(
        [
            attention_gain,
            feed_gain,
            bias_table.reshape(-1),
            jnp.stack([live_count // 128, live_count % 128]).astype(bf16),
        ]
    )
    size_small = small.shape[0]
    small = jnp.pad(small, (0, -size_small % 2048)).reshape(-1, 128)
    small_other = swap_x(small).reshape(-1)
    projections = [key_weight, value_weight, query_weight]
    sent_rows = jnp.concatenate([my_rows(w, core, quarter) for w in projections], axis=1)
    sent_rows = after(sent_rows, small)
    part = swap_x(sent_rows)
    lanes_left = -width % PAIR

    def padded(block):
        return jnp.pad(block, ((0, 0), (0, lanes_left)))

    mine, cot = plain(padded(tokens[0])), plain(padded(cotangent[0]))
    tokens_core = swap_core(after(mine, sent_rows))
    output_turned = jnp.transpose(output_weight)
    gain_other = small_other[:half]
    feed_other = small_other[half : 2 * half]
    table_other = small_other[2 * half : size_small - 2].reshape(bias_table.shape)
    counts = small_other[size_small - 2 : size_small].astype(f32).astype(jnp.int32)
    count_other = counts[0] * 128 + counts[1]
    gain_one = both_sides(attention_gain, gain_other, 0).astype(f32)
    gain_two = both_sides(feed_gain, feed_other, 0).astype(f32)
    table = both_sides(bias_table, table_other, 0)
    bucket_count = table.shape[0]
    reach = (buckets.shape[0] + 1) // 2
    offsets = jnp.clip(jnp.arange(SPAN_ROW, dtype=jnp.int32) - 511, 1 - reach, reach - 1) + (reach - 1)
    spots = jnp.arange(buckets.shape[0], dtype=jnp.int32)
    chosen = jnp.sum(jnp.where(offsets[:, None] == spots[None, :], buckets[None, :], 0), axis=1)
    onehot = (chosen[:, None] == jnp.arange(bucket_count, dtype=jnp.int32)[None, :]).astype(f32)
    offset_rows = lax.dot_general(
        table.astype(f32), onehot, (((0,), (1,)), ((), ())), precision=HIGH, preferred_element_type=f32
    )
    tiles, turned = bias_tiles(offset_rows)
    far = jnp.concatenate([offset_rows[:, 0], offset_rows[:, SPAN_ROW - 2]])
    entries = [here] + info_of([here, here ^ 1, next_block], True)
    near_info, far_info = 1, []
    for step in range(1, middle + 1):
        far_info.append(len(entries))
        entries += info_of(blocks_at(step), False)
    entries += info_of([next_block], True)
    infos = jnp.stack(entries).astype(jnp.int32)

    inputs = mine[:, :width].astype(f32)
    scale_one = row_scale(inputs)
    first = (inputs * scale_one * gain_one).astype(bf16)
    partner_inputs = tokens_core[:, :width].astype(f32)
    first_partner = (partner_inputs * row_scale(partner_inputs) * gain_one).astype(bf16)
    first_pair = jnp.concatenate([first, first_partner], axis=0)

    def lanes_of(block):
        low_half, high_half = block[:, :half], block[:, half:]
        return (
            jnp.where(side == 0, low_half, high_half),
            jnp.where(side == 0, high_half, low_half),
        )

    pair_lanes = lanes_of(first_pair)
    first_lanes = [block[:length] for block in pair_lanes]
    weight_mine = jnp.concatenate(projections, axis=1)
    projected = jnp.dot(pair_lanes[0], weight_mine, preferred_element_type=f32)
    held = lax.optimization_barrier((part, tiles, turned, far, infos, projected, pair_lanes[1], weight_mine))
    part, tiles, turned, far, infos, projected, lanes_other, weight_mine = held
    traded = swap_core(part)
    out_part = swap_x(after(my_rows(output_turned, core, quarter), part))
    tokens_side = swap_x(after(mine, out_part))
    cot_side = swap_x(after(cot, out_part))

    def join_rows(part, traded):
        return jnp.where(
            core == 0,
            jnp.concatenate([part, traded], axis=0),
            jnp.concatenate([traded, part], axis=0),
        )

    weight_other = join_rows(part, traded)
    projected = (projected + jnp.dot(lanes_other, weight_other, preferred_element_type=f32)).astype(bf16)
    chunk, query_chunk = projected[:, : 2 * inner], projected[:, 2 * inner :]
    joined, query = chunk, query_chunk

    def start_ring(block):
        return jnp.concatenate([block, swap_core(block)], axis=0)

    def next_chunk(chunk, step):
        if step == middle:
            return spread(chunk[:length], route_ring)
        return spread(chunk, route_ring)

    def views(chunk):
        return [(chunk, row) for row in range(chunk.shape[0] // length)]

    received = next_chunk(chunk, 1)
    query_first = query_chunk
    query_received = next_chunk(query_chunk, 1)
    next_joined = spread(chunk[:length], route_next)
    query_next = spread(query_chunk[:length], route_next)
    near_views = views(chunk) + [(next_joined, 0)]
    state = forward_call((infos, near_info), far, query, near_views[:2], tiles, (True, True), None, False)
    far_views, query_views = [], []
    for step in range(1, middle + 1):
        received, _ = lax.optimization_barrier((received, state))
        following = next_chunk(received, step + 1) if step < middle else None
        partner = swap_core(received)
        now = views(received) + views(partner)
        far_views.append(now)
        if step > 1:
            query_partner = swap_core(query_received)
            query_views.append(views(query_received) + views(query_partner))
            forced = (query_received, query_partner)
            query_received = next_chunk(query_received, step)
            state = lax.optimization_barrier((*state, *forced))[:2]
        if step == 1:
            out_traded = swap_core(after(out_part, chunk))
            output_full = both_sides(output_turned, join_rows(out_part, out_traded), 0)
            state = lax.optimization_barrier((*state, output_full))
            output_full, state = state[2], state[:2]
        if step == 2:
            cot_core = swap_core(after(cot, state))
            positions = here * length + jnp.arange(length, dtype=jnp.int32)
            live_own = (positions < live_count).astype(f32)[:, None]
            outer_own = cot[:, :width].astype(f32) * live_own
            grad_own = jnp.einsum(
                "td,di->ti", outer_own.astype(bf16), output_full, preferred_element_type=f32
            )
            tokens_side = after(tokens_side, *state)
            tokens_both = swap_core(tokens_side)
            state = lax.optimization_barrier((*state, grad_own, cot_core, tokens_both))
            grad_own, cot_core, tokens_both, state = state[2], state[3], state[4], state[:2]
        if step == 3:
            cot_side = after(cot_side, *state)
            cot_both = swap_core(cot_side)
            state = lax.optimization_barrier((*state, cot_both))
            cot_both, state = state[2], state[:2]
        if step == middle:
            blocks, nears = now + [near_views[2]], (False,) * len(now) + (True,)
        else:
            blocks, nears = now, (False,) * len(now)
        state = forward_call(
            (infos, far_info[step - 1]), far, query, blocks, tiles, nears, state, step == middle
        )
        query_received = lax.optimization_barrier((query_received, *state))[0]
        received = following
    attention, attention_low, aux = state
    query_partner = swap_core(query_received)

    mixed_side = swap_x(attention_low)
    mixed_core = swap_core(attention_low)
    mixed_both = swap_core(mixed_side)
    mixed_both, query_received, query_partner = lax.optimization_barrier((mixed_both, query_received, query_partner))
    query_views.append(views(query_received) + views(query_partner))
    feed_spots = jnp.stack([core, here, live_count, count_other]).astype(jnp.int32)
    (
        second,
        hidden,
        gate_low,
        up_low,
        outer_low,
        middle_own,
        both_kept,
        both_passed,
        both_sent,
        grad_kept,
        grad_sent,
        feed_gain_part,
    ) = feed_call(
        feed_spots,
        [(mine, 0), (tokens_side, 0), (tokens_core, 0), (tokens_both, 0)],
        [(cot, 0), (cot_side, 0), (cot_core, 0), (cot_both, 0)],
        [(attention_low, 0), (mixed_side, 0), (mixed_core, 0), (mixed_both, 0)],
        gain_two[None, :],
        output_full,
        gate_weight,
        up_weight,
        jnp.transpose(down_weight),
    )

    route_pair = route_of(lambda z, y, k, x: (z ^ 1, y, k, x) if z % 2 != k else None)
    route_cross = route_of(lambda z, y, k, x: (z ^ 2, y, k, x) if z % 2 == k else None)
    route_fourth = route_of(lambda z, y, k, x: (z, y, 1 - k, x) if z % 2 == k else None)
    z_low = lane_z % 2
    upper = lane_z // 2

    def join_x(kept, got, other):
        mine_of = add_low(kept[0], got)
        return jnp.where(side == upper, jnp.stack([mine_of, other]), jnp.stack([other, mine_of]))

    def reduce_last(block):
        return jnp.where(z_low == core, block[0], spread(block[1], route_fourth)).astype(f32)

    weight_spots = jnp.stack([lane_y, core, side]).astype(jnp.int32)
    grad_got = swap_core(grad_sent)
    grad_sum = grad_kept.astype(f32) + grad_got.astype(f32)
    grad_passed = grad_sum[length:].astype(bf16)
    grad_side = swap_x(grad_passed)
    mark(grad_passed)
    down_kept, down_apart, down_here = weight_call(weight_spots, then(hidden), outer_low)
    mark(down_apart)
    grad_side = then(grad_side)
    grads = finish_grads(grad_sum[:length], grad_side, grad_own, attention, aux)

    grad_chunk = start_ring(grads)
    received = next_chunk(grad_chunk, 1)
    grad_next = spread(grads, route_next)
    both_got = swap_core(after(both_sent, grad_chunk))
    query_state, diagonals = query_call((infos, near_info), far, query, after(grads, grad_chunk), near_views, tiles, None, False)
    mark(query_state)
    both_passed, both_got = then(both_passed, both_got)
    middle_passed = add_low(both_passed[1], both_got[1, length:])
    feed_passed = add_low(both_passed[0], both_got[0, length:])
    middle_side = swap_x(middle_passed)
    mark(query_state, middle_passed, feed_passed)
    grad_views = []
    for step in range(1, middle + 1):
        received = then(received)
        following = next_chunk(received, step + 1) if step < middle else None
        partner = swap_core(received)
        grad_views.append(views(received) + views(partner))
        outs = query_call(
            (infos, far_info[step - 1]), far, query, after(grads, received), far_views[step - 1], None, query_state, step == middle
        )
        query_state = outs[0]
        mark(query_state)
        if step == 2:
            gate_kept, gate_apart, gate_here = weight_call(weight_spots, then(gate_low), second)
            grad_next, query_next = then(grad_next, query_next)
            middle_side = then(middle_side)
            mark(query_state, grad_next, query_next, gate_apart, middle_side)
            feed_side = swap_x(after(feed_passed, middle_side))
        if step == 3:
            feed_side = then(feed_side)
            mark(query_state, feed_side)
        if step == middle:
            down_far = spread(after(down_apart, received), route_y)
            down_got = spread(after(down_here, received), route_y)
        received = following
    query_low, far_sums = outs

    def key_step(step, state):
        if step == 0:
            queries = views(query_first) + [(query_next, 0)]
            outs = key_call(
                (infos, near_info), far, then(chunk), queries, views(grad_chunk) + [(grad_next, 0)], turned, None, False
            )
        else:
            outs = key_call(
                (infos, far_info[step - 1]), far, then(chunk), query_views[step - 1], grad_views[step - 1], None, state, step == middle
            )
        mark(outs[0])
        return outs

    key_state = key_step(0, None)
    kept, down_far = then(down_kept, down_far)
    down_far = add_low(kept[1], down_far)
    down_x = swap_x(down_far)
    gate_far = spread(after(gate_apart, down_far), route_y)
    mark(down_far)
    up_kept, up_apart, up_here = weight_call(weight_spots, then(up_low), second)
    mark(up_apart)
    key_state = key_step(1, key_state)
    down_both = join_x(*then(down_kept, down_got, down_x))
    down_got = spread(down_both, route_pair)
    gate_got = spread(after(gate_here, down_both), route_y)
    mark(down_both)
    key_state = key_step(2, key_state)
    kept, gate_far = then(gate_kept, gate_far)
    gate_far = add_low(kept[1], gate_far)
    gate_x = swap_x(gate_far)
    up_far = spread(after(up_apart, gate_far), route_y)
    mark(gate_far)
    key_state = key_step(3, key_state)
    down_both = add_low(*then(down_both, down_got))
    down_got = spread(down_both[1], route_cross)
    mark(down_both)
    key_state = key_step(4, key_state)
    keys_low, values_low = key_state
    gate_both = join_x(*then(gate_kept, gate_got, gate_x))
    gate_got = spread(gate_both, route_pair)
    up_got = spread(after(up_here, gate_both), route_y)
    mark(gate_both)
    both_kept, both_got = then(both_kept, both_got)
    feed_total = both_kept[0].astype(f32) + both_got[0, :length, :width].astype(f32) + feed_side[:, :width].astype(f32)
    result = (middle_own + live_own * feed_total).astype(bf16)
    middle_total = both_kept[1].astype(f32) + both_got[1, :length, :width].astype(f32)
    middle_grad = outer_own + middle_total + middle_side[:, :width].astype(f32)
    branch_low = (live_own * middle_grad).astype(bf16)
    branch_lanes = lanes_of(branch_low)
    mark(*branch_lanes)
    kept, up_far = then(up_kept, up_far)
    up_far = add_low(kept[1], up_far)
    up_x = swap_x(up_far)
    mark(up_far, *branch_lanes)

    projection_spots = jnp.stack([core, lane_y, upper, z_low]).astype(jnp.int32)
    kept_core, sent_core = projection_call(
        projection_spots, query_low, keys_low, values_low, attention_low, first_lanes, then(*branch_lanes)
    )
    got_core = swap_core(sent_core)
    mark(sent_core)
    down_last = add_low(*then(down_both[0], down_got))
    down_out = reduce_last(down_last)
    gate_both = add_low(*then(gate_both, gate_got))
    gate_got = spread(gate_both[1], route_cross)
    mark(down_last, gate_both)
    kept_core, got_core = then(kept_core, got_core)
    passed = add_low(kept_core[4:], got_core[4:])
    got_x = swap_x(passed)
    mark(passed)
    up_both = join_x(*then(up_kept, up_got, up_x))
    up_got = spread(up_both, route_pair)
    mark(up_both)

    gradients = then(jnp.concatenate([keys_low, values_low, query_low], axis=1))
    first_grad = both_sides(contract_last(gradients, weight_mine), contract_last(gradients, weight_other), 1)
    unit_one = inputs * scale_one
    gain_one_part = jnp.sum(first_grad * unit_one, axis=0)
    scaled_one = first_grad * gain_one
    input_gradient = (
        middle_grad
        + scale_one * (scaled_one - unit_one * jnp.mean(scaled_one * unit_one, axis=-1, keepdims=True))
    ).astype(bf16)
    mark(input_gradient)

    lines = diagonals[:, :2].reshape(heads, SPAN_ROW)
    outside = far_sums[:, 0].reshape(heads // 2, PAIR)[:, :8].reshape(heads, 4)
    ends = jnp.arange(SPAN_ROW, dtype=jnp.int32)[None, :]
    lines = lines + jnp.where(ends == 0, outside[:, BEFORE : BEFORE + 1], 0.0)
    lines = lines + jnp.where(ends == SPAN_ROW - 2, outside[:, AFTER : AFTER + 1], 0.0)
    table_part = lax.dot_general(
        onehot, lines, (((0,), (1,)), ((), ())), precision=HIGH, preferred_element_type=f32
    )
    flat = jnp.concatenate([gain_one_part, feed_gain_part[0], table_part.reshape(-1)])
    used = flat.shape[0]
    flat = jnp.pad(flat, (0, -used % 1024)).reshape(-1, 128)
    flat = flat + spread(flat, route_core)
    flat_got = spread(flat, route_near)
    mark(flat)
    gate_last = add_low(*then(gate_both[0], gate_got))
    gate_out = jnp.transpose(reduce_last(gate_last))
    mark(gate_last)
    up_both = add_low(*then(up_both, up_got))
    up_got = spread(up_both[1], route_cross)
    flat, flat_got = then(flat, flat_got)
    flat = flat + flat_got
    flat_got = spread(flat, route_y)
    mark(up_both, flat)
    kept_core, got_core, got_x = then(kept_core, got_core, got_x)
    total = (kept_core[:4].astype(f32) + got_core[:4].astype(f32) + got_x.astype(f32)).astype(bf16)
    size = total.shape[1] // 2
    got = spread(total[:, size:], route_y)
    mark(total)
    flat, flat_got = then(flat, flat_got)
    flat = flat + flat_got
    flat_got = spread(flat, route_x)
    mark(flat)
    total, got = then(total, got)
    total = add_low(total[:, :size], got)
    size = size // 2
    got = spread(total[:, size:], route_far)
    mark(total)
    flat, flat_got = then(flat, flat_got)
    flat = flat + flat_got
    flat_got = spread(flat, route_far)
    up_last = add_low(*then(up_both[0], up_got))
    up_out = jnp.transpose(reduce_last(up_last))
    mark(up_last, flat)
    total, got = then(total, got)
    total = add_low(total[:, :size], got)
    size = size // 2
    got = spread(total[:, size:], route_near)
    mark(total)
    flat, flat_got = then(flat, flat_got)
    flat = (flat + flat_got).reshape(-1)
    total = add_low(total[:, :size], got).astype(f32)
    projection_out = jnp.transpose(total[:3], (0, 2, 1))
    gain_one_sum = flat[:width]
    feed_gain_sum = flat[width : 2 * width]
    table_sum = flat[2 * width : used].reshape(bucket_count, heads)

    def my_half(block):
        size = block.shape[0] // 2
        return lax.dynamic_slice_in_dim(block, side * size, size, 0)

    return (
        result[None],
        input_gradient[None],
        my_half(gain_one_sum),
        projection_out[0],
        projection_out[1],
        projection_out[2],
        total[3],
        my_half(table_sum),
        my_half(feed_gain_sum),
        gate_out,
        up_out,
        down_out,
    )


def solution(mesh):
    placed = (
        P("wsh", "ctx", None),
        P("wsh", None),
        P(),
        P("wsh"),
        P("wsh", None),
        P("wsh", None),
        P("wsh", None),
        P(None, "wsh"),
        P("wsh", None),
        P("wsh"),
        P(None, "wsh"),
        P(None, "wsh"),
        P("wsh", None),
        P("wsh", "ctx", None),
    )
    step = grouped_body if mesh.shape["ctx"] == 16 else body
    return jax.shard_map(
        step,
        mesh=mesh,
        in_specs=placed,
        out_specs=(
            P("wsh", "ctx", None),
            P("wsh", "ctx", None),
            P("wsh"),
            P("wsh", "ctx"),
            P("wsh", "ctx"),
            P("wsh", "ctx"),
            P("ctx", "wsh"),
            P("wsh", None),
            P("wsh"),
            P(None, ("ctx", "wsh")),
            P(None, ("ctx", "wsh")),
            P(("ctx", "wsh"), None),
        ),
        check_vma=False,
    )
```

```python
import functools

import jax
import jax.numpy as jnp
from jax import lax
from jax.experimental import pallas as pl
from jax.experimental.layout import Layout, with_layout_constraint
from jax.experimental.pallas import tpu as pltpu
from jax.sharding import PartitionSpec as P

EPSILON = 1e-06
MASKED = -1e30
HIGH = lax.Precision.HIGHEST


def shifted(block, axis, distance):
    devices = range(lax.axis_size(axis))
    route = [((i - distance) % len(devices), i) for i in devices]
    return lax.ppermute(block, axis, route)


def row_scale(values):
    return lax.rsqrt(jnp.mean(values * values, axis=-1, keepdims=True) + EPSILON)


def normalize(values, gain):
    return values * row_scale(values) * gain


def skew_expand(offset_bias, length):
    count = offset_bias.shape[0]
    padded = jnp.pad(offset_bias, ((0, 0), (0, 1)))
    tiled = jnp.tile(padded, (1, length))[:, : length * (2 * length - 1)]
    return tiled.reshape(count, length, 2 * length - 1)[:, :, length - 1 :]


def diagonal_sums(grid, length):
    count = grid.shape[0]
    wide = jnp.pad(grid, ((0, 0), (0, 0), (length - 1, 0))).reshape(
        count, length * (2 * length - 1)
    )
    wide = jnp.pad(wide, ((0, 0), (0, length)))
    return jnp.sum(wide.reshape(count, length, 2 * length), axis=1)[:, : 2 * length - 1]


def bucket_onehot(offset_start, length, buckets, bucket_count):
    reach = (buckets.shape[0] + 1) // 2
    offsets = offset_start + jnp.arange(2 * length - 1, dtype=jnp.int32) - (length - 1)
    spots = jnp.clip(offsets, 1 - reach, reach - 1) + (reach - 1)
    table_spots = jnp.arange(buckets.shape[0], dtype=jnp.int32)
    chosen = jnp.sum(jnp.where(spots[:, None] == table_spots[None, :], buckets[None, :], 0), axis=1)
    return chosen[:, None] == jnp.arange(bucket_count, dtype=jnp.int32)[None, :]


def block_scores(query3, keys3, table, onehot, key_live, length):
    scores = jnp.einsum("ihd,jhd->hij", query3, keys3, preferred_element_type=jnp.float32)
    offset_bias = jnp.einsum(
        "ob,bh->ho", onehot.astype(jnp.bfloat16), table, preferred_element_type=jnp.float32
    )
    scores = scores + skew_expand(offset_bias, length)
    return jnp.where(key_live[None, None, :], scores, MASKED)


def body(
    tokens,
    lengths,
    buckets,
    attention_gain,
    query_weight,
    key_weight,
    value_weight,
    output_weight,
    bias_table,
    feed_gain,
    gate_weight,
    up_weight,
    down_weight,
    cotangent,
):
    (
        gain_first,
        query_full,
        key_full,
        value_full,
        output_full,
        table_full,
        gain_second,
        gate_full,
        up_full,
        down_full,
    ) = (
        lax.all_gather(attention_gain, "wsh", axis=0, tiled=True),
        lax.all_gather(query_weight, "wsh", axis=0, tiled=True),
        lax.all_gather(key_weight, "wsh", axis=0, tiled=True),
        lax.all_gather(value_weight, "wsh", axis=0, tiled=True),
        lax.all_gather(output_weight, "wsh", axis=1, tiled=True),
        lax.all_gather(bias_table, "wsh", axis=0, tiled=True),
        lax.all_gather(feed_gain, "wsh", axis=0, tiled=True),
        lax.all_gather(gate_weight, "wsh", axis=1, tiled=True),
        lax.all_gather(up_weight, "wsh", axis=1, tiled=True),
        lax.all_gather(down_weight, "wsh", axis=0, tiled=True),
    )
    length = tokens.shape[1]
    heads = table_full.shape[1]
    bucket_count = table_full.shape[0]
    inner = query_full.shape[1]
    head_size = inner // heads
    seq_count = lengths.shape[1]
    wide_count = lax.axis_size("ctx")
    span = wide_count // seq_count
    here = lax.axis_index("ctx")
    my_seq = here % seq_count
    my_block = here // seq_count
    seq_pick = jnp.arange(seq_count, dtype=jnp.int32) == my_seq
    my_length = jnp.sum(jnp.where(seq_pick, lengths[0], 0))
    positions = jnp.arange(length, dtype=jnp.int32)
    live = (my_block * length + positions < my_length).astype(jnp.float32)[:, None]
    inputs = tokens[0].astype(jnp.float32)
    gain_one = gain_first.astype(jnp.float32)
    first = normalize(inputs, gain_one).astype(jnp.bfloat16)
    query = jnp.dot(first, query_full, preferred_element_type=jnp.float32).astype(jnp.bfloat16)
    keys = jnp.dot(first, key_full, preferred_element_type=jnp.float32).astype(jnp.bfloat16)
    values = jnp.dot(first, value_full, preferred_element_type=jnp.float32).astype(jnp.bfloat16)
    query3 = query.reshape(length, heads, head_size)

    def forward_step(carry, block_keys, block_values, key_block):
        run_max, run_total, running = carry
        onehot = bucket_onehot((key_block - my_block) * length, length, buckets, bucket_count)
        key_live = key_block * length + positions < my_length
        scores = block_scores(
            query3,
            block_keys.reshape(length, heads, head_size),
            table_full,
            onehot,
            key_live,
            length,
        )
        new_max = jnp.maximum(run_max, jnp.max(scores, axis=2))
        weights = jnp.exp(scores - new_max[:, :, None])
        factor = jnp.exp(run_max - new_max)
        run_total = run_total * factor + jnp.sum(weights, axis=2)
        update = jnp.einsum(
            "hij,jhd->ihd",
            weights.astype(jnp.bfloat16),
            block_values.reshape(length, heads, head_size),
            preferred_element_type=jnp.float32,
        )
        running = running * jnp.transpose(factor)[:, :, None] + update
        return (new_max, run_total, running)

    start_carry = (
        jnp.full((heads, length), MASKED, jnp.float32),
        jnp.zeros((heads, length), jnp.float32),
        jnp.zeros((length, heads, head_size), jnp.float32),
    )
    start_carry = forward_step(start_carry, keys, values, my_block)
    stored = ()

    def cycle_turn(turn, state):
        carry, block_keys, block_values, stored_blocks = state
        block_keys, block_values = shifted((block_keys, block_values), "ctx", seq_count)
        carry = forward_step(carry, block_keys, block_values, (my_block - turn) % span)
        return (carry, block_keys, block_values, stored_blocks)

    (run_max, run_total, running), _, _, stored = lax.fori_loop(
        1, span, cycle_turn, (start_carry, keys, values, stored)
    )
    log_total = run_max + jnp.log(run_total)
    attention = (running / jnp.transpose(run_total)[:, :, None]).reshape(length, inner)
    attention_low = attention.astype(jnp.bfloat16)
    branch = jnp.dot(attention_low, output_full, preferred_element_type=jnp.float32)
    middle = inputs + live * branch
    gain_two = gain_second.astype(jnp.float32)
    second = normalize(middle, gain_two).astype(jnp.bfloat16)
    gate = jnp.dot(second, gate_full, preferred_element_type=jnp.float32)
    up = jnp.dot(second, up_full, preferred_element_type=jnp.float32)
    hidden = (jax.nn.gelu(gate, approximate=True) * up).astype(jnp.bfloat16)
    feed = jnp.dot(hidden, down_full, preferred_element_type=jnp.float32)
    result = (middle + live * feed).astype(jnp.bfloat16)
    outer = live * cotangent[0].astype(jnp.float32)
    outer_low = outer.astype(jnp.bfloat16)
    down_grad = jnp.einsum("tf,td->fd", hidden, outer_low, preferred_element_type=jnp.float32)
    hidden_grad = jnp.einsum("td,fd->tf", outer_low, down_full, preferred_element_type=jnp.float32)

    def gated(gate_in, up_in):
        return jax.nn.gelu(gate_in, approximate=True) * up_in

    _, gate_pull = jax.vjp(gated, gate, up)
    gate_back, up_back = gate_pull(hidden_grad)
    gate_low = gate_back.astype(jnp.bfloat16)
    up_low = up_back.astype(jnp.bfloat16)
    gate_grad = jnp.einsum("td,tf->df", second, gate_low, preferred_element_type=jnp.float32)
    up_grad = jnp.einsum("td,tf->df", second, up_low, preferred_element_type=jnp.float32)
    second_grad = jnp.einsum(
        "tf,df->td", gate_low, gate_full, preferred_element_type=jnp.float32
    ) + jnp.einsum("tf,df->td", up_low, up_full, preferred_element_type=jnp.float32)
    _, norm_pull = jax.vjp(normalize, middle, gain_two)
    middle_back, gain_two_grad = norm_pull(second_grad)
    middle_grad = outer + middle_back
    branch_low = (live * middle_grad).astype(jnp.bfloat16)
    output_grad = jnp.einsum(
        "ti,td->id", attention_low, branch_low, preferred_element_type=jnp.float32
    )
    attention_grad = jnp.einsum(
        "td,id->ti", branch_low, output_full, preferred_element_type=jnp.float32
    ).astype(jnp.bfloat16)
    attention_grad3 = attention_grad.reshape(length, heads, head_size)
    delta = jnp.transpose(
        jnp.sum(
            (attention_grad.astype(jnp.float32) * attention).reshape(length, heads, head_size),
            axis=2,
        )
    )

    def backward_step(block_keys, block_values, key_block):
        keys3 = block_keys.reshape(length, heads, head_size)
        values3 = block_values.reshape(length, heads, head_size)
        onehot = bucket_onehot((key_block - my_block) * length, length, buckets, bucket_count)
        key_live = key_block * length + positions < my_length
        scores = block_scores(query3, keys3, table_full, onehot, key_live, length)
        probs = jnp.exp(scores - log_total[:, :, None])
        prob_grad = jnp.einsum(
            "ihd,jhd->hij", attention_grad3, values3, preferred_element_type=jnp.float32
        )
        score_grad = (probs * (prob_grad - delta[:, :, None])).astype(jnp.bfloat16)
        part_query = jnp.einsum(
            "hij,jhd->ihd", score_grad, keys3, preferred_element_type=jnp.float32
        )
        part_keys = jnp.einsum(
            "hij,ihd->jhd", score_grad, query3, preferred_element_type=jnp.float32
        )
        part_values = jnp.einsum(
            "hij,ihd->jhd",
            probs.astype(jnp.bfloat16),
            attention_grad3,
            preferred_element_type=jnp.float32,
        )
        part_table = jnp.einsum(
            "ho,ob->bh",
            diagonal_sums(score_grad.astype(jnp.float32), length),
            onehot.astype(jnp.float32),
            precision=HIGH,
        )
        return (
            part_query.reshape(length, inner),
            part_keys.reshape(length, inner),
            part_values.reshape(length, inner),
            part_table,
        )

    def back_turn(turn, state):
        block_keys, block_values, keys_sum, values_sum, query_sum, table_sum = state
        part_query, part_keys, part_values, part_table = backward_step(
            block_keys, block_values, (my_block - turn) % span
        )
        keys_next = keys_sum + part_keys
        values_next = values_sum + part_values
        keys_sum, values_sum = (
            shifted(keys_next.astype(jnp.bfloat16), "ctx", seq_count).astype(keys_next.dtype),
            shifted(values_next.astype(jnp.bfloat16), "ctx", seq_count).astype(values_next.dtype),
        )
        block_keys, block_values = shifted((block_keys, block_values), "ctx", seq_count)
        return (
            block_keys,
            block_values,
            keys_sum,
            values_sum,
            query_sum + part_query,
            table_sum + part_table,
        )

    zeros_rows = jnp.zeros((length, inner), jnp.float32)
    back_state = (
        keys,
        values,
        zeros_rows,
        zeros_rows,
        zeros_rows,
        jnp.zeros((bucket_count, heads), jnp.float32),
    )
    _, _, keys_sum, values_sum, query_sum, table_grad = lax.fori_loop(
        0, span, back_turn, back_state
    )
    query_low = query_sum.astype(jnp.bfloat16)
    keys_low = keys_sum.astype(jnp.bfloat16)
    values_low = values_sum.astype(jnp.bfloat16)
    query_grad = jnp.einsum("td,ti->di", first, query_low, preferred_element_type=jnp.float32)
    key_grad = jnp.einsum("td,ti->di", first, keys_low, preferred_element_type=jnp.float32)
    value_grad = jnp.einsum("td,ti->di", first, values_low, preferred_element_type=jnp.float32)
    first_grad = (
        jnp.einsum("ti,di->td", query_low, query_full, preferred_element_type=jnp.float32)
        + jnp.einsum("ti,di->td", keys_low, key_full, preferred_element_type=jnp.float32)
        + jnp.einsum("ti,di->td", values_low, value_full, preferred_element_type=jnp.float32)
    )
    _, first_pull = jax.vjp(normalize, inputs, gain_one)
    inputs_back, gain_one_grad = first_pull(first_grad)
    input_gradient = (middle_grad + inputs_back).astype(jnp.bfloat16)
    small = lax.psum((gain_one_grad, table_grad, gain_two_grad), "ctx")
    wide = (
        lax.psum_scatter(query_grad, "ctx", scatter_dimension=1, tiled=True),
        lax.psum_scatter(key_grad, "ctx", scatter_dimension=1, tiled=True),
        lax.psum_scatter(value_grad, "ctx", scatter_dimension=1, tiled=True),
        lax.psum_scatter(output_grad, "ctx", scatter_dimension=0, tiled=True),
        lax.psum_scatter(gate_grad, "ctx", scatter_dimension=1, tiled=True),
        lax.psum_scatter(up_grad, "ctx", scatter_dimension=1, tiled=True),
        lax.psum_scatter(down_grad, "ctx", scatter_dimension=0, tiled=True),
    )
    final = (
        lax.psum_scatter(
            small[0].astype(jnp.bfloat16), "wsh", scatter_dimension=0, tiled=True
        ).astype(jnp.float32),
        lax.psum_scatter(
            small[1].astype(jnp.bfloat16), "wsh", scatter_dimension=0, tiled=True
        ).astype(jnp.float32),
        lax.psum_scatter(
            small[2].astype(jnp.bfloat16), "wsh", scatter_dimension=0, tiled=True
        ).astype(jnp.float32),
        lax.psum_scatter(
            wide[0].astype(jnp.bfloat16), "wsh", scatter_dimension=0, tiled=True
        ).astype(jnp.float32),
        lax.psum_scatter(
            wide[1].astype(jnp.bfloat16), "wsh", scatter_dimension=0, tiled=True
        ).astype(jnp.float32),
        lax.psum_scatter(
            wide[2].astype(jnp.bfloat16), "wsh", scatter_dimension=0, tiled=True
        ).astype(jnp.float32),
        lax.psum_scatter(
            wide[3].astype(jnp.bfloat16), "wsh", scatter_dimension=1, tiled=True
        ).astype(jnp.float32),
        lax.psum_scatter(
            wide[4].astype(jnp.bfloat16), "wsh", scatter_dimension=1, tiled=True
        ).astype(jnp.float32),
        lax.psum_scatter(
            wide[5].astype(jnp.bfloat16), "wsh", scatter_dimension=1, tiled=True
        ).astype(jnp.float32),
        lax.psum_scatter(
            wide[6].astype(jnp.bfloat16), "wsh", scatter_dimension=0, tiled=True
        ).astype(jnp.float32),
    )
    gain_one_out, table_out, gain_two_out = (final[0], final[1], final[2])
    query_out, key_out, value_out, output_out = (final[3], final[4], final[5], final[6])
    gate_out, up_out, down_out = (final[7], final[8], final[9])
    return (
        result[None],
        input_gradient[None],
        gain_one_out,
        query_out,
        key_out,
        value_out,
        output_out,
        table_out,
        gain_two_out,
        gate_out,
        up_out,
        down_out,
    )


BLOCK = 256
PAIR = 128
SPAN_ROW = 1024
CONTRACT_LAST = (((1,), (1,)), ((), ()))
AXES = ("ctx", "wsh")
GELU_SCALE = 0.7978845608028654
GELU_CUBE = 0.044715
LEFT_LANE, RIGHT_LANE, DEAD_LANE = 125, 126, 127
NEAR, BEFORE, AFTER = 0, 1, 2


SHARE = 0.01
RING_SHARE = 1.0
RINGED = ("attention_forward", "attention_query_grad", "attention_key_grad")


def estimate(flops, bytes_accessed, transcendentals, share=SHARE):
    return pl.CostEstimate(
        flops=int(flops * share),
        bytes_accessed=int(bytes_accessed * share),
        transcendentals=int(transcendentals * share),
    )


def lanes(rows=BLOCK):
    return lax.broadcasted_iota(jnp.int32, (rows, PAIR), 1)


def only_head(block, second):
    lane = lanes(block.shape[0])
    keep = lane >= PAIR // 2 if second else lane < PAIR // 2
    return jnp.where(keep, block, jnp.zeros_like(block))


def pair_select(first, second):
    return jnp.where(lanes(first.shape[0]) < PAIR // 2, first, second)


def contract_last(left, right):
    return lax.dot_general(left, right, CONTRACT_LAST, preferred_element_type=jnp.float32)


def stack_heads(block):
    return jnp.concatenate([only_head(block, False), only_head(block, True)], axis=0)


def dead_rows(start, limit):
    row = lax.broadcasted_iota(jnp.int32, (BLOCK, PAIR), 0)
    return start + row >= limit


def other_aux(start, limit, kind):
    lane = lanes()
    value = jnp.where(jnp.logical_and(lane < 48, lane % 8 < 6), 1.0, 0.0)
    value = jnp.where(jnp.logical_and(lane == LEFT_LANE, kind == BEFORE), 1.0, value)
    value = jnp.where(jnp.logical_and(lane == RIGHT_LANE, kind == AFTER), 1.0, value)
    value = jnp.where(jnp.logical_and(lane == DEAD_LANE, dead_rows(start, limit)), MASKED, value)
    return value.astype(jnp.bfloat16)


def own_lanes(far_ref, head, heads):
    lane = lanes()
    value = jnp.where(lane == DEAD_LANE, 1.0, 0.0)
    value = jnp.where(lane == LEFT_LANE, far_ref[head], value)
    return jnp.where(lane == RIGHT_LANE, far_ref[heads + head], value)


def parts_of(value):
    first = value.astype(jnp.bfloat16).astype(jnp.float32)
    second = (value - first).astype(jnp.bfloat16).astype(jnp.float32)
    return first, second, value - first - second


def place_parts(base, value, lane_start):
    lane = lanes()
    for spot, part in enumerate(parts_of(value)):
        base = jnp.where(lane == lane_start + spot, part, base)
    return base


def kind_of(block, own):
    return jnp.where(block < own, BEFORE, AFTER)


def tiles_kernel(row_ref, tile_ref, turned_ref):
    row = row_ref[0]
    wide = pltpu.roll(
        jnp.broadcast_to(row, (BLOCK, SPAN_ROW)), SPAN_ROW - 255, 1, stride=1, stride_axis=0
    )
    for spot in range(3):
        tile = wide[:, spot * BLOCK : (spot + 1) * BLOCK]
        tile_ref[0, spot] = tile.astype(jnp.bfloat16)
        turned_ref[0, spot] = jnp.transpose(tile).astype(jnp.bfloat16)


def bias_tiles(offset_rows):
    heads = offset_rows.shape[0]
    shape = jax.ShapeDtypeStruct((heads, 3, BLOCK, BLOCK), jnp.bfloat16)
    spec = pl.BlockSpec((1, 3, BLOCK, BLOCK), lambda h: (h, 0, 0, 0))
    return pl.pallas_call(
        tiles_kernel,
        grid=(heads,),
        out_shape=(shape, shape),
        in_specs=[pl.BlockSpec((1, 1, SPAN_ROW), lambda h: (h, 0, 0))],
        out_specs=(spec, spec),
        name="bias_tiles",
    )(offset_rows[:, None, :])


def view_spec(row, lane_block):
    return pl.BlockSpec((BLOCK, PAIR), lambda p, i, f: (row, lane_block(p)))


def tile_spec():
    return pl.BlockSpec((2, 3, BLOCK, BLOCK), lambda p, i, f: (p, 0, 0, 0))


def run_pairs(kernel, info, far, operands, in_specs, out_shape, out_specs, work, name):
    pairs = 3
    return pl.pallas_call(
        kernel,
        grid_spec=pltpu.PrefetchScalarGridSpec(
            num_scalar_prefetch=2, grid=(pairs,), in_specs=in_specs, out_specs=out_specs
        ),
        out_shape=out_shape,
        cost_estimate=estimate(
            flops=2 * pairs * work * BLOCK * BLOCK * BLOCK,
            bytes_accessed=pairs * work * BLOCK * PAIR * 2,
            transcendentals=pairs * work * BLOCK * BLOCK,
            share=RING_SHARE if name in RINGED else SHARE,
        ),
        name=name,
    )(info, far, *operands)


def forward_kernel(at, nears, first, last, heads, info_ref, far_ref, *refs):
    refs = list(refs)
    count = len(nears)
    query_ref = refs.pop(0)
    key_refs, refs = refs[:count], refs[count:]
    value_refs, refs = refs[:count], refs[count:]
    tile_ref = refs.pop(0) if any(nears) else None
    pair = pl.program_id(0)
    own = info_ref[0]
    query = query_ref[...]
    if first:
        old_max = jnp.full((BLOCK, PAIR), MASKED, jnp.float32)
        total = None
    else:
        max_ref, total_ref = refs.pop(0), refs.pop(0)
        old_max, total = max_ref[...], total_ref[...]
    keys = []
    for spot in range(count):
        block, limit = info_ref[at + 2 * spot], info_ref[at + 1 + 2 * spot]
        kind = NEAR if nears[spot] else kind_of(block, own)
        keys.append(
            jnp.concatenate([key_refs[spot][...], other_aux(block * BLOCK, limit, kind)], axis=1)
        )
    tops, weights = [], []
    for head in range(2):
        aux = own_lanes(far_ref, 2 * pair + head, heads).astype(jnp.bfloat16)
        left = jnp.concatenate([only_head(query, head == 1), aux], axis=1)
        scores = []
        for spot in range(count):
            score = contract_last(left, keys[spot])
            if nears[spot]:
                place = jnp.clip(info_ref[at + 2 * spot] - own, -1, 1) + 1
                score = score + tile_ref[head, place].astype(jnp.float32)
            scores.append(score)
        top = functools.reduce(jnp.maximum, scores)
        lane = head * (PAIR // 2)
        top = jnp.maximum(old_max[:, lane : lane + 1], jnp.max(top, axis=1, keepdims=True))
        tops.append(top)
        weights.append([jnp.exp(score - top).astype(jnp.bfloat16) for score in scores])
    new_max = pair_select(tops[0], tops[1])
    ones = stack_heads(jnp.ones((BLOCK, PAIR), jnp.bfloat16))
    update = None
    for spot in range(count):
        right = jnp.concatenate([stack_heads(value_refs[spot][...]), ones], axis=1)
        left = jnp.concatenate([weights[0][spot], weights[1][spot]], axis=1)
        part = jnp.dot(left, right, preferred_element_type=jnp.float32)
        update = part if update is None else update + part
    if not first:
        factor = jnp.exp(old_max - new_max)
        update = update + total * jnp.concatenate([factor, factor], axis=1)
    if last:
        out_ref, low_ref, aux_ref = refs
        out = update[:, :PAIR] / update[:, PAIR:]
        out_ref[...] = out
        low_ref[...] = out.astype(jnp.bfloat16)
        log = -(new_max + jnp.log(update[:, PAIR:]))
        base = jnp.where(lanes() >= LEFT_LANE, 1.0, 0.0)
        base = jnp.where(pair == 0, base, aux_ref[...])
        for head in range(2):
            lane = head * (PAIR // 2)
            base = place_parts(base, log[:, lane : lane + 1], 8 * (2 * pair + head) + 3)
        aux_ref[...] = base
    else:
        max_out, total_out = refs
        max_out[...] = new_max
        total_out[...] = update


def forward_call(info, far, query, blocks, tiles, nears, state, last):
    count, first = len(blocks), state is None
    inner = query.shape[1]
    pairs = inner // PAIR
    in_specs = [view_spec(0, lambda p: p)]
    in_specs += [view_spec(row, lambda p: p) for _, row in blocks]
    in_specs += [view_spec(row, lambda p: p + pairs) for _, row in blocks]
    operands = [query] + [array for array, _ in blocks] * 2
    if any(nears):
        in_specs.append(tile_spec())
        operands.append(tiles)
    block = view_spec(0, lambda p: p)
    double = pl.BlockSpec((BLOCK, 2 * PAIR), lambda p, i, f: (0, p))
    if not first:
        in_specs += [block, double]
        operands += list(state)
    f32 = functools.partial(jax.ShapeDtypeStruct, dtype=jnp.float32)
    if last:
        out_shape = (
            f32((BLOCK, inner)),
            jax.ShapeDtypeStruct((BLOCK, inner), jnp.bfloat16),
            f32((BLOCK, PAIR)),
        )
        out_specs = (block, block, view_spec(0, lambda p: 0))
    else:
        out_shape = (f32((BLOCK, inner)), f32((BLOCK, 2 * inner)))
        out_specs = (block, double)
    kernel = functools.partial(forward_kernel, info[1], nears, first, last, 2 * pairs)
    return run_pairs(
        kernel, info[0], far, operands, in_specs, out_shape, out_specs, 6 * count, "attention_forward"
    )


def head_aux(aux, head, start):
    lane = lanes()
    keep = jnp.logical_and(lane // 8 == head, jnp.logical_and(lane % 8 >= start, lane % 8 < start + 3))
    return jnp.where(jnp.logical_and(keep, lane < 48), aux, 0.0)


def query_kernel(at, count, near, first, last, heads, info_ref, far_ref, *refs):
    refs = list(refs)
    query_ref, grad_ref, aux_ref = refs.pop(0), refs.pop(0), refs.pop(0)
    key_refs, refs = refs[:count], refs[count:]
    value_refs, refs = refs[:count], refs[count:]
    tile_ref = refs.pop(0) if near else None
    pair = pl.program_id(0)
    own = info_ref[0]
    query, grad = query_ref[...], grad_ref[...]
    aux = aux_ref[...].astype(jnp.float32)
    total = None if first else refs.pop(0)[...]
    lefts, grads = [], []
    for head in range(2):
        which = 2 * pair + head
        mine = own_lanes(far_ref, which, heads) + head_aux(aux, which, 3)
        lefts.append(jnp.concatenate([only_head(query, head == 1), mine.astype(jnp.bfloat16)], axis=1))
        delta = head_aux(aux, which, 0).astype(jnp.bfloat16)
        grads.append(jnp.concatenate([only_head(grad, head == 1), delta], axis=1))
    if near:
        diag_ref = refs.pop()
        strips = [[jnp.zeros((BLOCK, BLOCK), jnp.float32)] * 3 for _ in range(2)]
    lane = lanes()
    for spot in range(count):
        block, limit = info_ref[at + 2 * spot], info_ref[at + 1 + 2 * spot]
        kind = NEAR if near else kind_of(block, own)
        key, value = key_refs[spot][...], value_refs[spot][...]
        side = other_aux(block * BLOCK, limit, kind)
        wide_key = jnp.concatenate([key, side], axis=1)
        wide_value = jnp.concatenate([value, jnp.where(lane < 48, side, jnp.zeros_like(side))], axis=1)
        place = jnp.clip(block - own, -1, 1) + 1
        pieces, counts = [], []
        for head in range(2):
            scores = contract_last(lefts[head], wide_key)
            if near:
                scores = scores + tile_ref[head, place].astype(jnp.float32)
            score_grad = jnp.exp(scores) * contract_last(grads[head], wide_value)
            if near:
                strips[head] = [
                    strip + jnp.where(place == spot_of, score_grad, 0.0)
                    for spot_of, strip in enumerate(strips[head])
                ]
            pieces.append(score_grad.astype(jnp.bfloat16))
            counts.append(jnp.where(lane == 4 * head + kind, 1.0, 0.0).astype(jnp.bfloat16))
        right = jnp.concatenate([stack_heads(key), jnp.concatenate(counts, axis=0)], axis=1)
        part = jnp.dot(jnp.concatenate(pieces, axis=1), right, preferred_element_type=jnp.float32)
        total = part if total is None else total + part
    if near:
        rows = []
        for head in range(2):
            wide = jnp.concatenate(strips[head] + [jnp.zeros((BLOCK, BLOCK), jnp.float32)], axis=1)
            eight = None
            for group in range(BLOCK // 8):
                turned = pltpu.roll(wide[8 * group : 8 * group + 8], (255 - 8 * group) % SPAN_ROW, 1)
                eight = turned if eight is None else eight + turned
            line = None
            for row in range(8):
                turned = pltpu.roll(eight, (SPAN_ROW - row) % SPAN_ROW, 1)[row : row + 1]
                line = turned if line is None else line + turned
            rows.append(line)
        diag_ref[0] = jnp.concatenate(rows + [jnp.zeros((6, SPAN_ROW), jnp.float32)], axis=0)
    if last:
        low_ref, sum_ref = refs
        low_ref[...] = total[:, :PAIR].astype(jnp.bfloat16)
        sum_ref[0] = jnp.broadcast_to(jnp.sum(total[:, PAIR:], axis=0, keepdims=True), (8, PAIR))
    else:
        (total_ref,) = refs
        total_ref[...] = total


def query_call(info, far, query, grads, blocks, tiles, state, last):
    count, near, first = len(blocks), tiles is not None, state is None
    inner = query.shape[1]
    pairs = inner // PAIR
    own = view_spec(0, lambda p: p)
    in_specs = [own, own, view_spec(0, lambda p: pairs)]
    in_specs += [view_spec(row, lambda p: p) for _, row in blocks]
    in_specs += [view_spec(row, lambda p: p + pairs) for _, row in blocks]
    operands = [query, grads, grads] + [array for array, _ in blocks] * 2
    if near:
        in_specs.append(tile_spec())
        operands.append(tiles)
    double = pl.BlockSpec((BLOCK, 2 * PAIR), lambda p, i, f: (0, p))
    if not first:
        in_specs.append(double)
        operands.append(state)
    f32 = functools.partial(jax.ShapeDtypeStruct, dtype=jnp.float32)
    if last:
        out_shape = [jax.ShapeDtypeStruct((BLOCK, inner), jnp.bfloat16), f32((pairs, 8, PAIR))]
        out_specs = [own, pl.BlockSpec((1, 8, PAIR), lambda p, i, f: (p, 0, 0))]
    else:
        out_shape, out_specs = [f32((BLOCK, 2 * inner))], [double]
    if near:
        out_shape.append(f32((pairs, 8, SPAN_ROW)))
        out_specs.append(pl.BlockSpec((1, 8, SPAN_ROW), lambda p, i, f: (p, 0, 0)))
    kernel = functools.partial(query_kernel, info[1], count, near, first, last, 2 * pairs)
    return run_pairs(
        kernel, info[0], far, operands, in_specs, out_shape, out_specs, 8 * count, "attention_query_grad"
    )


def key_kernel(at, count, near, first, last, heads, info_ref, far_ref, *refs):
    refs = list(refs)
    key_ref, value_ref = refs.pop(0), refs.pop(0)
    query_refs, refs = refs[:count], refs[count:]
    grad_refs, refs = refs[:count], refs[count:]
    aux_refs, refs = refs[:count], refs[count:]
    tile_ref = refs.pop(0) if near else None
    pair = pl.program_id(0)
    own = info_ref[0]
    key, value = key_ref[...], value_ref[...]
    key_sum = value_sum = None
    if not first:
        key_sum, value_sum = refs.pop(0)[...], refs.pop(0)[...]
    key_out, value_out = refs
    lane = lanes()
    keys = [only_head(key, False), only_head(key, True)]
    values = []
    for head in range(2):
        pick = jnp.logical_and(lane // 8 == 2 * pair + head, lane % 8 < 3)
        values.append(
            jnp.concatenate([only_head(value, head == 1), jnp.where(pick, 1.0, 0.0).astype(jnp.bfloat16)], axis=1)
        )
    for spot in range(count):
        block, limit = info_ref[at + 2 * spot], info_ref[at + 1 + 2 * spot]
        kind = NEAR if near else kind_of(own, block)
        query, grad, aux = query_refs[spot][...], grad_refs[spot][...], aux_refs[spot][...]
        wide_query = jnp.concatenate([query, aux], axis=1)
        wide_grad = jnp.concatenate([grad, aux], axis=1)
        place = jnp.clip(own - block, -1, 1) + 1
        dead = jnp.logical_and(lane == DEAD_LANE, dead_rows(own * BLOCK, limit))
        probs_low, slopes_low = [], []
        for head in range(2):
            which = 2 * pair + head
            pick = jnp.logical_and(lane // 8 == which, jnp.logical_and(lane % 8 >= 3, lane % 8 < 6))
            side = jnp.where(pick, 1.0, 0.0)
            if not near:
                constant = jnp.where(kind == BEFORE, far_ref[which], far_ref[heads + which])
                side = jnp.where(lane == RIGHT_LANE, constant, side)
            side = jnp.where(dead, MASKED, side).astype(jnp.bfloat16)
            scores = contract_last(jnp.concatenate([keys[head], side], axis=1), wide_query)
            if near:
                scores = scores + tile_ref[head, place].astype(jnp.float32)
            probs = jnp.exp(scores)
            slopes = probs * contract_last(values[head], wide_grad)
            probs_low.append(probs.astype(jnp.bfloat16))
            slopes_low.append(slopes.astype(jnp.bfloat16))
        part_value = jnp.dot(
            jnp.concatenate(probs_low, axis=1), stack_heads(grad), preferred_element_type=jnp.float32
        )
        part_key = jnp.dot(
            jnp.concatenate(slopes_low, axis=1), stack_heads(query), preferred_element_type=jnp.float32
        )
        key_sum = part_key if key_sum is None else key_sum + part_key
        value_sum = part_value if value_sum is None else value_sum + part_value
    key_out[...] = key_sum.astype(key_out.dtype)
    value_out[...] = value_sum.astype(value_out.dtype)


def key_call(info, far, joined, queries, grads, turned, state, last):
    count, near, first = len(queries), turned is not None, state is None
    inner = joined.shape[1] // 2
    pairs = inner // PAIR
    own = view_spec(0, lambda p: p)
    in_specs = [own, view_spec(0, lambda p: p + pairs)]
    in_specs += [view_spec(row, lambda p: p) for _, row in queries]
    in_specs += [view_spec(row, lambda p: p) for _, row in grads]
    in_specs += [view_spec(row, lambda p: pairs) for _, row in grads]
    arrays = [array for array, _ in grads]
    operands = [joined, joined] + [array for array, _ in queries] + arrays + arrays
    if near:
        in_specs.append(tile_spec())
        operands.append(turned)
    if not first:
        in_specs += [own, own]
        operands += list(state)
    shape = jax.ShapeDtypeStruct((BLOCK, inner), jnp.bfloat16 if last else jnp.float32)
    kernel = functools.partial(key_kernel, info[1], count, near, first, last, 2 * pairs)
    return run_pairs(
        kernel, info[0], far, operands, in_specs, (shape, shape), (own, own), 10 * count, "attention_key_grad"
    )


def grads_kernel(first_ref, second_ref, third_ref, out_ref, aux_ref, grad_ref):
    total = first_ref[...] + second_ref[...].astype(jnp.float32) + third_ref[...]
    low = total.astype(jnp.bfloat16)
    inner = low.shape[1]
    grad_ref[:, :inner] = low
    product = low.astype(jnp.float32) * out_ref[...]
    base = aux_ref[...]
    for pair in range(inner // PAIR):
        piece = product[:, pair * PAIR : (pair + 1) * PAIR]
        for head in range(2):
            delta = -jnp.sum(only_head(piece, head == 1), axis=1, keepdims=True)
            base = place_parts(base, delta, 8 * (2 * pair + head))
    grad_ref[:, inner:] = base.astype(jnp.bfloat16)


def finish_grads(first, second, third, out, aux):
    return pl.pallas_call(
        grads_kernel,
        out_shape=jax.ShapeDtypeStruct((BLOCK, out.shape[1] + PAIR), jnp.bfloat16),
        name="attention_out_grad",
    )(first, second, third, out, aux)

def feed_kernel(spot_ref, *refs):
    token_refs, cot_refs, mixed_refs = refs[:4], refs[4:8], refs[8:12]
    gain_ref, out_w_ref, gate_w_ref, up_w_ref, down_w_ref = refs[12:17]
    (
        second_ref,
        hidden_ref,
        gate_ref,
        up_ref,
        outer_ref,
        rows_ref,
        kept_ref,
        passed_ref,
        sent_ref,
        grad_kept_ref,
        grad_sent_ref,
        gain_sum_ref,
    ) = refs[17:29]
    token_all, cot_all, mixed_all, live_all = refs[29:]
    f32, bf16 = jnp.float32, jnp.bfloat16
    step = pl.program_id(0)
    gain = gain_ref[...]
    width = gain.shape[1]
    row = lax.broadcasted_iota(jnp.int32, (BLOCK, 1), 0)

    def load(which):
        for spot in range(2):
            at = slice(spot * BLOCK, (spot + 1) * BLOCK)
            token_all[at, :] = token_refs[2 * which + spot][:, :width]
            cot_all[at, :] = cot_refs[2 * which + spot][:, :width]
            mixed_all[at, :] = mixed_refs[2 * which + spot][...]
            block = spot_ref[1] if which == 0 else spot_ref[1] ^ 1
            alive = block * BLOCK + row < spot_ref[2 + spot]
            live_all[at, :] = jnp.broadcast_to(jnp.where(alive, 1.0, 0.0), (BLOCK, PAIR))

    @pl.when(step == 0)
    def _():
        load(0)

    @pl.when(step > 0)
    def _():
        load(1)

    live = live_all[:, 0:1]
    branch = contract_last(mixed_all[...], out_w_ref[...])
    rows = token_all[...].astype(f32) + live * branch
    scale = lax.rsqrt(jnp.mean(rows * rows, axis=-1, keepdims=True) + EPSILON)
    unit = rows * scale
    second = (unit * gain).astype(bf16)
    second_ref[...] = second
    outer = (cot_all[...].astype(f32) * live).astype(bf16)
    outer_ref[...] = outer
    count = gate_w_ref.shape[1]
    for start in range(0, count, 256):
        at = slice(start, min(start + 256, count))
        gate = jnp.dot(second, gate_w_ref[:, at], preferred_element_type=f32)
        up = jnp.dot(second, up_w_ref[:, at], preferred_element_type=f32)
        back = jnp.dot(outer, down_w_ref[:, at], preferred_element_type=f32)
        square = gate * gate
        bend = jnp.tanh(GELU_SCALE * gate * (1.0 + GELU_CUBE * square))
        curve = 0.5 * gate * (1.0 + bend)
        hidden_ref[:, at] = (curve * up).astype(bf16)
        rise = 0.5 * (1.0 + bend) + 0.5 * GELU_SCALE * gate * (1.0 - bend * bend) * (
            1.0 + 3.0 * GELU_CUBE * square
        )
        gate_ref[:, at] = (back * up * rise).astype(bf16)
        up_ref[:, at] = (back * curve).astype(bf16)
    second_grad = contract_last(gate_ref[...], gate_w_ref[...]) + contract_last(up_ref[...], up_w_ref[...])
    line = jnp.sum(second_grad * unit, axis=0, keepdims=True)

    @pl.when(step == 0)
    def _():
        gain_sum_ref[...] = line
        rows_ref[...] = rows[:BLOCK]

    @pl.when(step > 0)
    def _():
        gain_sum_ref[...] += line

    scaled = second_grad * gain
    middle = live * scale * (scaled - unit * jnp.mean(scaled * unit, axis=-1, keepdims=True))
    middle = middle.astype(bf16)
    grad = jnp.dot(middle, out_w_ref[...], preferred_element_type=f32).astype(bf16)
    feed = contract_last(hidden_ref[...], down_w_ref[...]).astype(bf16)

    @pl.when(step == 0)
    def _():
        kept_ref[0], kept_ref[1] = feed[:BLOCK], middle[:BLOCK]
        passed_ref[...] = jnp.zeros_like(passed_ref)
        passed_ref[0, :, :width], passed_ref[1, :, :width] = feed[BLOCK:], middle[BLOCK:]
        grad_kept_ref[...] = grad

    @pl.when(step > 0)
    def _():
        sent_ref[...] = jnp.zeros_like(sent_ref)
        sent_ref[0, :, :width], sent_ref[1, :, :width] = feed, middle
        grad_sent_ref[...] = grad


def feed_call(spots, tokens, cots, mixed, gain, out_w, gate_w, up_w, down_w):
    f32, bf16 = jnp.float32, jnp.bfloat16
    width, inner = out_w.shape
    wide = tokens[0][0].shape[1]
    units = gate_w.shape[1] // 2
    step, total = 2 * BLOCK, 4 * BLOCK
    once = pl.Buffered(1)

    def rows_of(row, lanes_of):
        return pl.BlockSpec((BLOCK, lanes_of), lambda s, i: (row, 0), pipeline_mode=once)

    def moving(lanes_of):
        return pl.BlockSpec((step, lanes_of), lambda s, i: (s, 0))

    def fixed(*shape):
        return pl.BlockSpec(shape, lambda s, i: (0,) * len(shape), pipeline_mode=once)

    shape = jax.ShapeDtypeStruct
    in_specs = [rows_of(row, array.shape[1]) for array, row in (*tokens, *cots, *mixed)]
    in_specs += [
        fixed(1, width),
        fixed(*out_w.shape),
        pl.BlockSpec((width, units), lambda s, i: (0, i[0]), pipeline_mode=once),
        pl.BlockSpec((width, units), lambda s, i: (0, i[0]), pipeline_mode=once),
        pl.BlockSpec((width, units), lambda s, i: (0, i[0]), pipeline_mode=once),
    ]
    return pl.pallas_call(
        feed_kernel,
        grid_spec=pltpu.PrefetchScalarGridSpec(
            num_scalar_prefetch=1,
            grid=(2,),
            in_specs=in_specs,
            out_specs=(
                moving(width),
                moving(units),
                moving(units),
                moving(units),
                moving(width),
                fixed(BLOCK, width),
                fixed(2, BLOCK, width),
                fixed(2, BLOCK, wide),
                fixed(2, step, wide),
                fixed(step, inner),
                fixed(step, inner),
                fixed(1, width),
            ),
            scratch_shapes=[
                pltpu.VMEM((step, width), bf16),
                pltpu.VMEM((step, width), bf16),
                pltpu.VMEM((step, inner), bf16),
                pltpu.VMEM((step, PAIR), f32),
            ],
        ),
        out_shape=(
            shape((total, width), bf16),
            shape((total, units), bf16),
            shape((total, units), bf16),
            shape((total, units), bf16),
            shape((total, width), bf16),
            shape((BLOCK, width), f32),
            shape((2, BLOCK, width), bf16),
            shape((2, BLOCK, wide), bf16),
            shape((2, step, wide), bf16),
            shape((step, inner), bf16),
            shape((step, inner), bf16),
            shape((1, width), f32),
        ),
        compiler_params=pltpu.CompilerParams(vmem_limit_bytes=63_000_000),
        cost_estimate=estimate(
            flops=2 * total * width * (6 * units + 2 * inner),
            bytes_accessed=2 * (3 * width * units + 8 * total * width),
            transcendentals=total * units,
        ),
        name="feed_forward",
    )(spots, *[array for array, _ in (*tokens, *cots, *mixed)], gain, out_w, gate_w, up_w, down_w)


def weight_kernel(spot_ref, left_ref, right_ref, kept_ref, apart_ref, here_ref, product_ref):
    y, core, side = spot_ref[0], spot_ref[1], spot_ref[2]
    use = kept_ref.shape[2]
    product_ref[...] = lax.dot_general(
        left_ref[...], right_ref[...], (((0,), (0,)), ((), ())), preferred_element_type=jnp.float32
    )

    def block_of(y_bit, apart_x, apart_k):
        k_bit = core if apart_k == 0 else 1 - core
        x_bit = side if apart_x == 0 else 1 - side
        block = y_bit * 4 + k_bit * 2 + x_bit
        return product_ref[pl.ds(pl.multiple_of(block * use, 16), use), :].astype(jnp.bfloat16)

    for apart_k in range(2):
        for apart_x in range(2):
            kept_ref[apart_x, apart_k] = block_of(y, apart_x, apart_k)
        apart_ref[apart_k] = block_of(1 - y, 1, apart_k)
        here_ref[apart_k] = block_of(1 - y, 0, apart_k)


def weight_call(spots, left, right):
    width = right.shape[1]
    use = left.shape[1] // 8
    whole = jax.ShapeDtypeStruct((2, 2, use, width), jnp.bfloat16)
    part = jax.ShapeDtypeStruct((2, use, width), jnp.bfloat16)
    part_spec = pl.BlockSpec(part.shape, lambda s, i: (0, 0, 0))
    return pl.pallas_call(
        weight_kernel,
        grid_spec=pltpu.PrefetchScalarGridSpec(
            num_scalar_prefetch=1,
            grid=(1,),
            in_specs=[
                pl.BlockSpec(left.shape, lambda s, i: (0, 0)),
                pl.BlockSpec(right.shape, lambda s, i: (0, 0)),
            ],
            out_specs=(pl.BlockSpec(whole.shape, lambda s, i: (0, 0, 0, 0)), part_spec, part_spec),
            scratch_shapes=[pltpu.VMEM((left.shape[1], width), jnp.float32)],
        ),
        out_shape=(whole, part, part),
        compiler_params=pltpu.CompilerParams(vmem_limit_bytes=60_000_000),
        cost_estimate=estimate(
            flops=2 * left.shape[0] * left.shape[1] * width,
            bytes_accessed=2 * (left.size + right.size + 8 * use * width),
            transcendentals=0,
            share=RING_SHARE,
        ),
        name="feed_weight_grad",
    )(spots, left, right)


def projection_kernel(spot_ref, query_ref, key_ref, value_ref, mixed_ref, first_kept_ref, first_sent_ref, branch_kept_ref, branch_sent_ref, kept_ref, sent_ref):
    core, y, z_high, z_low = spot_ref[0], spot_ref[1], spot_ref[2], spot_ref[3]
    inner = query_ref.shape[1]
    columns = inner // 16
    size = inner // 2
    for out_ref, k_bit in ((kept_ref, core), (sent_ref, 1 - core)):
        target = lax.broadcasted_iota(jnp.int32, (inner, size), 1)
        group, inside = target // columns, target % columns
        z_bits = ((group // 2) % 2) ^ z_high, (group % 2) ^ z_low
        source = (((z_bits[0] * 2 + z_bits[1]) * 2 + ((group // 4) ^ y)) * 2 + k_bit) * columns + inside
        chooser = jnp.where(lax.broadcasted_iota(jnp.int32, (inner, size), 0) == source, 1.0, 0.0).astype(jnp.bfloat16)
        for spot, ref in enumerate((query_ref, key_ref, value_ref, mixed_ref)):
            picked = jnp.dot(ref[...], chooser, preferred_element_type=jnp.float32).astype(jnp.bfloat16)
            rights = (branch_kept_ref, branch_sent_ref) if spot == 3 else (first_kept_ref, first_sent_ref)
            for lane_half, right in enumerate(rights):
                out_ref[lane_half * 4 + spot] = lax.dot_general(
                    picked, right[...], (((0,), (0,)), ((), ())), preferred_element_type=jnp.float32
                ).astype(jnp.bfloat16)


def projection_call(spots, query, keys, values, mixed, first_lanes, branch_lanes):
    shape = jax.ShapeDtypeStruct((8, query.shape[1] // 2, first_lanes[0].shape[1]), jnp.bfloat16)
    operands = [query, keys, values, mixed, *first_lanes, *branch_lanes]
    return pl.pallas_call(
        projection_kernel,
        grid_spec=pltpu.PrefetchScalarGridSpec(
            num_scalar_prefetch=1,
            grid=(1,),
            in_specs=[pl.BlockSpec((BLOCK, a.shape[1]), lambda s, i: (0, 0)) for a in operands],
            out_specs=[pl.BlockSpec(shape.shape, lambda s, i: (0, 0, 0))] * 2,
        ),
        out_shape=[shape, shape],
        cost_estimate=estimate(
            flops=2 * 4 * query.size * 2 * first_lanes[0].shape[1],
            bytes_accessed=8 * 2 * query.size,
            transcendentals=0,
            share=RING_SHARE,
        ),
        name="projection_weight_grad",
    )(spots, *operands)


def grouped_body(
    tokens,
    lengths,
    buckets,
    attention_gain,
    query_weight,
    key_weight,
    value_weight,
    output_weight,
    bias_table,
    feed_gain,
    gate_weight,
    up_weight,
    down_weight,
    cotangent,
):
    bf16, f32 = jnp.bfloat16, jnp.float32
    places = lax.axis_size("ctx")
    chips = places // 2
    rows_of_chips = chips // 2
    here = lax.axis_index("ctx")
    side = lax.axis_index("wsh")
    core = here % 2
    chip = here // 2
    lane_y = chip % 2
    lane_z = chip // 2
    length = tokens.shape[1]
    half = tokens.shape[2] // 2
    heads = bias_table.shape[1]
    inner = query_weight.shape[1]
    nowhere = -(1 << 20)

    def spread(block, route):
        return lax.ppermute(block, AXES, route)

    def route_of(move):
        pairs = []
        for c in range(places):
            for w in range(2):
                target = move(c // 4, (c // 2) % 2, c % 2, w)
                if target is not None:
                    z, y, k, x = target
                    pairs.append((c * 2 + w, (((z * 2 + y) * 2) + k) * 2 + x))
        return pairs

    route_core = route_of(lambda z, y, k, x: (z, y, 1 - k, x))
    route_x = route_of(lambda z, y, k, x: (z, y, k, 1 - x))
    route_y = route_of(lambda z, y, k, x: (z, 1 - y, k, x))
    route_far = route_of(lambda z, y, k, x: (z ^ 2, y, k, x))
    route_near = route_of(lambda z, y, k, x: (z ^ 1, y, k, x))
    order = [(i, 0) for i in range(rows_of_chips)] + [
        (rows_of_chips - 1 - i, 1) for i in range(rows_of_chips)
    ]
    place = {spot: i for i, spot in enumerate(order)}
    route_ring = route_of(
        lambda z, y, k, x: (*order[(place[(z, y)] + 1 - 2 * k) % chips], k, x)
    )
    route_next = [
        ((c * 2 + w), (c + (1 if c % 2 else -1)) * 2 + w)
        for c in range(places)
        for w in range(2)
        if 0 <= c + (1 if c % 2 else -1) < places
    ]
    my_place = jnp.where(lane_y == 0, lane_z, 2 * rows_of_chips - 1 - lane_z)
    toward = jnp.where(core == 0, -1, 1)
    next_block = here - 1 + 2 * core
    has_next = jnp.logical_and(next_block >= 0, next_block < places)

    def chip_at(spot):
        spot = (spot + 2 * chips) % chips
        return jnp.where(
            spot < rows_of_chips, 2 * spot, 2 * (2 * rows_of_chips - 1 - spot) + 1
        )

    def swap_core(block):
        return spread(block, route_core)

    def swap_x(block):
        return spread(block, route_x)

    def both_sides(mine, other, axis):
        return jnp.where(
            side == 0,
            jnp.concatenate([mine, other], axis=axis),
            jnp.concatenate([other, mine], axis=axis),
        )

    def after(block, *others):
        return lax.optimization_barrier((block, *others))[0]

    live_count = jnp.minimum(lengths[0, 0], places * length)
    middle = chips // 2
    width = tokens.shape[2]

    def blocks_at(step):
        ahead = chip_at(my_place + toward * step)
        if step == middle:
            return [ahead * 2 + core, ahead * 2 + 1 - core]
        behind = chip_at(my_place - toward * step)
        return [ahead * 2 + core, ahead * 2 + 1 - core, behind * 2 + 1 - core, behind * 2 + core]

    def info_of(blocks, near):
        entries = []
        for block in blocks:
            limit = live_count
            if near:
                limit = jnp.where(jnp.logical_or(block != next_block, has_next), limit, nowhere)
            else:
                limit = jnp.where(block == next_block, nowhere, limit)
            entries += [block, limit]
        return entries

    marks = []

    def then(*blocks):
        if not marks:
            return blocks if len(blocks) > 1 else blocks[0]
        held = lax.optimization_barrier((*blocks, *marks))[: len(blocks)]
        return held if len(blocks) > 1 else held[0]

    def mark(*blocks):
        marks[:] = blocks

    def add_low(left, right):
        return (left.astype(f32) + right.astype(f32)).astype(bf16)

    quarter = half // 2

    def my_rows(block, which, count):
        return lax.dynamic_slice_in_dim(block, which * count, count, 0)

    def plain(block):
        return with_layout_constraint(block, Layout(tuple(range(block.ndim))))

    small = jnp.concatenate(
        [
            attention_gain,
            feed_gain,
            bias_table.reshape(-1),
            jnp.stack([live_count // 128, live_count % 128]).astype(bf16),
        ]
    )
    size_small = small.shape[0]
    small = jnp.pad(small, (0, -size_small % 2048)).reshape(-1, 128)
    small_other = swap_x(small).reshape(-1)
    projections = [key_weight, value_weight, query_weight]
    sent_rows = jnp.concatenate([my_rows(w, core, quarter) for w in projections], axis=1)
    sent_rows = after(sent_rows, small)
    part = swap_x(sent_rows)
    lanes_left = -width % PAIR

    def padded(block):
        return jnp.pad(block, ((0, 0), (0, lanes_left)))

    mine, cot = plain(padded(tokens[0])), plain(padded(cotangent[0]))
    tokens_core = swap_core(after(mine, sent_rows))
    output_turned = jnp.transpose(output_weight)
    gain_other = small_other[:half]
    feed_other = small_other[half : 2 * half]
    table_other = small_other[2 * half : size_small - 2].reshape(bias_table.shape)
    counts = small_other[size_small - 2 : size_small].astype(f32).astype(jnp.int32)
    count_other = counts[0] * 128 + counts[1]
    gain_one = both_sides(attention_gain, gain_other, 0).astype(f32)
    gain_two = both_sides(feed_gain, feed_other, 0).astype(f32)
    table = both_sides(bias_table, table_other, 0)
    bucket_count = table.shape[0]
    reach = (buckets.shape[0] + 1) // 2
    offsets = jnp.clip(jnp.arange(SPAN_ROW, dtype=jnp.int32) - 511, 1 - reach, reach - 1) + (reach - 1)
    spots = jnp.arange(buckets.shape[0], dtype=jnp.int32)
    chosen = jnp.sum(jnp.where(offsets[:, None] == spots[None, :], buckets[None, :], 0), axis=1)
    onehot = (chosen[:, None] == jnp.arange(bucket_count, dtype=jnp.int32)[None, :]).astype(f32)
    offset_rows = lax.dot_general(
        table.astype(f32), onehot, (((0,), (1,)), ((), ())), precision=HIGH, preferred_element_type=f32
    )
    tiles, turned = bias_tiles(offset_rows)
    far = jnp.concatenate([offset_rows[:, 0], offset_rows[:, SPAN_ROW - 2]])
    entries = [here] + info_of([here, here ^ 1, next_block], True)
    near_info, far_info = 1, []
    for step in range(1, middle + 1):
        far_info.append(len(entries))
        entries += info_of(blocks_at(step), False)
    entries += info_of([next_block], True)
    infos = jnp.stack(entries).astype(jnp.int32)

    inputs = mine[:, :width].astype(f32)
    scale_one = row_scale(inputs)
    first = (inputs * scale_one * gain_one).astype(bf16)
    partner_inputs = tokens_core[:, :width].astype(f32)
    first_partner = (partner_inputs * row_scale(partner_inputs) * gain_one).astype(bf16)
    first_pair = jnp.concatenate([first, first_partner], axis=0)

    def lanes_of(block):
        low_half, high_half = block[:, :half], block[:, half:]
        return (
            jnp.where(side == 0, low_half, high_half),
            jnp.where(side == 0, high_half, low_half),
        )

    pair_lanes = lanes_of(first_pair)
    first_lanes = pair_lanes
    weight_mine = jnp.concatenate(projections, axis=1)
    projected = jnp.dot(pair_lanes[0], weight_mine, preferred_element_type=f32)
    held = lax.optimization_barrier((part, tiles, turned, far, infos, projected, pair_lanes[1], weight_mine))
    part, tiles, turned, far, infos, projected, lanes_other, weight_mine = held
    traded = swap_core(part)
    out_part = swap_x(after(my_rows(output_turned, core, quarter), part))
    tokens_side = swap_x(after(mine, out_part))
    cot_side = swap_x(after(cot, out_part))

    def join_rows(part, traded):
        return jnp.where(
            core == 0,
            jnp.concatenate([part, traded], axis=0),
            jnp.concatenate([traded, part], axis=0),
        )

    weight_other = join_rows(part, traded)
    projected = (projected + jnp.dot(lanes_other, weight_other, preferred_element_type=f32)).astype(bf16)
    chunk, query_chunk = projected[:, : 2 * inner], projected[:, 2 * inner :]
    joined, query = chunk, query_chunk

    def start_ring(block):
        return jnp.concatenate([block, swap_core(block)], axis=0)

    def next_chunk(chunk, step):
        if step == middle:
            return spread(chunk[:length], route_ring)
        return spread(chunk, route_ring)

    def views(chunk):
        return [(chunk, row) for row in range(chunk.shape[0] // length)]

    received = next_chunk(chunk, 1)
    query_first = query_chunk
    query_received = next_chunk(query_chunk, 1)
    next_joined = spread(chunk[:length], route_next)
    query_next = spread(query_chunk[:length], route_next)
    near_views = views(chunk) + [(next_joined, 0)]
    state = forward_call((infos, near_info), far, query, near_views[:2], tiles, (True, True), None, False)
    far_views, query_views = [], []
    for step in range(1, middle + 1):
        received, _ = lax.optimization_barrier((received, state))
        following = next_chunk(received, step + 1) if step < middle else None
        partner = swap_core(received)
        now = views(received) + views(partner)
        far_views.append(now)
        if step > 1:
            query_partner = swap_core(query_received)
            query_views.append(views(query_received) + views(query_partner))
            forced = (query_received, query_partner)
            query_received = next_chunk(query_received, step)
            state = lax.optimization_barrier((*state, *forced))[:2]
        if step == 1:
            out_traded = swap_core(after(out_part, chunk))
            output_full = both_sides(output_turned, join_rows(out_part, out_traded), 0)
            state = lax.optimization_barrier((*state, output_full))
            output_full, state = state[2], state[:2]
        if step == 2:
            cot_core = swap_core(after(cot, state))
            positions = here * length + jnp.arange(length, dtype=jnp.int32)
            live_own = (positions < live_count).astype(f32)[:, None]
            outer_own = cot[:, :width].astype(f32) * live_own
            grad_own = jnp.einsum(
                "td,di->ti", outer_own.astype(bf16), output_full, preferred_element_type=f32
            )
            tokens_side = after(tokens_side, *state)
            tokens_both = swap_core(tokens_side)
            state = lax.optimization_barrier((*state, grad_own, cot_core, tokens_both))
            grad_own, cot_core, tokens_both, state = state[2], state[3], state[4], state[:2]
        if step == 3:
            cot_side = after(cot_side, *state)
            cot_both = swap_core(cot_side)
            state = lax.optimization_barrier((*state, cot_both))
            cot_both, state = state[2], state[:2]
        if step == middle:
            blocks, nears = now + [near_views[2]], (False,) * len(now) + (True,)
        else:
            blocks, nears = now, (False,) * len(now)
        state = forward_call(
            (infos, far_info[step - 1]), far, query, blocks, tiles, nears, state, step == middle
        )
        query_received = lax.optimization_barrier((query_received, *state))[0]
        received = following
    attention, attention_low, aux = state
    query_partner = swap_core(query_received)

    mixed_side = swap_x(attention_low)
    mixed_core = swap_core(attention_low)
    mixed_both = swap_core(mixed_side)
    mixed_both, query_received, query_partner = lax.optimization_barrier((mixed_both, query_received, query_partner))
    query_views.append(views(query_received) + views(query_partner))
    feed_spots = jnp.stack([core, here, live_count, count_other]).astype(jnp.int32)
    (
        second,
        hidden,
        gate_low,
        up_low,
        outer_low,
        middle_own,
        both_kept,
        both_passed,
        both_sent,
        grad_kept,
        grad_sent,
        feed_gain_part,
    ) = feed_call(
        feed_spots,
        [(mine, 0), (tokens_side, 0), (tokens_core, 0), (tokens_both, 0)],
        [(cot, 0), (cot_side, 0), (cot_core, 0), (cot_both, 0)],
        [(attention_low, 0), (mixed_side, 0), (mixed_core, 0), (mixed_both, 0)],
        gain_two[None, :],
        output_full,
        gate_weight,
        up_weight,
        jnp.transpose(down_weight),
    )

    route_pair = route_of(lambda z, y, k, x: (z ^ 1, y, k, x) if z % 2 != k else None)
    route_cross = route_of(lambda z, y, k, x: (z ^ 2, y, k, x) if z % 2 == k else None)
    route_fourth = route_of(lambda z, y, k, x: (z, y, 1 - k, x) if z % 2 == k else None)
    z_low = lane_z % 2
    upper = lane_z // 2

    def join_x(kept, got, other):
        mine_of = add_low(kept[0], got)
        return jnp.where(side == upper, jnp.stack([mine_of, other]), jnp.stack([other, mine_of]))

    def reduce_last(block):
        return jnp.where(z_low == core, block[0], spread(block[1], route_fourth)).astype(f32)

    weight_spots = jnp.stack([lane_y, core, side]).astype(jnp.int32)
    grad_got = swap_core(grad_sent)
    grad_sum = grad_kept.astype(f32) + grad_got.astype(f32)
    grad_passed = grad_sum[length:].astype(bf16)
    grad_side = swap_x(grad_passed)
    mark(grad_passed)
    down_kept, down_apart, down_here = weight_call(weight_spots, then(hidden), outer_low)
    mark(down_apart)
    grad_side = then(grad_side)
    grads = finish_grads(grad_sum[:length], grad_side, grad_own, attention, aux)

    grad_chunk = start_ring(grads)
    received = next_chunk(grad_chunk, 1)
    grad_next = spread(grads, route_next)
    both_got = swap_core(after(both_sent, grad_chunk))
    query_state, diagonals = query_call((infos, near_info), far, query, after(grads, grad_chunk), near_views, tiles, None, False)
    mark(query_state)
    both_passed, both_got = then(both_passed, both_got)
    middle_passed = add_low(both_passed[1], both_got[1, length:])
    feed_passed = add_low(both_passed[0], both_got[0, length:])
    middle_side = swap_x(middle_passed)
    mark(query_state, middle_passed, feed_passed)
    grad_views = []
    for step in range(1, middle + 1):
        received = then(received)
        following = next_chunk(received, step + 1) if step < middle else None
        partner = swap_core(received)
        grad_views.append(views(received) + views(partner))
        outs = query_call(
            (infos, far_info[step - 1]), far, query, after(grads, received), far_views[step - 1], None, query_state, step == middle
        )
        query_state = outs[0]
        mark(query_state)
        if step == 2:
            gate_kept, gate_apart, gate_here = weight_call(weight_spots, then(gate_low), second)
            grad_next, query_next = then(grad_next, query_next)
            mark(query_state, grad_next, query_next, gate_apart)
        if step == 3:
            middle_side = then(middle_side)
            mark(query_state, middle_side)
            feed_side = swap_x(after(feed_passed, middle_side))
        if step == middle:
            down_far = spread(after(down_apart, received), route_y)
            down_got = spread(after(down_here, received), route_y)
        received = following
    query_low, far_sums = outs

    def key_step(step, state):
        if step == 0:
            queries = views(query_first) + [(query_next, 0)]
            outs = key_call(
                (infos, near_info), far, then(chunk), queries, views(grad_chunk) + [(grad_next, 0)], turned, None, False
            )
        else:
            outs = key_call(
                (infos, far_info[step - 1]), far, then(chunk), query_views[step - 1], grad_views[step - 1], None, state, step == middle
            )
        mark(outs[0])
        return outs

    key_state = key_step(0, None)
    kept, down_far = then(down_kept, down_far)
    down_far = add_low(kept[1], down_far)
    down_x = swap_x(down_far)
    gate_far = spread(after(gate_apart, down_far), route_y)
    mark(down_far)
    up_kept, up_apart, up_here = weight_call(weight_spots, then(up_low), second)
    mark(up_apart)
    key_state = key_step(1, key_state)
    down_both = join_x(*then(down_kept, down_got, down_x))
    down_got = spread(down_both, route_pair)
    gate_got = spread(after(gate_here, down_both), route_y)
    mark(down_both)
    key_state = key_step(2, key_state)
    kept, gate_far = then(gate_kept, gate_far)
    gate_far = add_low(kept[1], gate_far)
    gate_x = swap_x(gate_far)
    up_far = spread(after(up_apart, gate_far), route_y)
    mark(gate_far)
    feed_side = then(feed_side)
    mark(feed_side)
    key_state = key_step(3, key_state)
    down_both = add_low(*then(down_both, down_got))
    down_got = spread(down_both[1], route_cross)
    mark(down_both)
    key_state = key_step(4, key_state)
    keys_low, values_low = key_state
    gate_both = join_x(*then(gate_kept, gate_got, gate_x))
    gate_got = spread(gate_both, route_pair)
    up_got = spread(after(up_here, gate_both), route_y)
    mark(gate_both)
    both_kept, both_got = then(both_kept, both_got)
    feed_total = both_kept[0].astype(f32) + both_got[0, :length, :width].astype(f32) + feed_side[:, :width].astype(f32)
    result = (middle_own + live_own * feed_total).astype(bf16)
    middle_total = both_kept[1].astype(f32) + both_got[1, :length, :width].astype(f32)
    middle_grad = outer_own + middle_total + middle_side[:, :width].astype(f32)
    branch_low = (live_own * middle_grad).astype(bf16)
    branch_lanes = lanes_of(branch_low)
    mark(*branch_lanes)
    kept, up_far = then(up_kept, up_far)
    up_far = add_low(kept[1], up_far)
    up_x = swap_x(up_far)
    mark(up_far, *branch_lanes)

    projection_spots = jnp.stack([core, lane_y, upper, z_low]).astype(jnp.int32)
    kept_core, sent_core = projection_call(
        projection_spots, query_low, keys_low, values_low, attention_low, first_lanes, then(*branch_lanes)
    )
    got_core = swap_core(sent_core)
    mark(sent_core)
    down_last = add_low(*then(down_both[0], down_got))
    down_out = reduce_last(down_last)
    gate_both = add_low(*then(gate_both, gate_got))
    gate_got = spread(gate_both[1], route_cross)
    mark(down_last, gate_both)
    kept_core, got_core = then(kept_core, got_core)
    passed = add_low(kept_core[4:], got_core[4:])
    got_x = swap_x(passed)
    mark(passed)
    up_both = join_x(*then(up_kept, up_got, up_x))
    up_got = spread(up_both, route_pair)
    mark(up_both)

    gradients = then(jnp.concatenate([keys_low, values_low, query_low], axis=1))
    first_grad = both_sides(contract_last(gradients, weight_mine), contract_last(gradients, weight_other), 1)
    unit_one = inputs * scale_one
    gain_one_part = jnp.sum(first_grad * unit_one, axis=0)
    scaled_one = first_grad * gain_one
    input_gradient = (
        middle_grad
        + scale_one * (scaled_one - unit_one * jnp.mean(scaled_one * unit_one, axis=-1, keepdims=True))
    ).astype(bf16)
    mark(input_gradient)

    lines = diagonals[:, :2].reshape(heads, SPAN_ROW)
    outside = far_sums[:, 0].reshape(heads // 2, PAIR)[:, :8].reshape(heads, 4)
    ends = jnp.arange(SPAN_ROW, dtype=jnp.int32)[None, :]
    lines = lines + jnp.where(ends == 0, outside[:, BEFORE : BEFORE + 1], 0.0)
    lines = lines + jnp.where(ends == SPAN_ROW - 2, outside[:, AFTER : AFTER + 1], 0.0)
    table_part = lax.dot_general(
        onehot, lines, (((0,), (1,)), ((), ())), precision=HIGH, preferred_element_type=f32
    )
    flat = jnp.concatenate([gain_one_part, feed_gain_part[0], table_part.reshape(-1)])
    used = flat.shape[0]
    flat = jnp.pad(flat, (0, -used % 1024)).reshape(-1, 128)
    flat = flat + spread(flat, route_core)
    flat_got = spread(flat, route_near)
    mark(flat)
    gate_last = add_low(*then(gate_both[0], gate_got))
    gate_out = jnp.transpose(reduce_last(gate_last))
    mark(gate_last)
    up_both = add_low(*then(up_both, up_got))
    up_got = spread(up_both[1], route_cross)
    flat, flat_got = then(flat, flat_got)
    flat = flat + flat_got
    flat_got = spread(flat, route_y)
    mark(up_both, flat)
    kept_core, got_core, got_x = then(kept_core, got_core, got_x)
    total = (kept_core[:4].astype(f32) + got_core[:4].astype(f32) + got_x.astype(f32)).astype(bf16)
    size = total.shape[1] // 2
    got = spread(total[:, size:], route_y)
    mark(total)
    flat, flat_got = then(flat, flat_got)
    flat = flat + flat_got
    flat_got = spread(flat, route_x)
    mark(flat)
    total, got = then(total, got)
    total = add_low(total[:, :size], got)
    size = size // 2
    got = spread(total[:, size:], route_far)
    mark(total)
    flat, flat_got = then(flat, flat_got)
    flat = flat + flat_got
    flat_got = spread(flat, route_far)
    up_last = add_low(*then(up_both[0], up_got))
    up_out = jnp.transpose(reduce_last(up_last))
    mark(up_last, flat)
    total, got = then(total, got)
    total = add_low(total[:, :size], got)
    size = size // 2
    got = spread(total[:, size:], route_near)
    mark(total)
    flat, flat_got = then(flat, flat_got)
    flat = (flat + flat_got).reshape(-1)
    total = add_low(total[:, :size], got).astype(f32)
    projection_out = jnp.transpose(total[:3], (0, 2, 1))
    gain_one_sum = flat[:width]
    feed_gain_sum = flat[width : 2 * width]
    table_sum = flat[2 * width : used].reshape(bucket_count, heads)

    def my_half(block):
        size = block.shape[0] // 2
        return lax.dynamic_slice_in_dim(block, side * size, size, 0)

    return (
        result[None],
        input_gradient[None],
        my_half(gain_one_sum),
        projection_out[0],
        projection_out[1],
        projection_out[2],
        total[3],
        my_half(table_sum),
        my_half(feed_gain_sum),
        gate_out,
        up_out,
        down_out,
    )


def solution(mesh):
    placed = (
        P("wsh", "ctx", None),
        P("wsh", None),
        P(),
        P("wsh"),
        P("wsh", None),
        P("wsh", None),
        P("wsh", None),
        P(None, "wsh"),
        P("wsh", None),
        P("wsh"),
        P(None, "wsh"),
        P(None, "wsh"),
        P("wsh", None),
        P("wsh", "ctx", None),
    )
    step = grouped_body if mesh.shape["ctx"] == 16 else body
    return jax.shard_map(
        step,
        mesh=mesh,
        in_specs=placed,
        out_specs=(
            P("wsh", "ctx", None),
            P("wsh", "ctx", None),
            P("wsh"),
            P("wsh", "ctx"),
            P("wsh", "ctx"),
            P("wsh", "ctx"),
            P("ctx", "wsh"),
            P("wsh", None),
            P("wsh"),
            P(None, ("ctx", "wsh")),
            P(None, ("ctx", "wsh")),
            P(("ctx", "wsh"), None),
        ),
        check_vma=False,
    )
```
